128 devices in a mesh: ctx: 4 (over z_hi, core), req: 32 (over x, y, z_lo).
Axes of the slice: x: 4, y: 4, z: 4 (z_hi: 2, z_lo: 2; z = z_hi * 2 + z_lo), core: 2. Of those that a mesh axis runs over, the one named last changes fastest.
Arguments:
- pre_latent: bfloat16 [32, 256, 576], P('req', 'ctx')
- pre_qlat: bfloat16 [32, 256, 8, 512], P('req', 'ctx')
- pre_qrope: bfloat16 [32, 256, 8, 64], P('req', 'ctx'), may hold values from -6 to 6
- pre_resid: bfloat16 [32, 256, 2048], P('req', 'ctx'), may hold values from -6 to 6
- block_order: int32 [8], replicated, may hold values from 0 to 7, each once
- dec_new: bfloat16 [4, 32, 576], P(None, 'req')
- dec_qlat: bfloat16 [4, 32, 8, 512], P(None, 'req')
- dec_qrope: bfloat16 [4, 32, 8, 64], P(None, 'req'), may hold values from -6 to 6
- dec_resid: bfloat16 [4, 32, 2048], P(None, 'req'), may hold values from -6 to 6
- cache_len: int32 [4, 32], P(None, 'req'), may hold values from 1 to 2047
- page_table: int32 [4, 32, 32], P(None, 'req', 'ctx'), may hold values from 0 to 31, as said below
- cache_pool: bfloat16 [4096, 64, 576], P(('ctx', 'req')), may hold values from -6 to 6
- w_uv: bfloat16 [8, 512, 128], replicated, may hold values from -0.25 to 0.25
- w_out: bfloat16 [1024, 2048], replicated, may hold values from -0.1875 to 0.1875
- norm_gain: float32 [2048], replicated, may hold values from 0.1 to 1.9
- router: float32 [2048, 64], replicated, may hold values from -0.125 to 0.125
- routes: int32 [8320, 6], P(('ctx', 'req')), may hold values from 0 to 63, all different within a row; in each aligned block of 65 rows (0 to 64, 65 to 129, ...) at most 8 rows name the same one
- w_gate: bfloat16 [128, 2048, 704], P(('ctx', 'req')), may hold values from -0.125 to 0.125
- w_up: bfloat16 [128, 2048, 704], P(('ctx', 'req')), may hold values from -0.125 to 0.125
- w_down: bfloat16 [128, 704, 2048], P(('ctx', 'req')), may hold values from -0.15625 to 0.15625
Outputs:
- pre_out: bfloat16 [32, 256, 2048], P('req', 'ctx')
- dec_out: bfloat16 [4, 32, 2048], P('ctx', 'req')
- cache_out: bfloat16 [4096, 64, 576], P(('ctx', 'req'))
The draws below stay inside these ranges and needn't reach their ends.
Inputs may be any that keep to these rules, and one draw needn't show every extreme that they name: `routes`: each row names 6 different experts; within the rows of one device no expert is named by more than 8 rows. `block_order`: each block appears once. `page_table`: for each request group and each 8 columns held by one ctx device, the entries of the 4 requests name each of that device's 32 pages once.
All inputs are finite; a program needn't handle non-finite values.
Results may differ from the reference program's by a relative error of at most 0.019.
Values may be sent and summed in bfloat16 or wider, within the bound.
A program may use at most 128 MiB of HBM per device.

```python
import math
import jax
import jax.numpy as jnp
import numpy as np
from jax import lax

D = 2048
H = 8
DC = 512
DR = 64
DN = 128
DV = 128
FF = 1408
TOPK = 6
PAGE = 64
PPD = 8
REQ_DEV = 4
PRE_DEV = 64
GROUPS = 32
SEQ = 256
BLK = 32
DL = 576
HALF = 704
E = 64
DEC = 1
R_DEV = 65
CAP = 8
SLOTS = 32
LMAX = 2048
N_CTX = 4
DEVICES = 128


def prefill_base(key):
    latent_base = jax.random.normal(jax.random.fold_in(key, 101), (GROUPS, SEQ, DL), jnp.float32)
    return latent_base


def decode_base(key):
    latent_base = jax.random.normal(jax.random.fold_in(key, 111), (REQ_DEV, GROUPS, DL), jnp.float32)
    return latent_base


def drawn_strength(selector):
    targets = jnp.array([120.0, 200.0, 320.0], jnp.float32)[selector % 3]
    return targets * (DN + DR) ** 0.5 / DC


def draw_pre_latent(key, part):
    return prefill_base(key).astype(jnp.bfloat16)


def draw_pre_qlat(key, part):
    queries = jax.random.normal(jax.random.fold_in(key, 103), (GROUPS, SEQ, H, DC), jnp.float32)
    latent_part = prefill_base(key)[:, :, :DC]
    row_index = jnp.arange(SEQ)
    strength = drawn_strength(row_index // 11)
    picked = row_index % 11 == 0
    aligned = strength[None, :, None, None] * latent_part[:, :, None, :] + 0.1 * queries
    queries = jnp.where(picked[None, :, None, None], aligned, queries)
    return queries.astype(jnp.bfloat16)


def draw_dec_new(key, part):
    return decode_base(key).astype(jnp.bfloat16)


def draw_dec_qlat(key, part):
    queries = jax.random.normal(jax.random.fold_in(key, 113), (REQ_DEV, GROUPS, H, DC), jnp.float32)
    latent_part = decode_base(key)[:, :, :DC]
    group_index = jnp.arange(GROUPS)
    strength = drawn_strength(group_index // 3)
    picked = group_index % 3 == 0
    aligned = strength[None, :, None, None] * latent_part[:, :, None, :] + 0.1 * queries
    queries = jnp.where(picked[None, :, None, None], aligned, queries)
    return queries.astype(jnp.bfloat16)


def draw_cache_len(key, part):
    lengths = jax.random.randint(jax.random.fold_in(key, 201), (REQ_DEV * GROUPS,), 1, LMAX)
    longest = jax.random.randint(jax.random.fold_in(key, 202), (), 0, REQ_DEV * GROUPS)
    lengths = lengths.at[longest].set(LMAX - 1)
    return lengths.reshape(REQ_DEV, GROUPS).astype(jnp.int32)


def draw_page_table(key, part):
    cycle_size = LMAX // (PAGE * PPD)
    subkeys = jax.random.split(jax.random.fold_in(key, 301), GROUPS * cycle_size)
    orders = jax.vmap(lambda subkey: jax.random.permutation(subkey, SLOTS))(subkeys)
    orders = jnp.transpose(orders.reshape(GROUPS, cycle_size, REQ_DEV, PPD), (2, 0, 1, 3))
    return orders.reshape(REQ_DEV, GROUPS, cycle_size * PPD).astype(jnp.int32)


def levels(rng, shape, shards, least, high):
    def one(position, blocks):
        draws = jax.random.uniform(jax.random.fold_in(jax.random.fold_in(rng, 6), position), (blocks,), jnp.float32, least / len(shards), high / len(shards))
        return jnp.repeat(jnp.exp(draws), shape[position] // blocks).reshape((-1,) + (1,) * (len(shape) - position - 1))

    level = one(*shards[0])
    for cut in shards[1:]:
        level = level * one(*cut)
    return level


def deal_out(rng, own, number, rows, amount, top, limit, skew):
    ranking = jax.random.permutation(rng, amount)
    heavy_load, ordinary = portions_of(amount, rows * top, limit, skew, True), portions_of(amount, rows * top, limit, skew, False)
    places = jnp.arange(amount)

    def named(sizes, rotation):
        used = int((sizes > 0).sum())
        fixed = max(1, used // 4)
        shifted = fixed + (places - fixed + rotation * (used - fixed)) % max(1, amount - fixed)
        return jnp.zeros((amount,), jnp.int32).at[ranking[jnp.where(places < fixed, places, shifted)]].set(jnp.asarray(sizes, jnp.int32))

    sizes = jnp.where(number % 4 == 0, named(heavy_load, number // 4), named(ordinary, number - number // 4 - 1))
    mixed = jax.random.permutation(jax.random.fold_in(own, 3), amount)
    donor, sink = mixed[0:amount // 2 * 2:2], mixed[1:amount // 2 * 2:2]
    room = jnp.minimum(sizes[donor] - 1, limit - sizes[sink]) // 2
    room = jnp.where((donor == ranking[0]) | (sink == ranking[0]) | (sizes[sink] == 0), 0, jnp.maximum(room, 0))
    shifted = jax.random.randint(jax.random.fold_in(own, 4), (amount // 2,), 0, 1 << 20) % (room + 1)
    sizes = sizes.at[donor].add(-shifted).at[sink].add(shifted)
    items = jnp.searchsorted(jnp.cumsum(sizes), jnp.arange(rows * top), side="right").astype(jnp.int32)
    grid = items.reshape(top, rows).T
    grid = grid[jax.random.permutation(jax.random.fold_in(own, 1), rows)]
    rotation = jax.random.randint(jax.random.fold_in(own, 2), (rows, 1), 0, top)
    return jnp.take_along_axis(grid, (jnp.arange(top)[None, :] + rotation) % top, axis=1)


def portions_of(number_of, total, most, skew, full):
    loads = [(1 << 20) // math.isqrt(rank ** skew) + 1 for rank in range(1, number_of + 1)]
    largest = most if full else min(most, max(-(-total // number_of), total * loads[0] // sum(loads)))
    least = 1 if total - largest >= number_of - 1 else 0
    given, surplus = [largest] + [least] * (number_of - 1), total - largest - least * (number_of - 1)
    while surplus > 0:
        candidates = [i for i in range(1, number_of) if given[i] < largest] or [i for i in range(1, number_of) if given[i] < most]
        mass, remaining = sum([loads[i] for i in candidates]), surplus
        for i in candidates:
            more = min(most - given[i], max(1, remaining * loads[i] // mass), surplus)
            given[i] = given[i] + more
            surplus = surplus - more
    return np.array(given)


def noise(stream_key, dims, spread, limit, cuts=(), held_as=jnp.bfloat16):
    values = jax.random.normal(stream_key, dims, jnp.float32) * spread
    if len(cuts) > 0:
        values = levels(stream_key, dims, cuts, -0.22, 0.18) * values
    return jnp.clip(values, min=-limit, max=limit).astype(held_as)


def setup_inputs(seed: int = 0) -> dict:
    seeds = jax.random.split(jax.random.key(seed), 21)
    pre_latent = draw_pre_latent(jax.random.fold_in(seeds[20], 71), 0)
    pre_qlat = draw_pre_qlat(jax.random.fold_in(seeds[20], 71), 0)
    pre_qrope = noise(seeds[2], (GROUPS, SEQ, H, DR), 1.0, 6.0, ((0, 32), (1, 4)))
    pre_resid = noise(seeds[3], (GROUPS, SEQ, D), 1.0, 6.0, ((0, 32), (1, 4)))
    block_order = jax.random.permutation(seeds[4], 2 * N_CTX).astype(jnp.int32)
    dec_new = draw_dec_new(jax.random.fold_in(seeds[20], 71), 0)
    dec_qlat = draw_dec_qlat(jax.random.fold_in(seeds[20], 71), 0)
    dec_qrope = noise(seeds[7], (REQ_DEV, GROUPS, H, DR), 1.0, 6.0, ((1, 32),))
    dec_resid = noise(seeds[8], (REQ_DEV, GROUPS, D), 1.0, 6.0, ((1, 32),))
    cache_len = draw_cache_len(jax.random.fold_in(seeds[20], 71), 0)
    page_table = draw_page_table(jax.random.fold_in(seeds[20], 71), 0)
    cache_pool = noise(seeds[11], (N_CTX * GROUPS * SLOTS, PAGE, DL), 1.0, 6.0, ((0, 128),))
    w_uv = noise(seeds[12], (H, DC, DV), DC ** -0.5, 0.25)
    w_out = noise(seeds[13], (H * DV, D), (H * DV) ** -0.5, 0.1875)
    norm_gain = jnp.clip(1.0 + 0.18 * jax.random.normal(seeds[14], (D,), jnp.float32), 0.1, 1.9)
    router = noise(seeds[15], (D, E), D ** -0.5, 0.125, (), jnp.float32)
    routes_keys = jax.random.split(jax.random.fold_in(seeds[16], 1), (DEVICES * R_DEV) // R_DEV)
    routes_turns = jax.random.permutation(jax.random.fold_in(seeds[16], 3), (DEVICES * R_DEV) // R_DEV)
    routes = jax.vmap(lambda own, number: deal_out(jax.random.fold_in(seeds[16], 2), own, number, R_DEV, E, TOPK, CAP, 2))(routes_keys, routes_turns).reshape((DEVICES * R_DEV, TOPK))
    w_gate = noise(seeds[17], (2 * E, D, HALF), D ** -0.5, 0.125, ((0, 128),))
    w_up = noise(seeds[18], (2 * E, D, HALF), D ** -0.5, 0.125, ((0, 128),))
    w_down = noise(seeds[19], (2 * E, HALF, D), FF ** -0.5, 0.15625, ((0, 128),))
    return dict(pre_latent=pre_latent, pre_qlat=pre_qlat, pre_qrope=pre_qrope, pre_resid=pre_resid, block_order=block_order, dec_new=dec_new, dec_qlat=dec_qlat, dec_qrope=dec_qrope, dec_resid=dec_resid, cache_len=cache_len, page_table=page_table, cache_pool=cache_pool, w_uv=w_uv, w_out=w_out, norm_gain=norm_gain, router=router, routes=routes, w_gate=w_gate, w_up=w_up, w_down=w_down)


THETA = 50000.0
ROUTE_SCALE = 2.446
EPSILON = 1e-06
NEG_FILL = -1e+30

def rope_tables(positions, rope_width):
    halfway = rope_width // 2
    inverse = THETA ** (-(jnp.arange(halfway).astype(jnp.float32) * 2.0) / rope_width)
    angles = positions.astype(jnp.float32)[..., None] * inverse
    return (jnp.cos(angles), jnp.sin(angles))

def rotate(values, cos_table, sin_table):
    halfway = values.shape[-1] // 2
    leading = values[..., :halfway].astype(jnp.float32)
    trailing = values[..., halfway:].astype(jnp.float32)
    return jnp.concatenate([leading * cos_table - trailing * sin_table, trailing * cos_table + leading * sin_table], axis=-1)

def attend(queries, stored, query_pos, key_pos):
    score_scale = (DN + DR) ** (-0.5)
    scores = jnp.einsum('qhd,kd->hqk', queries.astype(jnp.float32), stored.astype(jnp.float32)) * score_scale
    visible = (key_pos[None, :] <= query_pos[:, None])[None]
    masked = jnp.where(visible, scores, NEG_FILL)
    largest = lax.optimization_barrier(jnp.max(masked, axis=-1, keepdims=True))
    weights = jnp.where(visible, jnp.exp(masked - largest), 0.0)
    totals = lax.optimization_barrier(jnp.sum(weights, axis=-1))
    rounded = lax.optimization_barrier(weights.astype(jnp.bfloat16))
    mixed = jnp.einsum('hqk,kc->qhc', rounded.astype(jnp.float32), stored[:, :DC].astype(jnp.float32))
    return (mixed / jnp.transpose(totals)[:, :, None]).astype(jnp.bfloat16)

def prefill_sequence(block_order, latent, query_latent, query_rope):
    row_index = jnp.arange(SEQ).astype(jnp.int32)
    positions = block_order[row_index // BLK] * BLK + row_index % BLK
    cos_table, sin_table = rope_tables(positions, DR)
    key_rope = rotate(latent[:, DC:], cos_table, sin_table).astype(jnp.bfloat16)
    stored = jnp.concatenate([latent[:, :DC], key_rope], axis=-1)
    rotated = rotate(query_rope, cos_table[:, None, :], sin_table[:, None, :]).astype(jnp.bfloat16)
    queries = jnp.concatenate([query_latent, rotated], axis=-1)
    return attend(queries, stored, positions, positions)

def project(mixed, resid, w_uv, w_out):
    values = jnp.einsum('nhc,hcv->nhv', mixed.astype(jnp.float32), w_uv.astype(jnp.float32)).astype(jnp.bfloat16)
    output = jnp.dot(values.reshape(values.shape[0], H * DV), w_out, preferred_element_type=jnp.float32)
    return resid.astype(jnp.float32) + output

def expert_half(inputs, gate_part, up_part, down_part):
    gate_out = jnp.dot(inputs, gate_part, preferred_element_type=jnp.float32)
    upward = jnp.dot(inputs, up_part, preferred_element_type=jnp.float32)
    hidden = (jax.nn.silu(gate_out) * upward).astype(jnp.bfloat16)
    return jnp.dot(hidden, down_part, preferred_element_type=jnp.float32).astype(jnp.bfloat16)

def reference(pre_latent, pre_qlat, pre_qrope, pre_resid, block_order, dec_new, dec_qlat, dec_qrope, dec_resid, cache_len, page_table, cache_pool, w_uv, w_out, norm_gain, router, routes, w_gate, w_up, w_down):
    pre_mixed = lax.map(lambda packed: prefill_sequence(block_order, packed[0], packed[1], packed[2]), (pre_latent, pre_qlat, pre_qrope))
    flat_pool = cache_pool.reshape(-1, DL)
    owner_block = (jnp.arange(N_CTX * PPD).astype(jnp.int32) // PPD)[None, None, :] * GROUPS + jnp.arange(GROUPS).astype(jnp.int32)[None, :, None]
    global_page = owner_block * SLOTS + page_table
    cos_new, sin_new = rope_tables(cache_len, DR)
    new_rope = rotate(dec_new[..., DC:], cos_new, sin_new).astype(jnp.bfloat16)
    new_rows = jnp.concatenate([dec_new[..., :DC], new_rope], axis=-1)
    page_of = jnp.take_along_axis(global_page, (cache_len // PAGE)[..., None], axis=2)[..., 0]
    target = page_of * PAGE + cache_len % PAGE
    flat_out = flat_pool.at[target.reshape(-1)].set(new_rows.reshape(-1, DL))
    query_rot = rotate(dec_qrope, cos_new[:, :, None, :], sin_new[:, :, None, :]).astype(jnp.bfloat16)
    dec_queries = jnp.concatenate([dec_qlat, query_rot], axis=-1).reshape(REQ_DEV * GROUPS, H, DL)
    row_index = (global_page[..., None] * PAGE + jnp.arange(PAGE).astype(jnp.int32)).reshape(REQ_DEV * GROUPS, LMAX)
    key_pos = jnp.arange(LMAX).astype(jnp.int32)

    def decode_one(packed):
        stored = flat_out[packed[1]]
        return attend(packed[0][None], stored, packed[2][None], key_pos)[0]
    dec_mixed = lax.map(decode_one, (dec_queries, row_index, cache_len.reshape(-1)))
    pre_hidden = project(pre_mixed.reshape(GROUPS * SEQ, H, DC), pre_resid.reshape(GROUPS * SEQ, D), w_uv, w_out).reshape(GROUPS, SEQ, D)
    dec_hidden = project(dec_mixed, dec_resid.reshape(REQ_DEV * GROUPS, D), w_uv, w_out).reshape(REQ_DEV, GROUPS, D)
    pre_part = jnp.transpose(pre_hidden.reshape(GROUPS, N_CTX, PRE_DEV, D), (1, 0, 2, 3))
    dec_part = jnp.transpose(dec_hidden.reshape(N_CTX, DEC, GROUPS, D), (0, 2, 1, 3))
    row_total = DEVICES * R_DEV
    hidden_rows = jnp.concatenate([pre_part, dec_part], axis=2).reshape(row_total, D)
    normed = (hidden_rows * lax.rsqrt(lax.optimization_barrier(jnp.mean(hidden_rows * hidden_rows, axis=-1, keepdims=True)) + EPSILON) * norm_gain).astype(jnp.bfloat16)
    logits = jnp.dot(normed.astype(jnp.float32), router, precision=lax.Precision.HIGHEST)
    probable = jax.nn.sigmoid(logits)
    chosen = jnp.take_along_axis(probable, routes, axis=1)
    mixing = ROUTE_SCALE * chosen / lax.optimization_barrier(jnp.sum(chosen, axis=1, keepdims=True))
    expert_hits = (routes[:, :, None] == jnp.arange(E).astype(jnp.int32)[None, None, :]).astype(jnp.int32).sum(1)
    grouped = expert_hits.reshape(DEVICES, R_DEV, E)
    before = (jnp.cumsum(grouped, axis=1) - grouped).reshape(row_total, E)
    slot_index = jnp.take_along_axis(before, routes, axis=1)
    device_of = (jnp.arange(row_total).astype(jnp.int32) // R_DEV)[:, None]
    target_slot = ((routes * DEVICES + device_of) * CAP + slot_index).reshape(-1)
    row_ids = jnp.repeat(jnp.arange(row_total).astype(jnp.int32), TOPK)
    slot_table = jnp.full((E * DEVICES * CAP,), row_total, jnp.int32).at[target_slot].set(row_ids)
    weight_table = jnp.zeros((E * DEVICES * CAP,), jnp.float32).at[target_slot].set(mixing.reshape(-1))
    padded = jnp.concatenate([normed, jnp.zeros((1, D), jnp.bfloat16)], axis=0)

    def one_expert(running, packed):
        rows_e, weights_e, gate_e, up_e, down_e = packed
        inputs = padded[rows_e]
        leading = expert_half(inputs, gate_e[0], up_e[0], down_e[0])
        trailing = expert_half(inputs, gate_e[1], up_e[1], down_e[1])
        result = (leading.astype(jnp.float32) + trailing.astype(jnp.float32)).astype(jnp.bfloat16)
        return (running.at[rows_e].add(weights_e[:, None] * result.astype(jnp.float32), mode='drop'), None)
    moe, unused = lax.scan(one_expert, jnp.zeros((row_total, D), jnp.float32), (slot_table.reshape(E, -1), weight_table.reshape(E, -1), w_gate.reshape(E, 2, D, HALF), w_up.reshape(E, 2, D, HALF), w_down.reshape(E, 2, HALF, D)))
    final = (hidden_rows + moe).astype(jnp.bfloat16).reshape(N_CTX, GROUPS, R_DEV, D)
    pre_out = jnp.transpose(final[:, :, :PRE_DEV], (1, 0, 2, 3)).reshape(GROUPS, SEQ, D)
    dec_out = jnp.transpose(final[:, :, PRE_DEV:], (0, 2, 1, 3)).reshape(REQ_DEV, GROUPS, D)
    return (pre_out, dec_out, flat_out.reshape(cache_pool.shape))
```

```python
import jax
import jax.numpy as jnp
from jax import lax
from jax.sharding import PartitionSpec as P

DC = 512
DR = 64
DN = 128


THETA = 50000.0
ROUTE_SCALE = 2.446
EPSILON = 1e-06
NEG_FILL = -1e30


def joined(part, axis, combine):
    gathered = jax.tree.map(lambda a: lax.all_gather(a, axis), part)

    def take(source):
        return jax.tree.map(lambda a: lax.dynamic_index_in_dim(a, source, 0, False), gathered)

    return lax.fori_loop(
        1, lax.axis_size(axis), lambda source, state: combine(state, take(source)), take(0)
    )


def rope_tables(positions, rope_width):
    halfway = rope_width // 2
    inverse = THETA ** (-(jnp.arange(halfway).astype(jnp.float32) * 2.0) / rope_width)
    angles = positions.astype(jnp.float32)[..., None] * inverse
    return (jnp.cos(angles), jnp.sin(angles))


def rotate(values, cos_table, sin_table):
    halfway = values.shape[-1] // 2
    leading = values[..., :halfway].astype(jnp.float32)
    trailing = values[..., halfway:].astype(jnp.float32)
    return jnp.concatenate(
        [leading * cos_table - trailing * sin_table, trailing * cos_table + leading * sin_table],
        axis=-1,
    )


def block_position(block_order, global_rows, shard_rows):
    shard_id = global_rows // shard_rows
    within = global_rows % shard_rows
    half_rows = shard_rows // 2
    return block_order[2 * shard_id + within // half_rows] * half_rows + within % half_rows


def expert_half(inputs, gate_part, up_part, down_part):
    flat_rows = inputs.reshape(-1, inputs.shape[-1])
    gate_out = jnp.dot(flat_rows, gate_part, preferred_element_type=jnp.float32)
    upward = jnp.dot(flat_rows, up_part, preferred_element_type=jnp.float32)
    hidden = (jax.nn.silu(gate_out) * upward).astype(jnp.bfloat16)
    partial_out = jnp.dot(hidden, down_part, preferred_element_type=jnp.float32).astype(
        jnp.bfloat16
    )
    return partial_out.reshape(inputs.shape)


def merge_softmax(earlier, later):
    left_peak, left_total, left_accum = earlier
    right_peak, right_total, right_accum = later
    new_peak = jnp.maximum(left_peak, right_peak)
    left_factor = jnp.exp(left_peak - new_peak)
    right_factor = jnp.exp(right_peak - new_peak)
    merged_total = left_total * left_factor + right_total * right_factor
    merged_accum = left_accum * left_factor[..., None] + right_accum * right_factor[..., None]
    return (new_peak, merged_total, merged_accum)


def body(
    pre_latent,
    pre_qlat,
    pre_qrope,
    pre_resid,
    block_order,
    dec_new,
    dec_qlat,
    dec_qrope,
    dec_resid,
    cache_len,
    page_table,
    cache_pool,
    w_uv,
    w_out,
    norm_gain,
    router,
    routes,
    w_gate,
    w_up,
    w_down,
):
    ctx_count = lax.axis_size("ctx")
    ctx_index = lax.axis_index("ctx")
    score_scale = (DN + DR) ** (-0.5)
    latent = pre_latent[0]
    shard_rows = latent.shape[0]
    local_rows = jnp.arange(shard_rows)
    own_pos = block_position(block_order, ctx_index * shard_rows + local_rows, shard_rows)
    cos_table, sin_table = rope_tables(own_pos, DR)
    key_rope = rotate(latent[:, DC:], cos_table, sin_table).astype(jnp.bfloat16)
    stored = jnp.concatenate([latent[:, :DC], key_rope], axis=-1)
    rotated = rotate(pre_qrope[0], cos_table[:, None, :], sin_table[:, None, :]).astype(
        jnp.bfloat16
    )
    queries = jnp.concatenate([pre_qlat[0], rotated], axis=-1)
    head_count = queries.shape[1]

    lengths = cache_len[:, 0]
    tables = page_table[:, 0, :]
    request_count = tables.shape[0]
    pages_dev = tables.shape[1]
    page_rows = cache_pool.shape[1]
    slot_count = cache_pool.shape[0]
    row_width = cache_pool.shape[2]
    cos_new, sin_new = rope_tables(lengths, DR)
    new_rope = rotate(dec_new[:, 0, DC:], cos_new, sin_new).astype(jnp.bfloat16)
    new_rows = jnp.concatenate([dec_new[:, 0, :DC], new_rope], axis=-1)
    page_index = lengths // page_rows
    owner_ctx = page_index // pages_dev
    page_hit = tables[:, :, None] == jnp.arange(slot_count)[None, None, :]
    slot_of = jnp.sum(
        jnp.where((jnp.arange(pages_dev)[None, :] == (page_index % pages_dev)[:, None])[:, :, None],
                  page_hit, False).astype(jnp.int32) * jnp.arange(slot_count)[None, None, :],
        axis=(1, 2),
    )
    flat_pool = cache_pool.reshape(slot_count * page_rows, row_width)
    for request in range(request_count):
        owned = owner_ctx[request] == ctx_index
        spot = jnp.where(owned, slot_of[request] * page_rows + lengths[request] % page_rows, 0)
        old_row = lax.dynamic_slice_in_dim(flat_pool, spot, 1, 0)
        row = jnp.where(owned, new_rows[request][None], old_row)
        flat_pool = lax.dynamic_update_slice_in_dim(flat_pool, row, spot, 0)
    page_valid = jnp.any(page_hit, axis=1)
    page_logical = jnp.sum(page_hit.astype(jnp.int32) * jnp.arange(pages_dev)[None, :, None], axis=1)
    page_start = (ctx_index * pages_dev + page_logical) * page_rows
    key_pos = (page_start[:, :, None] + jnp.arange(page_rows)[None, None, :]).reshape(
        request_count, slot_count * page_rows
    )
    dec_visible = (
        jnp.repeat(page_valid, page_rows, axis=1) & (key_pos <= lengths[:, None])
    )[:, None, :]
    query_rot = rotate(dec_qrope[:, 0], cos_new[:, None, :], sin_new[:, None, :]).astype(
        jnp.bfloat16
    )
    dec_queries = jnp.concatenate([dec_qlat[:, 0], query_rot], axis=-1)
    dec_scores = (
        jnp.einsum("rhd,kd->rhk", dec_queries, flat_pool, preferred_element_type=jnp.float32)
        * score_scale
    )
    dec_masked = jnp.where(dec_visible, dec_scores, NEG_FILL)
    local_peak = jnp.max(dec_masked, axis=-1)
    dec_weights = jnp.where(dec_visible, jnp.exp(dec_masked - local_peak[..., None]), 0.0)
    local_total = jnp.sum(dec_weights, axis=-1)
    local_accum = jnp.einsum(
        "rhk,kc->rhc",
        dec_weights.astype(jnp.bfloat16),
        flat_pool[:, :DC],
        preferred_element_type=jnp.float32,
    )

    dec_block = jnp.concatenate(
        [
            local_accum.reshape(request_count * head_count, DC),
            local_peak.reshape(-1, 1),
            local_total.reshape(-1, 1),
            jnp.zeros((request_count * head_count, row_width - DC - 2), jnp.float32),
        ],
        axis=1,
    )
    packed = jnp.concatenate([stored.astype(jnp.float32), dec_block], axis=0)
    gathered = lax.all_gather(packed, "ctx")
    moving = gathered[:, :shard_rows].reshape(ctx_count * shard_rows, row_width).astype(jnp.bfloat16)
    dec_parts = gathered[:, shard_rows:].reshape(ctx_count, request_count, head_count, row_width)
    dec_share = request_count // ctx_count
    own_parts = lax.dynamic_slice_in_dim(dec_parts, ctx_index * dec_share, dec_share, 1)
    part_accum = own_parts[..., :DC]
    part_peak = own_parts[..., DC]
    part_total = own_parts[..., DC + 1]
    merged_peak = jnp.max(part_peak, axis=0)
    factor = jnp.exp(part_peak - merged_peak[None])
    merged_total = jnp.sum(part_total * factor, axis=0)
    merged_accum = jnp.sum(part_accum * factor[..., None], axis=0)
    own_mixed = (merged_accum / merged_total[..., None]).astype(jnp.bfloat16)

    key_pos_pre = block_position(block_order, jnp.arange(moving.shape[0]), shard_rows)
    scores = (
        jnp.einsum("qhd,kd->hqk", queries, moving, preferred_element_type=jnp.float32) * score_scale
    )
    visible = (key_pos_pre[None, :] <= own_pos[:, None])[None]
    masked = jnp.where(visible, scores, NEG_FILL)
    new_peak = jnp.max(masked, axis=-1)
    weights = jnp.where(visible, jnp.exp(masked - new_peak[..., None]), 0.0)
    totals = jnp.sum(weights, axis=-1)
    accumulated = jnp.einsum(
        "hqk,kc->qhc",
        weights.astype(jnp.bfloat16),
        moving[:, :DC],
        preferred_element_type=jnp.float32,
    )
    pre_mixed = (accumulated / jnp.transpose(totals)[:, :, None]).astype(jnp.bfloat16)

    own_resid = lax.dynamic_slice_in_dim(dec_resid[:, 0], ctx_index * dec_share, dec_share, 0)
    mixed_all = jnp.concatenate([pre_mixed, own_mixed], axis=0)
    resid_all = jnp.concatenate([pre_resid[0], own_resid], axis=0)
    values = jnp.einsum("nhc,hcv->nhv", mixed_all, w_uv, preferred_element_type=jnp.float32).astype(
        jnp.bfloat16
    )
    hidden_state = resid_all.astype(jnp.float32) + jnp.dot(
        values.reshape(values.shape[0], -1), w_out, preferred_element_type=jnp.float32
    )
    normed = (
        hidden_state
        * lax.rsqrt(jnp.mean(hidden_state * hidden_state, axis=-1, keepdims=True) + EPSILON)
        * norm_gain
    ).astype(jnp.bfloat16)
    logits = jnp.dot(normed.astype(jnp.float32), router, precision=lax.Precision.HIGHEST)
    probable = jax.nn.sigmoid(logits)
    row_count = normed.shape[0]
    width = normed.shape[1]
    top_count = routes.shape[1]
    expert_count = router.shape[1]
    devices = ctx_count * lax.axis_size("req")
    capacity = 2 * ((row_count * top_count + 2 * expert_count - 1) // (2 * expert_count))
    route_hit = routes[:, :, None] == jnp.arange(expert_count)[None, None, :]
    chosen = jnp.sum(jnp.where(route_hit, probable[:, None, :], 0.0), axis=-1)
    mixing = ROUTE_SCALE * chosen / jnp.sum(chosen, axis=1, keepdims=True)
    expert_hits = route_hit.astype(jnp.int32).sum(1)
    earlier = (jnp.arange(row_count)[None, :] < jnp.arange(row_count)[:, None]).astype(jnp.bfloat16)
    before = jnp.dot(
        earlier, expert_hits.astype(jnp.bfloat16), preferred_element_type=jnp.float32
    ).astype(jnp.int32)
    slot_index = jnp.sum(jnp.where(route_hit, before[:, None, :], 0), axis=-1)
    target_slot = routes * capacity + slot_index
    slot_hit = target_slot[:, :, None] == jnp.arange(expert_count * capacity)[None, None, :]
    dispatch = jnp.any(slot_hit, axis=1).astype(jnp.bfloat16)
    outgoing = lax.dot_general(
        dispatch, normed, (((0,), (0,)), ((), ())), preferred_element_type=jnp.float32
    ).astype(jnp.bfloat16).reshape(expert_count, capacity, width)
    doubled = jnp.broadcast_to(outgoing[:, None], (expert_count, 2, capacity, width)).reshape(
        devices, capacity, width
    )
    partial_out = expert_half(
        lax.all_to_all(doubled, ("ctx", "req"), split_axis=0, concat_axis=0, tiled=True),
        w_gate[0],
        w_up[0],
        w_down[0],
    )
    returned = lax.all_to_all(
        partial_out, ("ctx", "req"), split_axis=0, concat_axis=0, tiled=True
    ).reshape(expert_count, 2, capacity, width)
    results = (returned[:, 0].astype(jnp.float32) + returned[:, 1].astype(jnp.float32)).astype(
        jnp.bfloat16
    ).reshape(expert_count * capacity, width)
    combine = jnp.sum(jnp.where(slot_hit, mixing[:, :, None], 0.0), axis=1)
    moe = jnp.dot(combine, results.astype(jnp.float32), precision=lax.Precision.HIGHEST)
    final = (hidden_state + moe).astype(jnp.bfloat16)
    pre_out = final[:shard_rows][None]
    dec_out = final[shard_rows:][:, None]
    cache_out = flat_pool.reshape(cache_pool.shape)
    return (pre_out, dec_out, cache_out)


def solution(mesh):
    in_specs = (
        P("req", "ctx", None),
        P("req", "ctx", None, None),
        P("req", "ctx", None, None),
        P("req", "ctx", None),
        P(),
        P(None, "req", None),
        P(None, "req", None, None),
        P(None, "req", None, None),
        P(None, "req", None),
        P(None, "req"),
        P(None, "req", "ctx"),
        P(("ctx", "req"), None, None),
        P(),
        P(),
        P(),
        P(),
        P(("ctx", "req"), None),
        P(("ctx", "req"), None, None),
        P(("ctx", "req"), None, None),
        P(("ctx", "req"), None, None),
    )
    out_specs = (P("req", "ctx", None), P("ctx", "req", None), P(("ctx", "req"), None, None))
    return jax.shard_map(body, mesh=mesh, in_specs=in_specs, out_specs=out_specs, check_vma=False)
```

```python
import functools

import jax
import jax.numpy as jnp
from jax import lax
from jax.experimental import pallas as pl
from jax.experimental.pallas import tpu as pltpu
from jax.sharding import PartitionSpec as P

MESH = pl.DeviceIdType.MESH

DC = 512
DR = 64
DN = 128


THETA = 50000.0
ROUTE_SCALE = 2.446
EPSILON = 1e-06
NEG_FILL = -1e30


def joined(part, axis, combine):
    gathered = jax.tree.map(lambda a: lax.all_gather(a, axis), part)

    def take(source):
        return jax.tree.map(lambda a: lax.dynamic_index_in_dim(a, source, 0, False), gathered)

    return lax.fori_loop(
        1, lax.axis_size(axis), lambda source, state: combine(state, take(source)), take(0)
    )


def rope_tables(positions, rope_width):
    halfway = rope_width // 2
    inverse = THETA ** (-(jnp.arange(halfway).astype(jnp.float32) * 2.0) / rope_width)
    angles = positions.astype(jnp.float32)[..., None] * inverse
    return (jnp.cos(angles), jnp.sin(angles))


def rotate(values, cos_table, sin_table):
    halfway = values.shape[-1] // 2
    leading = values[..., :halfway].astype(jnp.float32)
    trailing = values[..., halfway:].astype(jnp.float32)
    return jnp.concatenate(
        [leading * cos_table - trailing * sin_table, trailing * cos_table + leading * sin_table],
        axis=-1,
    )


def block_position(block_order, global_rows, shard_rows):
    shard_id = global_rows // shard_rows
    within = global_rows % shard_rows
    half_rows = shard_rows // 2
    return block_order[2 * shard_id + within // half_rows] * half_rows + within % half_rows


def expert_half(inputs, gate_part, up_part, down_part):
    flat_rows = inputs.reshape(-1, inputs.shape[-1])
    gate_out = jnp.dot(flat_rows, gate_part, preferred_element_type=jnp.float32)
    upward = jnp.dot(flat_rows, up_part, preferred_element_type=jnp.float32)
    hidden = (jax.nn.silu(gate_out) * upward).astype(jnp.bfloat16)
    partial_out = jnp.dot(hidden, down_part, preferred_element_type=jnp.float32).astype(
        jnp.bfloat16
    )
    return partial_out.reshape(inputs.shape)


def merge_softmax(earlier, later):
    left_peak, left_total, left_accum = earlier
    right_peak, right_total, right_accum = later
    new_peak = jnp.maximum(left_peak, right_peak)
    left_factor = jnp.exp(left_peak - new_peak)
    right_factor = jnp.exp(right_peak - new_peak)
    merged_total = left_total * left_factor + right_total * right_factor
    merged_accum = left_accum * left_factor[..., None] + right_accum * right_factor[..., None]
    return (new_peak, merged_total, merged_accum)


def exchange_kernel(n_req, total, x_ref, out_ref, send_sem, recv_sem, local_sem):
    me = lax.axis_index("ctx") * n_req + lax.axis_index("req")

    def device(d):
        return (d // n_req, d % n_req)

    def outgoing(d):
        return pltpu.make_async_remote_copy(
            src_ref=x_ref.at[d],
            dst_ref=out_ref.at[me],
            send_sem=send_sem.at[d],
            recv_sem=recv_sem.at[me],
            device_id=device(d),
            device_id_type=MESH,
        )

    def incoming(s):
        return pltpu.make_async_remote_copy(
            src_ref=x_ref.at[me],
            dst_ref=out_ref.at[s],
            send_sem=send_sem.at[s],
            recv_sem=recv_sem.at[s],
            device_id=device(s),
            device_id_type=MESH,
        )

    barrier = pltpu.get_barrier_semaphore()

    def greet(k, carry):
        d = lax.rem(me + k, total)
        pl.semaphore_signal(barrier, inc=1, device_id=device(d), device_id_type=MESH)
        return carry

    lax.fori_loop(1, total, greet, 0)
    pl.semaphore_wait(barrier, total - 1)
    local = pltpu.make_async_copy(x_ref.at[me], out_ref.at[me], local_sem)
    local.start()

    def send(k, carry):
        outgoing(lax.rem(me + k, total)).start()
        return carry

    lax.fori_loop(1, total, send, 0)

    def finish(k, carry):
        outgoing(lax.rem(me + k, total)).wait_send()
        incoming(lax.rem(me + total - k, total)).wait_recv()
        return carry

    lax.fori_loop(1, total, finish, 0)
    local.wait()


def exchange(x, n_req, total, collective_id):
    return pl.pallas_call(
        functools.partial(exchange_kernel, n_req, total),
        out_shape=jax.ShapeDtypeStruct(x.shape, x.dtype),
        in_specs=[pl.BlockSpec(memory_space=pl.ANY)],
        out_specs=pl.BlockSpec(memory_space=pl.ANY),
        scratch_shapes=[
            pltpu.SemaphoreType.DMA((total,)),
            pltpu.SemaphoreType.DMA((total,)),
            pltpu.SemaphoreType.DMA(()),
        ],
        compiler_params=pltpu.CompilerParams(collective_id=collective_id, has_side_effects=True),
    )(x)


def body(
    pre_latent,
    pre_qlat,
    pre_qrope,
    pre_resid,
    block_order,
    dec_new,
    dec_qlat,
    dec_qrope,
    dec_resid,
    cache_len,
    page_table,
    cache_pool,
    w_uv,
    w_out,
    norm_gain,
    router,
    routes,
    w_gate,
    w_up,
    w_down,
):
    ctx_count = lax.axis_size("ctx")
    ctx_index = lax.axis_index("ctx")
    score_scale = (DN + DR) ** (-0.5)
    latent = pre_latent[0]
    shard_rows = latent.shape[0]
    local_rows = jnp.arange(shard_rows)
    own_pos = block_position(block_order, ctx_index * shard_rows + local_rows, shard_rows)
    cos_table, sin_table = rope_tables(own_pos, DR)
    key_rope = rotate(latent[:, DC:], cos_table, sin_table).astype(jnp.bfloat16)
    stored = jnp.concatenate([latent[:, :DC], key_rope], axis=-1)
    rotated = rotate(pre_qrope[0], cos_table[:, None, :], sin_table[:, None, :]).astype(
        jnp.bfloat16
    )
    queries = jnp.concatenate([pre_qlat[0], rotated], axis=-1)
    head_count = queries.shape[1]

    lengths = cache_len[:, 0]
    tables = page_table[:, 0, :]
    request_count = tables.shape[0]
    pages_dev = tables.shape[1]
    page_rows = cache_pool.shape[1]
    slot_count = cache_pool.shape[0]
    row_width = cache_pool.shape[2]
    cos_new, sin_new = rope_tables(lengths, DR)
    new_rope = rotate(dec_new[:, 0, DC:], cos_new, sin_new).astype(jnp.bfloat16)
    new_rows = jnp.concatenate([dec_new[:, 0, :DC], new_rope], axis=-1)
    page_index = lengths // page_rows
    owner_ctx = page_index // pages_dev
    page_hit = tables[:, :, None] == jnp.arange(slot_count)[None, None, :]
    slot_of = jnp.sum(
        jnp.where((jnp.arange(pages_dev)[None, :] == (page_index % pages_dev)[:, None])[:, :, None],
                  page_hit, False).astype(jnp.int32) * jnp.arange(slot_count)[None, None, :],
        axis=(1, 2),
    )
    flat_pool = cache_pool.reshape(slot_count * page_rows, row_width)
    for request in range(request_count):
        owned = owner_ctx[request] == ctx_index
        spot = jnp.where(owned, slot_of[request] * page_rows + lengths[request] % page_rows, 0)
        old_row = lax.dynamic_slice_in_dim(flat_pool, spot, 1, 0)
        row = jnp.where(owned, new_rows[request][None], old_row)
        flat_pool = lax.dynamic_update_slice_in_dim(flat_pool, row, spot, 0)
    page_valid = jnp.any(page_hit, axis=1)
    page_logical = jnp.sum(page_hit.astype(jnp.int32) * jnp.arange(pages_dev)[None, :, None], axis=1)
    page_start = (ctx_index * pages_dev + page_logical) * page_rows
    key_pos = (page_start[:, :, None] + jnp.arange(page_rows)[None, None, :]).reshape(
        request_count, slot_count * page_rows
    )
    dec_visible = (
        jnp.repeat(page_valid, page_rows, axis=1) & (key_pos <= lengths[:, None])
    )[:, None, :]
    query_rot = rotate(dec_qrope[:, 0], cos_new[:, None, :], sin_new[:, None, :]).astype(
        jnp.bfloat16
    )
    dec_queries = jnp.concatenate([dec_qlat[:, 0], query_rot], axis=-1)
    dec_scores = (
        jnp.einsum("rhd,kd->rhk", dec_queries, flat_pool, preferred_element_type=jnp.float32)
        * score_scale
    )
    dec_masked = jnp.where(dec_visible, dec_scores, NEG_FILL)
    local_peak = jnp.max(dec_masked, axis=-1)
    dec_weights = jnp.where(dec_visible, jnp.exp(dec_masked - local_peak[..., None]), 0.0)
    local_total = jnp.sum(dec_weights, axis=-1)
    local_accum = jnp.einsum(
        "rhk,kc->rhc",
        dec_weights.astype(jnp.bfloat16),
        flat_pool[:, :DC],
        preferred_element_type=jnp.float32,
    )

    dec_block = jnp.concatenate(
        [
            local_accum.reshape(request_count * head_count, DC),
            local_peak.reshape(-1, 1),
            local_total.reshape(-1, 1),
            jnp.zeros((request_count * head_count, row_width - DC - 2), jnp.float32),
        ],
        axis=1,
    )
    packed = jnp.concatenate([stored.astype(jnp.float32), dec_block], axis=0)
    gathered = lax.all_gather(packed, "ctx")
    moving = gathered[:, :shard_rows].reshape(ctx_count * shard_rows, row_width).astype(jnp.bfloat16)
    dec_parts = gathered[:, shard_rows:].reshape(ctx_count, request_count, head_count, row_width)
    dec_share = request_count // ctx_count
    own_parts = lax.dynamic_slice_in_dim(dec_parts, ctx_index * dec_share, dec_share, 1)
    part_accum = own_parts[..., :DC]
    part_peak = own_parts[..., DC]
    part_total = own_parts[..., DC + 1]
    merged_peak = jnp.max(part_peak, axis=0)
    factor = jnp.exp(part_peak - merged_peak[None])
    merged_total = jnp.sum(part_total * factor, axis=0)
    merged_accum = jnp.sum(part_accum * factor[..., None], axis=0)
    own_mixed = (merged_accum / merged_total[..., None]).astype(jnp.bfloat16)

    key_pos_pre = block_position(block_order, jnp.arange(moving.shape[0]), shard_rows)
    scores = (
        jnp.einsum("qhd,kd->hqk", queries, moving, preferred_element_type=jnp.float32) * score_scale
    )
    visible = (key_pos_pre[None, :] <= own_pos[:, None])[None]
    masked = jnp.where(visible, scores, NEG_FILL)
    new_peak = jnp.max(masked, axis=-1)
    weights = jnp.where(visible, jnp.exp(masked - new_peak[..., None]), 0.0)
    totals = jnp.sum(weights, axis=-1)
    accumulated = jnp.einsum(
        "hqk,kc->qhc",
        weights.astype(jnp.bfloat16),
        moving[:, :DC],
        preferred_element_type=jnp.float32,
    )
    pre_mixed = (accumulated / jnp.transpose(totals)[:, :, None]).astype(jnp.bfloat16)

    own_resid = lax.dynamic_slice_in_dim(dec_resid[:, 0], ctx_index * dec_share, dec_share, 0)
    mixed_all = jnp.concatenate([pre_mixed, own_mixed], axis=0)
    resid_all = jnp.concatenate([pre_resid[0], own_resid], axis=0)
    values = jnp.einsum("nhc,hcv->nhv", mixed_all, w_uv, preferred_element_type=jnp.float32).astype(
        jnp.bfloat16
    )
    hidden_state = resid_all.astype(jnp.float32) + jnp.dot(
        values.reshape(values.shape[0], -1), w_out, preferred_element_type=jnp.float32
    )
    normed = (
        hidden_state
        * lax.rsqrt(jnp.mean(hidden_state * hidden_state, axis=-1, keepdims=True) + EPSILON)
        * norm_gain
    ).astype(jnp.bfloat16)
    logits = jnp.dot(normed.astype(jnp.float32), router, precision=lax.Precision.HIGHEST)
    probable = jax.nn.sigmoid(logits)
    row_count = normed.shape[0]
    width = normed.shape[1]
    top_count = routes.shape[1]
    expert_count = router.shape[1]
    devices = ctx_count * lax.axis_size("req")
    capacity = 2 * ((row_count * top_count + 2 * expert_count - 1) // (2 * expert_count))
    route_hit = routes[:, :, None] == jnp.arange(expert_count)[None, None, :]
    chosen = jnp.sum(jnp.where(route_hit, probable[:, None, :], 0.0), axis=-1)
    mixing = ROUTE_SCALE * chosen / jnp.sum(chosen, axis=1, keepdims=True)
    expert_hits = route_hit.astype(jnp.int32).sum(1)
    earlier = (jnp.arange(row_count)[None, :] < jnp.arange(row_count)[:, None]).astype(jnp.bfloat16)
    before = jnp.dot(
        earlier, expert_hits.astype(jnp.bfloat16), preferred_element_type=jnp.float32
    ).astype(jnp.int32)
    slot_index = jnp.sum(jnp.where(route_hit, before[:, None, :], 0), axis=-1)
    target_slot = routes * capacity + slot_index
    slot_hit = target_slot[:, :, None] == jnp.arange(expert_count * capacity)[None, None, :]
    dispatch = jnp.any(slot_hit, axis=1).astype(jnp.bfloat16)
    outgoing = lax.dot_general(
        dispatch, normed, (((0,), (0,)), ((), ())), preferred_element_type=jnp.float32
    ).astype(jnp.bfloat16).reshape(expert_count, capacity, width)
    doubled = jnp.broadcast_to(outgoing[:, None], (expert_count, 2, capacity, width)).reshape(
        devices, capacity, width
    )
    req_count = lax.axis_size("req")
    partial_out = expert_half(
        exchange(doubled, req_count, devices, 0),
        w_gate[0],
        w_up[0],
        w_down[0],
    )
    returned = exchange(partial_out, req_count, devices, 1).reshape(
        expert_count, 2, capacity, width
    )
    results = (returned[:, 0].astype(jnp.float32) + returned[:, 1].astype(jnp.float32)).astype(
        jnp.bfloat16
    ).reshape(expert_count * capacity, width)
    combine = jnp.sum(jnp.where(slot_hit, mixing[:, :, None], 0.0), axis=1)
    moe = jnp.dot(combine, results.astype(jnp.float32), precision=lax.Precision.HIGHEST)
    final = (hidden_state + moe).astype(jnp.bfloat16)
    pre_out = final[:shard_rows][None]
    dec_out = final[shard_rows:][:, None]
    cache_out = flat_pool.reshape(cache_pool.shape)
    return (pre_out, dec_out, cache_out)


def solution(mesh):
    in_specs = (
        P("req", "ctx", None),
        P("req", "ctx", None, None),
        P("req", "ctx", None, None),
        P("req", "ctx", None),
        P(),
        P(None, "req", None),
        P(None, "req", None, None),
        P(None, "req", None, None),
        P(None, "req", None),
        P(None, "req"),
        P(None, "req", "ctx"),
        P(("ctx", "req"), None, None),
        P(),
        P(),
        P(),
        P(),
        P(("ctx", "req"), None),
        P(("ctx", "req"), None, None),
        P(("ctx", "req"), None, None),
        P(("ctx", "req"), None, None),
    )
    out_specs = (P("req", "ctx", None), P("ctx", "req", None), P(("ctx", "req"), None, None))
    return jax.shard_map(body, mesh=mesh, in_specs=in_specs, out_specs=out_specs, check_vma=False)
```

```python
import functools

import jax
import jax.numpy as jnp
from jax import lax
from jax.experimental import pallas as pl
from jax.experimental.pallas import tpu as pltpu
from jax.sharding import PartitionSpec as P

MESH = pl.DeviceIdType.MESH

DC = 512
DR = 64
DN = 128


THETA = 50000.0
ROUTE_SCALE = 2.446
EPSILON = 1e-06
NEG_FILL = -1e30


def joined(part, axis, combine):
    gathered = jax.tree.map(lambda a: lax.all_gather(a, axis), part)

    def take(source):
        return jax.tree.map(lambda a: lax.dynamic_index_in_dim(a, source, 0, False), gathered)

    return lax.fori_loop(
        1, lax.axis_size(axis), lambda source, state: combine(state, take(source)), take(0)
    )


def rope_tables(positions, rope_width):
    halfway = rope_width // 2
    inverse = THETA ** (-(jnp.arange(halfway).astype(jnp.float32) * 2.0) / rope_width)
    angles = positions.astype(jnp.float32)[..., None] * inverse
    return (jnp.cos(angles), jnp.sin(angles))


def rotate(values, cos_table, sin_table):
    halfway = values.shape[-1] // 2
    leading = values[..., :halfway].astype(jnp.float32)
    trailing = values[..., halfway:].astype(jnp.float32)
    return jnp.concatenate(
        [leading * cos_table - trailing * sin_table, trailing * cos_table + leading * sin_table],
        axis=-1,
    )


def block_position(block_order, global_rows, shard_rows):
    half_rows = shard_rows // 2
    block = global_rows // half_rows
    hit = block[:, None] == jnp.arange(block_order.shape[0])[None, :]
    logical = jnp.sum(jnp.where(hit, block_order[None, :], 0), axis=1)
    return logical * half_rows + global_rows % half_rows


def expert_half(inputs, gate_part, up_part, down_part):
    flat_rows = inputs.reshape(-1, inputs.shape[-1])
    gate_out = jnp.dot(flat_rows, gate_part, preferred_element_type=jnp.float32)
    upward = jnp.dot(flat_rows, up_part, preferred_element_type=jnp.float32)
    hidden = (jax.nn.silu(gate_out) * upward).astype(jnp.bfloat16)
    partial_out = jnp.dot(hidden, down_part, preferred_element_type=jnp.float32).astype(
        jnp.bfloat16
    )
    return partial_out.reshape(inputs.shape)


def merge_softmax(earlier, later):
    left_peak, left_total, left_accum = earlier
    right_peak, right_total, right_accum = later
    new_peak = jnp.maximum(left_peak, right_peak)
    left_factor = jnp.exp(left_peak - new_peak)
    right_factor = jnp.exp(right_peak - new_peak)
    merged_total = left_total * left_factor + right_total * right_factor
    merged_accum = left_accum * left_factor[..., None] + right_accum * right_factor[..., None]
    return (new_peak, merged_total, merged_accum)


def exchange_kernel(n_req, total, x_ref, out_ref, send_sem, recv_sem, local_sem):
    me = lax.axis_index("ctx") * n_req + lax.axis_index("req")

    def device(d):
        return (d // n_req, d % n_req)

    def outgoing(d):
        return pltpu.make_async_remote_copy(
            src_ref=x_ref.at[d],
            dst_ref=out_ref.at[me],
            send_sem=send_sem.at[d],
            recv_sem=recv_sem.at[me],
            device_id=device(d),
            device_id_type=MESH,
        )

    def incoming(s):
        return pltpu.make_async_remote_copy(
            src_ref=x_ref.at[me],
            dst_ref=out_ref.at[s],
            send_sem=send_sem.at[s],
            recv_sem=recv_sem.at[s],
            device_id=device(s),
            device_id_type=MESH,
        )

    barrier = pltpu.get_barrier_semaphore()

    def greet(k, carry):
        d = lax.rem(me + k, total)
        pl.semaphore_signal(barrier, inc=1, device_id=device(d), device_id_type=MESH)
        return carry

    lax.fori_loop(1, total, greet, 0)
    pl.semaphore_wait(barrier, total - 1)
    local = pltpu.make_async_copy(x_ref.at[me], out_ref.at[me], local_sem)
    local.start()

    def send(k, carry):
        outgoing(lax.rem(me + k, total)).start()
        return carry

    lax.fori_loop(1, total, send, 0)

    def finish(k, carry):
        outgoing(lax.rem(me + k, total)).wait_send()
        incoming(lax.rem(me + total - k, total)).wait_recv()
        return carry

    lax.fori_loop(1, total, finish, 0)
    local.wait()


def exchange(x, n_req, total, collective_id):
    return pl.pallas_call(
        functools.partial(exchange_kernel, n_req, total),
        out_shape=jax.ShapeDtypeStruct(x.shape, x.dtype),
        in_specs=[pl.BlockSpec(memory_space=pl.ANY)],
        out_specs=pl.BlockSpec(memory_space=pl.ANY),
        scratch_shapes=[
            pltpu.SemaphoreType.DMA((total,)),
            pltpu.SemaphoreType.DMA((total,)),
            pltpu.SemaphoreType.DMA(()),
        ],
        compiler_params=pltpu.CompilerParams(collective_id=collective_id, has_side_effects=True),
    )(x)


def body(
    pre_latent,
    pre_qlat,
    pre_qrope,
    pre_resid,
    block_order,
    dec_new,
    dec_qlat,
    dec_qrope,
    dec_resid,
    cache_len,
    page_table,
    cache_pool,
    w_uv,
    w_out,
    norm_gain,
    router,
    routes,
    w_gate,
    w_up,
    w_down,
):
    ctx_count = lax.axis_size("ctx")
    ctx_index = lax.axis_index("ctx")
    score_scale = (DN + DR) ** (-0.5)
    latent = pre_latent[0]
    shard_rows = latent.shape[0]
    local_rows = jnp.arange(shard_rows)
    own_pos = block_position(block_order, ctx_index * shard_rows + local_rows, shard_rows)
    cos_table, sin_table = rope_tables(own_pos, DR)
    key_rope = rotate(latent[:, DC:], cos_table, sin_table).astype(jnp.bfloat16)
    stored = jnp.concatenate([latent[:, :DC], key_rope], axis=-1)
    rotated = rotate(pre_qrope[0], cos_table[:, None, :], sin_table[:, None, :]).astype(
        jnp.bfloat16
    )
    queries = jnp.concatenate([pre_qlat[0], rotated], axis=-1)
    head_count = queries.shape[1]

    lengths = cache_len[:, 0]
    tables = page_table[:, 0, :]
    request_count = tables.shape[0]
    pages_dev = tables.shape[1]
    page_rows = cache_pool.shape[1]
    slot_count = cache_pool.shape[0]
    row_width = cache_pool.shape[2]
    cos_new, sin_new = rope_tables(lengths, DR)
    new_rope = rotate(dec_new[:, 0, DC:], cos_new, sin_new).astype(jnp.bfloat16)
    new_rows = jnp.concatenate([dec_new[:, 0, :DC], new_rope], axis=-1)
    page_index = lengths // page_rows
    owner_ctx = page_index // pages_dev
    page_hit = tables[:, :, None] == jnp.arange(slot_count)[None, None, :]
    wanted = jnp.arange(pages_dev)[None, :] == (page_index % pages_dev)[:, None]
    slot_of = jnp.sum(jnp.where(wanted, tables, 0), axis=1)
    target = jnp.where(
        owner_ctx == ctx_index, slot_of * page_rows + lengths % page_rows, slot_count * page_rows
    )
    row_hit = jnp.arange(slot_count * page_rows)[:, None] == target[None, :]
    written = jnp.dot(
        row_hit.astype(jnp.bfloat16), new_rows, preferred_element_type=jnp.float32
    ).astype(jnp.bfloat16)
    flat_pool = jnp.where(
        jnp.any(row_hit, axis=1)[:, None],
        written,
        cache_pool.reshape(slot_count * page_rows, row_width),
    )
    page_valid = jnp.any(page_hit, axis=1)
    page_logical = jnp.sum(page_hit.astype(jnp.int32) * jnp.arange(pages_dev)[None, :, None], axis=1)
    page_start = (ctx_index * pages_dev + page_logical) * page_rows
    key_pos = (page_start[:, :, None] + jnp.arange(page_rows)[None, None, :]).reshape(
        request_count, slot_count * page_rows
    )
    dec_visible = (
        jnp.repeat(page_valid, page_rows, axis=1) & (key_pos <= lengths[:, None])
    )[:, None, :]
    query_rot = rotate(dec_qrope[:, 0], cos_new[:, None, :], sin_new[:, None, :]).astype(
        jnp.bfloat16
    )
    dec_queries = jnp.concatenate([dec_qlat[:, 0], query_rot], axis=-1)
    dec_scores = (
        jnp.einsum("rhd,kd->rhk", dec_queries, flat_pool, preferred_element_type=jnp.float32)
        * score_scale
    )
    dec_masked = jnp.where(dec_visible, dec_scores, NEG_FILL)
    local_peak = jnp.max(dec_masked, axis=-1)
    dec_weights = jnp.where(dec_visible, jnp.exp(dec_masked - local_peak[..., None]), 0.0)
    local_total = jnp.sum(dec_weights, axis=-1)
    local_accum = jnp.einsum(
        "rhk,kc->rhc",
        dec_weights.astype(jnp.bfloat16),
        flat_pool[:, :DC],
        preferred_element_type=jnp.float32,
    )

    dec_block = jnp.concatenate(
        [
            local_accum.reshape(request_count * head_count, DC),
            local_peak.reshape(-1, 1),
            local_total.reshape(-1, 1),
            jnp.zeros((request_count * head_count, row_width - DC - 2), jnp.float32),
        ],
        axis=1,
    )
    packed = jnp.concatenate([stored.astype(jnp.float32), dec_block], axis=0)
    gathered = lax.all_gather(packed, "ctx")
    moving = gathered[:, :shard_rows].reshape(ctx_count * shard_rows, row_width).astype(jnp.bfloat16)
    dec_parts = gathered[:, shard_rows:].reshape(ctx_count, request_count, head_count, row_width)
    dec_share = request_count // ctx_count
    own_parts = lax.dynamic_slice_in_dim(dec_parts, ctx_index * dec_share, dec_share, 1)
    part_accum = own_parts[..., :DC]
    part_peak = own_parts[..., DC]
    part_total = own_parts[..., DC + 1]
    merged_peak = jnp.max(part_peak, axis=0)
    factor = jnp.exp(part_peak - merged_peak[None])
    merged_total = jnp.sum(part_total * factor, axis=0)
    merged_accum = jnp.sum(part_accum * factor[..., None], axis=0)
    own_mixed = (merged_accum / merged_total[..., None]).astype(jnp.bfloat16)

    key_pos_pre = block_position(block_order, jnp.arange(moving.shape[0]), shard_rows)
    scores = (
        jnp.einsum("qhd,kd->hqk", queries, moving, preferred_element_type=jnp.float32) * score_scale
    )
    visible = (key_pos_pre[None, :] <= own_pos[:, None])[None]
    masked = jnp.where(visible, scores, NEG_FILL)
    new_peak = jnp.max(masked, axis=-1)
    weights = jnp.where(visible, jnp.exp(masked - new_peak[..., None]), 0.0)
    totals = jnp.sum(weights, axis=-1)
    accumulated = jnp.einsum(
        "hqk,kc->qhc",
        weights.astype(jnp.bfloat16),
        moving[:, :DC],
        preferred_element_type=jnp.float32,
    )
    pre_mixed = (accumulated / jnp.transpose(totals)[:, :, None]).astype(jnp.bfloat16)

    own_resid = lax.dynamic_slice_in_dim(dec_resid[:, 0], ctx_index * dec_share, dec_share, 0)
    mixed_all = jnp.concatenate([pre_mixed, own_mixed], axis=0)
    resid_all = jnp.concatenate([pre_resid[0], own_resid], axis=0)
    values = jnp.einsum("nhc,hcv->nhv", mixed_all, w_uv, preferred_element_type=jnp.float32).astype(
        jnp.bfloat16
    )
    hidden_state = resid_all.astype(jnp.float32) + jnp.dot(
        values.reshape(values.shape[0], -1), w_out, preferred_element_type=jnp.float32
    )
    normed = (
        hidden_state
        * lax.rsqrt(jnp.mean(hidden_state * hidden_state, axis=-1, keepdims=True) + EPSILON)
        * norm_gain
    ).astype(jnp.bfloat16)
    logits = jnp.dot(normed.astype(jnp.float32), router, precision=lax.Precision.HIGHEST)
    probable = jax.nn.sigmoid(logits)
    row_count = normed.shape[0]
    width = normed.shape[1]
    top_count = routes.shape[1]
    expert_count = router.shape[1]
    devices = ctx_count * lax.axis_size("req")
    capacity = 2 * ((row_count * top_count + 2 * expert_count - 1) // (2 * expert_count))
    route_hit = routes[:, :, None] == jnp.arange(expert_count)[None, None, :]
    chosen = jnp.sum(jnp.where(route_hit, probable[:, None, :], 0.0), axis=-1)
    mixing = ROUTE_SCALE * chosen / jnp.sum(chosen, axis=1, keepdims=True)
    expert_hits = route_hit.astype(jnp.int32).sum(1)
    earlier = (jnp.arange(row_count)[None, :] < jnp.arange(row_count)[:, None]).astype(jnp.bfloat16)
    before = jnp.dot(
        earlier, expert_hits.astype(jnp.bfloat16), preferred_element_type=jnp.float32
    ).astype(jnp.int32)
    slot_index = jnp.sum(jnp.where(route_hit, before[:, None, :], 0), axis=-1)
    target_slot = routes * capacity + slot_index
    slot_hit = target_slot[:, :, None] == jnp.arange(expert_count * capacity)[None, None, :]
    dispatch = jnp.any(slot_hit, axis=1).astype(jnp.bfloat16)
    outgoing = lax.dot_general(
        dispatch, normed, (((0,), (0,)), ((), ())), preferred_element_type=jnp.float32
    ).astype(jnp.bfloat16).reshape(expert_count, capacity, width)
    doubled = jnp.broadcast_to(outgoing[:, None], (expert_count, 2, capacity, width)).reshape(
        devices, capacity, width
    )
    partial_out = expert_half(
        lax.all_to_all(doubled, ("ctx", "req"), split_axis=0, concat_axis=0, tiled=True),
        w_gate[0],
        w_up[0],
        w_down[0],
    )
    returned = lax.all_to_all(
        partial_out, ("ctx", "req"), split_axis=0, concat_axis=0, tiled=True
    ).reshape(expert_count, 2, capacity, width)
    results = (returned[:, 0].astype(jnp.float32) + returned[:, 1].astype(jnp.float32)).astype(
        jnp.bfloat16
    ).reshape(expert_count * capacity, width)
    combine = jnp.sum(jnp.where(slot_hit, mixing[:, :, None], 0.0), axis=1)
    moe = jnp.dot(combine, results.astype(jnp.float32), precision=lax.Precision.HIGHEST)
    final = (hidden_state + moe).astype(jnp.bfloat16)
    pre_out = final[:shard_rows][None]
    dec_out = final[shard_rows:][:, None]
    cache_out = flat_pool.reshape(cache_pool.shape)
    return (pre_out, dec_out, cache_out)


def solution(mesh):
    in_specs = (
        P("req", "ctx", None),
        P("req", "ctx", None, None),
        P("req", "ctx", None, None),
        P("req", "ctx", None),
        P(),
        P(None, "req", None),
        P(None, "req", None, None),
        P(None, "req", None, None),
        P(None, "req", None),
        P(None, "req"),
        P(None, "req", "ctx"),
        P(("ctx", "req"), None, None),
        P(),
        P(),
        P(),
        P(),
        P(("ctx", "req"), None),
        P(("ctx", "req"), None, None),
        P(("ctx", "req"), None, None),
        P(("ctx", "req"), None, None),
    )
    out_specs = (P("req", "ctx", None), P("ctx", "req", None), P(("ctx", "req"), None, None))
    return jax.shard_map(body, mesh=mesh, in_specs=in_specs, out_specs=out_specs, check_vma=False)
```

```python
import functools

import jax
import jax.numpy as jnp
from jax import lax
from jax.experimental import pallas as pl
from jax.experimental.pallas import tpu as pltpu
from jax.sharding import PartitionSpec as P

MESH = pl.DeviceIdType.MESH

DC = 512
DR = 64
DN = 128


THETA = 50000.0
ROUTE_SCALE = 2.446
EPSILON = 1e-06
NEG_FILL = -1e30


def joined(part, axis, combine):
    gathered = jax.tree.map(lambda a: lax.all_gather(a, axis), part)

    def take(source):
        return jax.tree.map(lambda a: lax.dynamic_index_in_dim(a, source, 0, False), gathered)

    return lax.fori_loop(
        1, lax.axis_size(axis), lambda source, state: combine(state, take(source)), take(0)
    )


def rope_tables(positions, rope_width):
    halfway = rope_width // 2
    inverse = THETA ** (-(jnp.arange(halfway).astype(jnp.float32) * 2.0) / rope_width)
    angles = positions.astype(jnp.float32)[..., None] * inverse
    return (jnp.cos(angles), jnp.sin(angles))


def rotate(values, cos_table, sin_table):
    halfway = values.shape[-1] // 2
    leading = values[..., :halfway].astype(jnp.float32)
    trailing = values[..., halfway:].astype(jnp.float32)
    return jnp.concatenate(
        [leading * cos_table - trailing * sin_table, trailing * cos_table + leading * sin_table],
        axis=-1,
    )


def block_position(block_order, global_rows, shard_rows):
    half_rows = shard_rows // 2
    block = global_rows // half_rows
    hit = block[:, None] == jnp.arange(block_order.shape[0])[None, :]
    logical = jnp.sum(jnp.where(hit, block_order[None, :], 0), axis=1)
    return logical * half_rows + global_rows % half_rows


def expert_half(inputs, gate_part, up_part, down_part):
    flat_rows = inputs.reshape(-1, inputs.shape[-1])
    gate_out = jnp.dot(flat_rows, gate_part, preferred_element_type=jnp.float32)
    upward = jnp.dot(flat_rows, up_part, preferred_element_type=jnp.float32)
    hidden = (jax.nn.silu(gate_out) * upward).astype(jnp.bfloat16)
    partial_out = jnp.dot(hidden, down_part, preferred_element_type=jnp.float32).astype(
        jnp.bfloat16
    )
    return partial_out.reshape(inputs.shape)


def merge_softmax(earlier, later):
    left_peak, left_total, left_accum = earlier
    right_peak, right_total, right_accum = later
    new_peak = jnp.maximum(left_peak, right_peak)
    left_factor = jnp.exp(left_peak - new_peak)
    right_factor = jnp.exp(right_peak - new_peak)
    merged_total = left_total * left_factor + right_total * right_factor
    merged_accum = left_accum * left_factor[..., None] + right_accum * right_factor[..., None]
    return (new_peak, merged_total, merged_accum)


def exchange_kernel(n_req, total, x_ref, out_ref, send_sem, recv_sem, local_sem):
    me = lax.axis_index("ctx") * n_req + lax.axis_index("req")

    def device(d):
        return (d // n_req, d % n_req)

    def outgoing(d):
        return pltpu.make_async_remote_copy(
            src_ref=x_ref.at[d],
            dst_ref=out_ref.at[me],
            send_sem=send_sem.at[d],
            recv_sem=recv_sem.at[me],
            device_id=device(d),
            device_id_type=MESH,
        )

    def incoming(s):
        return pltpu.make_async_remote_copy(
            src_ref=x_ref.at[me],
            dst_ref=out_ref.at[s],
            send_sem=send_sem.at[s],
            recv_sem=recv_sem.at[s],
            device_id=device(s),
            device_id_type=MESH,
        )

    barrier = pltpu.get_barrier_semaphore()

    def greet(k, carry):
        d = lax.rem(me + k, total)
        pl.semaphore_signal(barrier, inc=1, device_id=device(d), device_id_type=MESH)
        return carry

    lax.fori_loop(1, total, greet, 0)
    pl.semaphore_wait(barrier, total - 1)
    local = pltpu.make_async_copy(x_ref.at[me], out_ref.at[me], local_sem)
    local.start()

    def send(k, carry):
        outgoing(lax.rem(me + k, total)).start()
        return carry

    lax.fori_loop(1, total, send, 0)

    def finish(k, carry):
        outgoing(lax.rem(me + k, total)).wait_send()
        incoming(lax.rem(me + total - k, total)).wait_recv()
        return carry

    lax.fori_loop(1, total, finish, 0)
    local.wait()


def exchange(x, n_req, total, collective_id):
    return pl.pallas_call(
        functools.partial(exchange_kernel, n_req, total),
        out_shape=jax.ShapeDtypeStruct(x.shape, x.dtype),
        in_specs=[pl.BlockSpec(memory_space=pl.ANY)],
        out_specs=pl.BlockSpec(memory_space=pl.ANY),
        scratch_shapes=[
            pltpu.SemaphoreType.DMA((total,)),
            pltpu.SemaphoreType.DMA((total,)),
            pltpu.SemaphoreType.DMA(()),
        ],
        compiler_params=pltpu.CompilerParams(collective_id=collective_id, has_side_effects=True),
    )(x)


def body(
    pre_latent,
    pre_qlat,
    pre_qrope,
    pre_resid,
    block_order,
    dec_new,
    dec_qlat,
    dec_qrope,
    dec_resid,
    cache_len,
    page_table,
    cache_pool,
    w_uv,
    w_out,
    norm_gain,
    router,
    routes,
    w_gate,
    w_up,
    w_down,
):
    ctx_count = lax.axis_size("ctx")
    ctx_index = lax.axis_index("ctx")
    score_scale = (DN + DR) ** (-0.5)
    latent = pre_latent[0]
    shard_rows = latent.shape[0]
    local_rows = jnp.arange(shard_rows)
    own_pos = block_position(block_order, ctx_index * shard_rows + local_rows, shard_rows)
    cos_table, sin_table = rope_tables(own_pos, DR)
    key_rope = rotate(latent[:, DC:], cos_table, sin_table).astype(jnp.bfloat16)
    stored = jnp.concatenate([latent[:, :DC], key_rope], axis=-1)
    rotated = rotate(pre_qrope[0], cos_table[:, None, :], sin_table[:, None, :]).astype(
        jnp.bfloat16
    )
    queries = jnp.concatenate([pre_qlat[0], rotated], axis=-1)
    head_count = queries.shape[1]

    lengths = cache_len[:, 0]
    tables = page_table[:, 0, :]
    request_count = tables.shape[0]
    pages_dev = tables.shape[1]
    page_rows = cache_pool.shape[1]
    slot_count = cache_pool.shape[0]
    row_width = cache_pool.shape[2]
    cos_new, sin_new = rope_tables(lengths, DR)
    new_rope = rotate(dec_new[:, 0, DC:], cos_new, sin_new).astype(jnp.bfloat16)
    new_rows = jnp.concatenate([dec_new[:, 0, :DC], new_rope], axis=-1)
    page_index = lengths // page_rows
    owner_ctx = page_index // pages_dev
    page_hit = tables[:, :, None] == jnp.arange(slot_count)[None, None, :]
    wanted = jnp.arange(pages_dev)[None, :] == (page_index % pages_dev)[:, None]
    slot_of = jnp.sum(jnp.where(wanted, tables, 0), axis=1)
    target = jnp.where(
        owner_ctx == ctx_index, slot_of * page_rows + lengths % page_rows, slot_count * page_rows
    )
    row_hit = jnp.arange(slot_count * page_rows)[:, None] == target[None, :]
    written = jnp.dot(
        row_hit.astype(jnp.bfloat16), new_rows, preferred_element_type=jnp.float32
    ).astype(jnp.bfloat16)
    flat_pool = jnp.where(
        jnp.any(row_hit, axis=1)[:, None],
        written,
        cache_pool.reshape(slot_count * page_rows, row_width),
    )
    page_valid = jnp.any(page_hit, axis=1)
    page_logical = jnp.sum(page_hit.astype(jnp.int32) * jnp.arange(pages_dev)[None, :, None], axis=1)
    page_start = (ctx_index * pages_dev + page_logical) * page_rows
    key_pos = (page_start[:, :, None] + jnp.arange(page_rows)[None, None, :]).reshape(
        request_count, slot_count * page_rows
    )
    dec_visible = (
        jnp.repeat(page_valid, page_rows, axis=1) & (key_pos <= lengths[:, None])
    )[:, None, :]
    query_rot = rotate(dec_qrope[:, 0], cos_new[:, None, :], sin_new[:, None, :]).astype(
        jnp.bfloat16
    )
    dec_queries = jnp.concatenate([dec_qlat[:, 0], query_rot], axis=-1)
    dec_scores = (
        jnp.einsum("rhd,kd->rhk", dec_queries, flat_pool, preferred_element_type=jnp.float32)
        * score_scale
    )
    dec_masked = jnp.where(dec_visible, dec_scores, NEG_FILL)
    local_peak = jnp.max(dec_masked, axis=-1)
    dec_weights = jnp.where(dec_visible, jnp.exp(dec_masked - local_peak[..., None]), 0.0)
    local_total = jnp.sum(dec_weights, axis=-1)
    local_accum = jnp.einsum(
        "rhk,kc->rhc",
        dec_weights.astype(jnp.bfloat16),
        flat_pool[:, :DC],
        preferred_element_type=jnp.float32,
    )

    dec_block = jnp.concatenate(
        [
            local_accum.reshape(request_count * head_count, DC),
            local_peak.reshape(-1, 1),
            local_total.reshape(-1, 1),
            jnp.zeros((request_count * head_count, row_width - DC - 2), jnp.float32),
        ],
        axis=1,
    )
    packed = jnp.concatenate([stored.astype(jnp.float32), dec_block], axis=0)
    gathered = lax.all_gather(packed, "ctx")
    moving = gathered[:, :shard_rows].reshape(ctx_count * shard_rows, row_width).astype(jnp.bfloat16)
    dec_parts = gathered[:, shard_rows:].reshape(ctx_count, request_count, head_count, row_width)
    dec_share = request_count // ctx_count
    own_parts = lax.dynamic_slice_in_dim(dec_parts, ctx_index * dec_share, dec_share, 1)
    part_accum = own_parts[..., :DC]
    part_peak = own_parts[..., DC]
    part_total = own_parts[..., DC + 1]
    merged_peak = jnp.max(part_peak, axis=0)
    factor = jnp.exp(part_peak - merged_peak[None])
    merged_total = jnp.sum(part_total * factor, axis=0)
    merged_accum = jnp.sum(part_accum * factor[..., None], axis=0)
    own_mixed = (merged_accum / merged_total[..., None]).astype(jnp.bfloat16)

    key_pos_pre = block_position(block_order, jnp.arange(moving.shape[0]), shard_rows)
    scores = (
        jnp.einsum("qhd,kd->hqk", queries, moving, preferred_element_type=jnp.float32) * score_scale
    )
    visible = (key_pos_pre[None, :] <= own_pos[:, None])[None]
    masked = jnp.where(visible, scores, NEG_FILL)
    new_peak = jnp.max(masked, axis=-1)
    weights = jnp.where(visible, jnp.exp(masked - new_peak[..., None]), 0.0)
    totals = jnp.sum(weights, axis=-1)
    accumulated = jnp.einsum(
        "hqk,kc->qhc",
        weights.astype(jnp.bfloat16),
        moving[:, :DC],
        preferred_element_type=jnp.float32,
    )
    pre_mixed = (accumulated / jnp.transpose(totals)[:, :, None]).astype(jnp.bfloat16)

    own_resid = lax.dynamic_slice_in_dim(dec_resid[:, 0], ctx_index * dec_share, dec_share, 0)
    mixed_all = jnp.concatenate([pre_mixed, own_mixed], axis=0)
    resid_all = jnp.concatenate([pre_resid[0], own_resid], axis=0)
    values = jnp.einsum("nhc,hcv->nhv", mixed_all, w_uv, preferred_element_type=jnp.float32).astype(
        jnp.bfloat16
    )
    hidden_state = resid_all.astype(jnp.float32) + jnp.dot(
        values.reshape(values.shape[0], -1), w_out, preferred_element_type=jnp.float32
    )
    normed = (
        hidden_state
        * lax.rsqrt(jnp.mean(hidden_state * hidden_state, axis=-1, keepdims=True) + EPSILON)
        * norm_gain
    ).astype(jnp.bfloat16)
    logits = jnp.dot(normed.astype(jnp.float32), router, precision=lax.Precision.HIGHEST)
    probable = jax.nn.sigmoid(logits)
    row_count = normed.shape[0]
    width = normed.shape[1]
    top_count = routes.shape[1]
    expert_count = router.shape[1]
    devices = ctx_count * lax.axis_size("req")
    capacity = 2 * ((row_count * top_count + 2 * expert_count - 1) // (2 * expert_count))
    route_hit = routes[:, :, None] == jnp.arange(expert_count)[None, None, :]
    chosen = jnp.sum(jnp.where(route_hit, probable[:, None, :], 0.0), axis=-1)
    mixing = ROUTE_SCALE * chosen / jnp.sum(chosen, axis=1, keepdims=True)
    expert_hits = route_hit.astype(jnp.int32).sum(1)
    earlier = (jnp.arange(row_count)[None, :] < jnp.arange(row_count)[:, None]).astype(jnp.bfloat16)
    before = jnp.dot(
        earlier, expert_hits.astype(jnp.bfloat16), preferred_element_type=jnp.float32
    ).astype(jnp.int32)
    slot_index = jnp.sum(jnp.where(route_hit, before[:, None, :], 0), axis=-1)
    target_slot = routes * capacity + slot_index
    slot_hit = target_slot[:, :, None] == jnp.arange(expert_count * capacity)[None, None, :]
    dispatch = jnp.any(slot_hit, axis=1).astype(jnp.bfloat16)
    outgoing = lax.dot_general(
        dispatch, normed, (((0,), (0,)), ((), ())), preferred_element_type=jnp.float32
    ).astype(jnp.bfloat16).reshape(expert_count, capacity, width)
    chunks = 2
    piece = capacity // chunks
    pieces = []
    for chunk in range(chunks):
        part = outgoing[:, chunk * piece:(chunk + 1) * piece]
        doubled = jnp.broadcast_to(part[:, None], (expert_count, 2, piece, width)).reshape(
            devices, piece, width
        )
        partial_out = expert_half(
            lax.all_to_all(doubled, ("ctx", "req"), split_axis=0, concat_axis=0, tiled=True),
            w_gate[0],
            w_up[0],
            w_down[0],
        )
        returned = lax.all_to_all(
            partial_out, ("ctx", "req"), split_axis=0, concat_axis=0, tiled=True
        ).reshape(expert_count, 2, piece, width)
        pieces.append(
            (returned[:, 0].astype(jnp.float32) + returned[:, 1].astype(jnp.float32)).astype(
                jnp.bfloat16
            )
        )
    results = jnp.concatenate(pieces, axis=1).reshape(expert_count * capacity, width)
    combine = jnp.sum(jnp.where(slot_hit, mixing[:, :, None], 0.0), axis=1)
    moe = jnp.dot(combine, results.astype(jnp.float32), precision=lax.Precision.HIGHEST)
    final = (hidden_state + moe).astype(jnp.bfloat16)
    pre_out = final[:shard_rows][None]
    dec_out = final[shard_rows:][:, None]
    cache_out = flat_pool.reshape(cache_pool.shape)
    return (pre_out, dec_out, cache_out)


def solution(mesh):
    in_specs = (
        P("req", "ctx", None),
        P("req", "ctx", None, None),
        P("req", "ctx", None, None),
        P("req", "ctx", None),
        P(),
        P(None, "req", None),
        P(None, "req", None, None),
        P(None, "req", None, None),
        P(None, "req", None),
        P(None, "req"),
        P(None, "req", "ctx"),
        P(("ctx", "req"), None, None),
        P(),
        P(),
        P(),
        P(),
        P(("ctx", "req"), None),
        P(("ctx", "req"), None, None),
        P(("ctx", "req"), None, None),
        P(("ctx", "req"), None, None),
    )
    out_specs = (P("req", "ctx", None), P("ctx", "req", None), P(("ctx", "req"), None, None))
    return jax.shard_map(body, mesh=mesh, in_specs=in_specs, out_specs=out_specs, check_vma=False)
```

```python
import functools

import jax
import jax.numpy as jnp
from jax import lax
from jax.experimental import pallas as pl
from jax.experimental.pallas import tpu as pltpu
from jax.sharding import PartitionSpec as P

MESH = pl.DeviceIdType.MESH

DC = 512
DR = 64
DN = 128


THETA = 50000.0
ROUTE_SCALE = 2.446
EPSILON = 1e-06
NEG_FILL = -1e30


def joined(part, axis, combine):
    gathered = jax.tree.map(lambda a: lax.all_gather(a, axis), part)

    def take(source):
        return jax.tree.map(lambda a: lax.dynamic_index_in_dim(a, source, 0, False), gathered)

    return lax.fori_loop(
        1, lax.axis_size(axis), lambda source, state: combine(state, take(source)), take(0)
    )


def rope_tables(positions, rope_width):
    halfway = rope_width // 2
    inverse = THETA ** (-(jnp.arange(halfway).astype(jnp.float32) * 2.0) / rope_width)
    angles = positions.astype(jnp.float32)[..., None] * inverse
    return (jnp.cos(angles), jnp.sin(angles))


def rotate(values, cos_table, sin_table):
    halfway = values.shape[-1] // 2
    leading = values[..., :halfway].astype(jnp.float32)
    trailing = values[..., halfway:].astype(jnp.float32)
    return jnp.concatenate(
        [leading * cos_table - trailing * sin_table, trailing * cos_table + leading * sin_table],
        axis=-1,
    )


def block_position(block_order, global_rows, shard_rows):
    half_rows = shard_rows // 2
    block = global_rows // half_rows
    hit = block[:, None] == jnp.arange(block_order.shape[0])[None, :]
    logical = jnp.sum(jnp.where(hit, block_order[None, :], 0), axis=1)
    return logical * half_rows + global_rows % half_rows


def expert_half(inputs, gate_part, up_part, down_part):
    flat_rows = inputs.reshape(-1, inputs.shape[-1])
    gate_out = jnp.dot(flat_rows, gate_part, preferred_element_type=jnp.float32)
    upward = jnp.dot(flat_rows, up_part, preferred_element_type=jnp.float32)
    hidden = (jax.nn.silu(gate_out) * upward).astype(jnp.bfloat16)
    partial_out = jnp.dot(hidden, down_part, preferred_element_type=jnp.float32).astype(
        jnp.bfloat16
    )
    return partial_out.reshape(inputs.shape)


def merge_softmax(earlier, later):
    left_peak, left_total, left_accum = earlier
    right_peak, right_total, right_accum = later
    new_peak = jnp.maximum(left_peak, right_peak)
    left_factor = jnp.exp(left_peak - new_peak)
    right_factor = jnp.exp(right_peak - new_peak)
    merged_total = left_total * left_factor + right_total * right_factor
    merged_accum = left_accum * left_factor[..., None] + right_accum * right_factor[..., None]
    return (new_peak, merged_total, merged_accum)


def exchange_kernel(n_req, total, x_ref, out_ref, send_sem, recv_sem, local_sem):
    me = lax.axis_index("ctx") * n_req + lax.axis_index("req")

    def device(d):
        return (d // n_req, d % n_req)

    def outgoing(d):
        return pltpu.make_async_remote_copy(
            src_ref=x_ref.at[d],
            dst_ref=out_ref.at[me],
            send_sem=send_sem.at[d],
            recv_sem=recv_sem.at[me],
            device_id=device(d),
            device_id_type=MESH,
        )

    def incoming(s):
        return pltpu.make_async_remote_copy(
            src_ref=x_ref.at[me],
            dst_ref=out_ref.at[s],
            send_sem=send_sem.at[s],
            recv_sem=recv_sem.at[s],
            device_id=device(s),
            device_id_type=MESH,
        )

    barrier = pltpu.get_barrier_semaphore()

    def greet(k, carry):
        d = lax.rem(me + k, total)
        pl.semaphore_signal(barrier, inc=1, device_id=device(d), device_id_type=MESH)
        return carry

    lax.fori_loop(1, total, greet, 0)
    pl.semaphore_wait(barrier, total - 1)
    local = pltpu.make_async_copy(x_ref.at[me], out_ref.at[me], local_sem)
    local.start()

    def send(k, carry):
        outgoing(lax.rem(me + k, total)).start()
        return carry

    lax.fori_loop(1, total, send, 0)

    def finish(k, carry):
        outgoing(lax.rem(me + k, total)).wait_send()
        incoming(lax.rem(me + total - k, total)).wait_recv()
        return carry

    lax.fori_loop(1, total, finish, 0)
    local.wait()


def exchange(x, n_req, total, collective_id):
    return pl.pallas_call(
        functools.partial(exchange_kernel, n_req, total),
        out_shape=jax.ShapeDtypeStruct(x.shape, x.dtype),
        in_specs=[pl.BlockSpec(memory_space=pl.ANY)],
        out_specs=pl.BlockSpec(memory_space=pl.ANY),
        scratch_shapes=[
            pltpu.SemaphoreType.DMA((total,)),
            pltpu.SemaphoreType.DMA((total,)),
            pltpu.SemaphoreType.DMA(()),
        ],
        compiler_params=pltpu.CompilerParams(collective_id=collective_id, has_side_effects=True),
    )(x)


def context_kernel(n_ctx, keys_ref, parts_ref, keys_out, parts_out, sems):
    me = lax.axis_index("ctx")
    row = lax.axis_index("req")
    barrier = pltpu.get_barrier_semaphore()
    for step in range(1, n_ctx):
        other = lax.rem(me + step, n_ctx)
        pl.semaphore_signal(barrier, inc=1, device_id=(other, row), device_id_type=MESH)
    pl.semaphore_wait(barrier, n_ctx - 1)

    def key_copy(source, target):
        return pltpu.make_async_remote_copy(
            src_ref=keys_ref,
            dst_ref=keys_out.at[source],
            send_sem=sems.at[0, target],
            recv_sem=sems.at[1, source],
            device_id=(target, row),
            device_id_type=MESH,
        )

    def part_copy(source, target):
        return pltpu.make_async_remote_copy(
            src_ref=parts_ref.at[target],
            dst_ref=parts_out.at[source],
            send_sem=sems.at[2, target],
            recv_sem=sems.at[3, source],
            device_id=(target, row),
            device_id_type=MESH,
        )

    own_keys = pltpu.make_async_copy(keys_ref, keys_out.at[me], sems.at[4, 0])
    own_parts = pltpu.make_async_copy(parts_ref.at[me], parts_out.at[me], sems.at[4, 1])
    own_keys.start()
    own_parts.start()
    for step in range(1, n_ctx):
        other = lax.rem(me + step, n_ctx)
        key_copy(me, other).start()
        part_copy(me, other).start()
    for step in range(1, n_ctx):
        other = lax.rem(me + step, n_ctx)
        source = lax.rem(me + n_ctx - step, n_ctx)
        key_copy(me, other).wait_send()
        part_copy(me, other).wait_send()
        key_copy(source, me).wait_recv()
        part_copy(source, me).wait_recv()
    own_keys.wait()
    own_parts.wait()


def context_exchange(keys, parts, n_ctx):
    return pl.pallas_call(
        functools.partial(context_kernel, n_ctx),
        out_shape=(
            jax.ShapeDtypeStruct((n_ctx,) + keys.shape, keys.dtype),
            jax.ShapeDtypeStruct(parts.shape, parts.dtype),
        ),
        in_specs=[pl.BlockSpec(memory_space=pl.ANY)] * 2,
        out_specs=(pl.BlockSpec(memory_space=pl.ANY), pl.BlockSpec(memory_space=pl.ANY)),
        scratch_shapes=[pltpu.SemaphoreType.DMA((5, n_ctx))],
        compiler_params=pltpu.CompilerParams(collective_id=2, has_side_effects=True),
    )(keys, parts)


def body(
    pre_latent,
    pre_qlat,
    pre_qrope,
    pre_resid,
    block_order,
    dec_new,
    dec_qlat,
    dec_qrope,
    dec_resid,
    cache_len,
    page_table,
    cache_pool,
    w_uv,
    w_out,
    norm_gain,
    router,
    routes,
    w_gate,
    w_up,
    w_down,
):
    ctx_count = lax.axis_size("ctx")
    ctx_index = lax.axis_index("ctx")
    score_scale = (DN + DR) ** (-0.5)
    latent = pre_latent[0]
    shard_rows = latent.shape[0]
    local_rows = jnp.arange(shard_rows)
    own_pos = block_position(block_order, ctx_index * shard_rows + local_rows, shard_rows)
    cos_table, sin_table = rope_tables(own_pos, DR)
    key_rope = rotate(latent[:, DC:], cos_table, sin_table).astype(jnp.bfloat16)
    stored = jnp.concatenate([latent[:, :DC], key_rope], axis=-1)
    rotated = rotate(pre_qrope[0], cos_table[:, None, :], sin_table[:, None, :]).astype(
        jnp.bfloat16
    )
    queries = jnp.concatenate([pre_qlat[0], rotated], axis=-1)
    head_count = queries.shape[1]

    lengths = cache_len[:, 0]
    tables = page_table[:, 0, :]
    request_count = tables.shape[0]
    pages_dev = tables.shape[1]
    page_rows = cache_pool.shape[1]
    slot_count = cache_pool.shape[0]
    row_width = cache_pool.shape[2]
    cos_new, sin_new = rope_tables(lengths, DR)
    new_rope = rotate(dec_new[:, 0, DC:], cos_new, sin_new).astype(jnp.bfloat16)
    new_rows = jnp.concatenate([dec_new[:, 0, :DC], new_rope], axis=-1)
    page_index = lengths // page_rows
    owner_ctx = page_index // pages_dev
    page_hit = tables[:, :, None] == jnp.arange(slot_count)[None, None, :]
    wanted = jnp.arange(pages_dev)[None, :] == (page_index % pages_dev)[:, None]
    slot_of = jnp.sum(jnp.where(wanted, tables, 0), axis=1)
    target = jnp.where(
        owner_ctx == ctx_index, slot_of * page_rows + lengths % page_rows, slot_count * page_rows
    )
    row_hit = jnp.arange(slot_count * page_rows)[:, None] == target[None, :]
    written = jnp.dot(
        row_hit.astype(jnp.bfloat16), new_rows, preferred_element_type=jnp.float32
    ).astype(jnp.bfloat16)
    flat_pool = jnp.where(
        jnp.any(row_hit, axis=1)[:, None],
        written,
        cache_pool.reshape(slot_count * page_rows, row_width),
    )
    page_valid = jnp.any(page_hit, axis=1)
    page_logical = jnp.sum(page_hit.astype(jnp.int32) * jnp.arange(pages_dev)[None, :, None], axis=1)
    page_start = (ctx_index * pages_dev + page_logical) * page_rows
    key_pos = (page_start[:, :, None] + jnp.arange(page_rows)[None, None, :]).reshape(
        request_count, slot_count * page_rows
    )
    dec_visible = (
        jnp.repeat(page_valid, page_rows, axis=1) & (key_pos <= lengths[:, None])
    )[:, None, :]
    query_rot = rotate(dec_qrope[:, 0], cos_new[:, None, :], sin_new[:, None, :]).astype(
        jnp.bfloat16
    )
    dec_queries = jnp.concatenate([dec_qlat[:, 0], query_rot], axis=-1)
    dec_scores = (
        jnp.einsum("rhd,kd->rhk", dec_queries, flat_pool, preferred_element_type=jnp.float32)
        * score_scale
    )
    dec_masked = jnp.where(dec_visible, dec_scores, NEG_FILL)
    local_peak = jnp.max(dec_masked, axis=-1)
    dec_weights = jnp.where(dec_visible, jnp.exp(dec_masked - local_peak[..., None]), 0.0)
    local_total = jnp.sum(dec_weights, axis=-1)
    local_accum = jnp.einsum(
        "rhk,kc->rhc",
        dec_weights.astype(jnp.bfloat16),
        flat_pool[:, :DC],
        preferred_element_type=jnp.float32,
    )

    dec_share = request_count // ctx_count
    part_width = 128 * ((DC + 2 + 127) // 128)
    dec_block = jnp.concatenate(
        [
            local_accum,
            local_peak[..., None],
            local_total[..., None],
            jnp.zeros((request_count, head_count, part_width - DC - 2), jnp.float32),
        ],
        axis=2,
    ).reshape(ctx_count, dec_share * head_count, part_width)
    keys_all, own_parts = context_exchange(stored, dec_block, ctx_count)
    moving = keys_all.reshape(ctx_count * shard_rows, row_width)
    own_parts = own_parts.reshape(ctx_count, dec_share, head_count, part_width)
    part_accum = own_parts[..., :DC]
    part_peak = own_parts[..., DC]
    part_total = own_parts[..., DC + 1]
    merged_peak = jnp.max(part_peak, axis=0)
    factor = jnp.exp(part_peak - merged_peak[None])
    merged_total = jnp.sum(part_total * factor, axis=0)
    merged_accum = jnp.sum(part_accum * factor[..., None], axis=0)
    own_mixed = (merged_accum / merged_total[..., None]).astype(jnp.bfloat16)

    key_pos_pre = block_position(block_order, jnp.arange(moving.shape[0]), shard_rows)
    scores = (
        jnp.einsum("qhd,kd->hqk", queries, moving, preferred_element_type=jnp.float32) * score_scale
    )
    visible = (key_pos_pre[None, :] <= own_pos[:, None])[None]
    masked = jnp.where(visible, scores, NEG_FILL)
    new_peak = jnp.max(masked, axis=-1)
    weights = jnp.where(visible, jnp.exp(masked - new_peak[..., None]), 0.0)
    totals = jnp.sum(weights, axis=-1)
    accumulated = jnp.einsum(
        "hqk,kc->qhc",
        weights.astype(jnp.bfloat16),
        moving[:, :DC],
        preferred_element_type=jnp.float32,
    )
    pre_mixed = (accumulated / jnp.transpose(totals)[:, :, None]).astype(jnp.bfloat16)

    own_resid = lax.dynamic_slice_in_dim(dec_resid[:, 0], ctx_index * dec_share, dec_share, 0)
    mixed_all = jnp.concatenate([pre_mixed, own_mixed], axis=0)
    resid_all = jnp.concatenate([pre_resid[0], own_resid], axis=0)
    values = jnp.einsum("nhc,hcv->nhv", mixed_all, w_uv, preferred_element_type=jnp.float32).astype(
        jnp.bfloat16
    )
    hidden_state = resid_all.astype(jnp.float32) + jnp.dot(
        values.reshape(values.shape[0], -1), w_out, preferred_element_type=jnp.float32
    )
    normed = (
        hidden_state
        * lax.rsqrt(jnp.mean(hidden_state * hidden_state, axis=-1, keepdims=True) + EPSILON)
        * norm_gain
    ).astype(jnp.bfloat16)
    logits = jnp.dot(normed.astype(jnp.float32), router, precision=lax.Precision.HIGHEST)
    probable = jax.nn.sigmoid(logits)
    row_count = normed.shape[0]
    width = normed.shape[1]
    top_count = routes.shape[1]
    expert_count = router.shape[1]
    devices = ctx_count * lax.axis_size("req")
    capacity = 2 * ((row_count * top_count + 2 * expert_count - 1) // (2 * expert_count))
    route_hit = routes[:, :, None] == jnp.arange(expert_count)[None, None, :]
    chosen = jnp.sum(jnp.where(route_hit, probable[:, None, :], 0.0), axis=-1)
    mixing = ROUTE_SCALE * chosen / jnp.sum(chosen, axis=1, keepdims=True)
    expert_hits = route_hit.astype(jnp.int32).sum(1)
    earlier = (jnp.arange(row_count)[None, :] < jnp.arange(row_count)[:, None]).astype(jnp.bfloat16)
    before = jnp.dot(
        earlier, expert_hits.astype(jnp.bfloat16), preferred_element_type=jnp.float32
    ).astype(jnp.int32)
    slot_index = jnp.sum(jnp.where(route_hit, before[:, None, :], 0), axis=-1)
    target_slot = routes * capacity + slot_index
    slot_hit = target_slot[:, :, None] == jnp.arange(expert_count * capacity)[None, None, :]
    dispatch = jnp.any(slot_hit, axis=1).astype(jnp.bfloat16)
    outgoing = lax.dot_general(
        dispatch, normed, (((0,), (0,)), ((), ())), preferred_element_type=jnp.float32
    ).astype(jnp.bfloat16).reshape(expert_count, capacity, width)
    doubled = jnp.broadcast_to(outgoing[:, None], (expert_count, 2, capacity, width)).reshape(
        devices, capacity, width
    )
    partial_out = expert_half(
        lax.all_to_all(doubled, ("ctx", "req"), split_axis=0, concat_axis=0, tiled=True),
        w_gate[0],
        w_up[0],
        w_down[0],
    )
    returned = lax.all_to_all(
        partial_out, ("ctx", "req"), split_axis=0, concat_axis=0, tiled=True
    ).reshape(expert_count, 2, capacity, width)
    results = (returned[:, 0].astype(jnp.float32) + returned[:, 1].astype(jnp.float32)).astype(
        jnp.bfloat16
    ).reshape(expert_count * capacity, width)
    combine = jnp.sum(jnp.where(slot_hit, mixing[:, :, None], 0.0), axis=1)
    moe = jnp.dot(combine, results.astype(jnp.float32), precision=lax.Precision.HIGHEST)
    final = (hidden_state + moe).astype(jnp.bfloat16)
    pre_out = final[:shard_rows][None]
    dec_out = final[shard_rows:][:, None]
    cache_out = flat_pool.reshape(cache_pool.shape)
    return (pre_out, dec_out, cache_out)


def solution(mesh):
    in_specs = (
        P("req", "ctx", None),
        P("req", "ctx", None, None),
        P("req", "ctx", None, None),
        P("req", "ctx", None),
        P(),
        P(None, "req", None),
        P(None, "req", None, None),
        P(None, "req", None, None),
        P(None, "req", None),
        P(None, "req"),
        P(None, "req", "ctx"),
        P(("ctx", "req"), None, None),
        P(),
        P(),
        P(),
        P(),
        P(("ctx", "req"), None),
        P(("ctx", "req"), None, None),
        P(("ctx", "req"), None, None),
        P(("ctx", "req"), None, None),
    )
    out_specs = (P("req", "ctx", None), P("ctx", "req", None), P(("ctx", "req"), None, None))
    return jax.shard_map(body, mesh=mesh, in_specs=in_specs, out_specs=out_specs, check_vma=False)
```

```python
import functools

import jax
import jax.numpy as jnp
from jax import lax
from jax.experimental import pallas as pl
from jax.experimental.pallas import tpu as pltpu
from jax.sharding import PartitionSpec as P

MESH = pl.DeviceIdType.MESH

DC = 512
DR = 64
DN = 128


THETA = 50000.0
ROUTE_SCALE = 2.446
EPSILON = 1e-06
NEG_FILL = -1e30


def joined(part, axis, combine):
    gathered = jax.tree.map(lambda a: lax.all_gather(a, axis), part)

    def take(source):
        return jax.tree.map(lambda a: lax.dynamic_index_in_dim(a, source, 0, False), gathered)

    return lax.fori_loop(
        1, lax.axis_size(axis), lambda source, state: combine(state, take(source)), take(0)
    )


def rope_tables(positions, rope_width):
    halfway = rope_width // 2
    inverse = THETA ** (-(jnp.arange(halfway).astype(jnp.float32) * 2.0) / rope_width)
    angles = positions.astype(jnp.float32)[..., None] * inverse
    return (jnp.cos(angles), jnp.sin(angles))


def rotate(values, cos_table, sin_table):
    halfway = values.shape[-1] // 2
    leading = values[..., :halfway].astype(jnp.float32)
    trailing = values[..., halfway:].astype(jnp.float32)
    return jnp.concatenate(
        [leading * cos_table - trailing * sin_table, trailing * cos_table + leading * sin_table],
        axis=-1,
    )


def block_position(block_order, global_rows, shard_rows):
    half_rows = shard_rows // 2
    block = global_rows // half_rows
    hit = block[:, None] == jnp.arange(block_order.shape[0])[None, :]
    logical = jnp.sum(jnp.where(hit, block_order[None, :], 0), axis=1)
    return logical * half_rows + global_rows % half_rows


def expert_half(inputs, gate_part, up_part, down_part):
    flat_rows = inputs.reshape(-1, inputs.shape[-1])
    gate_out = jnp.dot(flat_rows, gate_part, preferred_element_type=jnp.float32)
    upward = jnp.dot(flat_rows, up_part, preferred_element_type=jnp.float32)
    hidden = (jax.nn.silu(gate_out) * upward).astype(jnp.bfloat16)
    partial_out = jnp.dot(hidden, down_part, preferred_element_type=jnp.float32).astype(
        jnp.bfloat16
    )
    return partial_out.reshape(inputs.shape)


def merge_softmax(earlier, later):
    left_peak, left_total, left_accum = earlier
    right_peak, right_total, right_accum = later
    new_peak = jnp.maximum(left_peak, right_peak)
    left_factor = jnp.exp(left_peak - new_peak)
    right_factor = jnp.exp(right_peak - new_peak)
    merged_total = left_total * left_factor + right_total * right_factor
    merged_accum = left_accum * left_factor[..., None] + right_accum * right_factor[..., None]
    return (new_peak, merged_total, merged_accum)


def exchange_kernel(n_req, total, x_ref, out_ref, send_sem, recv_sem, local_sem):
    me = lax.axis_index("ctx") * n_req + lax.axis_index("req")

    def device(d):
        return (d // n_req, d % n_req)

    def outgoing(d):
        return pltpu.make_async_remote_copy(
            src_ref=x_ref.at[d],
            dst_ref=out_ref.at[me],
            send_sem=send_sem.at[d],
            recv_sem=recv_sem.at[me],
            device_id=device(d),
            device_id_type=MESH,
        )

    def incoming(s):
        return pltpu.make_async_remote_copy(
            src_ref=x_ref.at[me],
            dst_ref=out_ref.at[s],
            send_sem=send_sem.at[s],
            recv_sem=recv_sem.at[s],
            device_id=device(s),
            device_id_type=MESH,
        )

    barrier = pltpu.get_barrier_semaphore()

    def greet(k, carry):
        d = lax.rem(me + k, total)
        pl.semaphore_signal(barrier, inc=1, device_id=device(d), device_id_type=MESH)
        return carry

    lax.fori_loop(1, total, greet, 0)
    pl.semaphore_wait(barrier, total - 1)
    local = pltpu.make_async_copy(x_ref.at[me], out_ref.at[me], local_sem)
    local.start()

    def send(k, carry):
        outgoing(lax.rem(me + k, total)).start()
        return carry

    lax.fori_loop(1, total, send, 0)

    def finish(k, carry):
        outgoing(lax.rem(me + k, total)).wait_send()
        incoming(lax.rem(me + total - k, total)).wait_recv()
        return carry

    lax.fori_loop(1, total, finish, 0)
    local.wait()


def exchange(x, n_req, total, collective_id):
    return pl.pallas_call(
        functools.partial(exchange_kernel, n_req, total),
        out_shape=jax.ShapeDtypeStruct(x.shape, x.dtype),
        in_specs=[pl.BlockSpec(memory_space=pl.ANY)],
        out_specs=pl.BlockSpec(memory_space=pl.ANY),
        scratch_shapes=[
            pltpu.SemaphoreType.DMA((total,)),
            pltpu.SemaphoreType.DMA((total,)),
            pltpu.SemaphoreType.DMA(()),
        ],
        compiler_params=pltpu.CompilerParams(collective_id=collective_id, has_side_effects=True),
    )(x)


def context_kernel(n_ctx, keys_ref, parts_ref, keys_out, parts_out, sems):
    me = lax.axis_index("ctx")
    row = lax.axis_index("req")
    barrier = pltpu.get_barrier_semaphore()
    for step in range(1, n_ctx):
        other = lax.rem(me + step, n_ctx)
        pl.semaphore_signal(barrier, inc=1, device_id=(other, row), device_id_type=MESH)
    pl.semaphore_wait(barrier, n_ctx - 1)

    def key_copy(source, target):
        return pltpu.make_async_remote_copy(
            src_ref=keys_ref,
            dst_ref=keys_out.at[source],
            send_sem=sems.at[0, target],
            recv_sem=sems.at[1, source],
            device_id=(target, row),
            device_id_type=MESH,
        )

    def part_copy(source, target):
        return pltpu.make_async_remote_copy(
            src_ref=parts_ref.at[target],
            dst_ref=parts_out.at[source],
            send_sem=sems.at[2, target],
            recv_sem=sems.at[3, source],
            device_id=(target, row),
            device_id_type=MESH,
        )

    own_keys = pltpu.make_async_copy(keys_ref, keys_out.at[me], sems.at[4, 0])
    own_parts = pltpu.make_async_copy(parts_ref.at[me], parts_out.at[me], sems.at[4, 1])
    own_keys.start()
    own_parts.start()
    for step in range(1, n_ctx):
        other = lax.rem(me + step, n_ctx)
        key_copy(me, other).start()
        part_copy(me, other).start()
    for step in range(1, n_ctx):
        other = lax.rem(me + step, n_ctx)
        source = lax.rem(me + n_ctx - step, n_ctx)
        key_copy(me, other).wait_send()
        part_copy(me, other).wait_send()
        key_copy(source, me).wait_recv()
        part_copy(source, me).wait_recv()
    own_keys.wait()
    own_parts.wait()


def context_exchange(keys, parts, n_ctx):
    return pl.pallas_call(
        functools.partial(context_kernel, n_ctx),
        out_shape=(
            jax.ShapeDtypeStruct((n_ctx,) + keys.shape, keys.dtype),
            jax.ShapeDtypeStruct(parts.shape, parts.dtype),
        ),
        in_specs=[pl.BlockSpec(memory_space=pl.ANY)] * 2,
        out_specs=(pl.BlockSpec(memory_space=pl.ANY), pl.BlockSpec(memory_space=pl.ANY)),
        scratch_shapes=[pltpu.SemaphoreType.DMA((5, n_ctx))],
        compiler_params=pltpu.CompilerParams(collective_id=2, has_side_effects=True),
    )(keys, parts)


def body(
    pre_latent,
    pre_qlat,
    pre_qrope,
    pre_resid,
    block_order,
    dec_new,
    dec_qlat,
    dec_qrope,
    dec_resid,
    cache_len,
    page_table,
    cache_pool,
    w_uv,
    w_out,
    norm_gain,
    router,
    routes,
    w_gate,
    w_up,
    w_down,
):
    ctx_count = lax.axis_size("ctx")
    ctx_index = lax.axis_index("ctx")
    score_scale = (DN + DR) ** (-0.5)
    latent = pre_latent[0]
    shard_rows = latent.shape[0]
    local_rows = jnp.arange(shard_rows)
    own_pos = block_position(block_order, ctx_index * shard_rows + local_rows, shard_rows)
    cos_table, sin_table = rope_tables(own_pos, DR)
    key_rope = rotate(latent[:, DC:], cos_table, sin_table).astype(jnp.bfloat16)
    stored = jnp.concatenate([latent[:, :DC], key_rope], axis=-1)
    rotated = rotate(pre_qrope[0], cos_table[:, None, :], sin_table[:, None, :]).astype(
        jnp.bfloat16
    )
    head_count = pre_qlat.shape[2]

    lengths = cache_len[:, 0]
    tables = page_table[:, 0, :]
    request_count = tables.shape[0]
    pages_dev = tables.shape[1]
    page_rows = cache_pool.shape[1]
    slot_count = cache_pool.shape[0]
    row_width = cache_pool.shape[2]
    cos_new, sin_new = rope_tables(lengths, DR)
    new_rope = rotate(dec_new[:, 0, DC:], cos_new, sin_new).astype(jnp.bfloat16)
    new_rows = jnp.concatenate([dec_new[:, 0, :DC], new_rope], axis=-1)
    page_index = lengths // page_rows
    owner_ctx = page_index // pages_dev
    page_hit = tables[:, :, None] == jnp.arange(slot_count)[None, None, :]
    wanted = jnp.arange(pages_dev)[None, :] == (page_index % pages_dev)[:, None]
    slot_of = jnp.sum(jnp.where(wanted, tables, 0), axis=1)
    target = jnp.where(
        owner_ctx == ctx_index, slot_of * page_rows + lengths % page_rows, slot_count * page_rows
    )
    row_ids = jnp.arange(slot_count * page_rows)[:, None]
    flat_pool = cache_pool.reshape(slot_count * page_rows, row_width)
    for request in range(request_count):
        flat_pool = jnp.where(row_ids == target[request], new_rows[request][None, :], flat_pool)
    page_valid = jnp.any(page_hit, axis=1)
    page_logical = jnp.sum(page_hit.astype(jnp.int32) * jnp.arange(pages_dev)[None, :, None], axis=1)
    page_start = (ctx_index * pages_dev + page_logical) * page_rows
    key_pos = (page_start[:, :, None] + jnp.arange(page_rows)[None, None, :]).reshape(
        request_count, slot_count * page_rows
    )
    dec_visible = (
        jnp.repeat(page_valid, page_rows, axis=1) & (key_pos <= lengths[:, None])
    )[:, None, :]
    query_rot = rotate(dec_qrope[:, 0], cos_new[:, None, :], sin_new[:, None, :]).astype(
        jnp.bfloat16
    )
    dec_queries = jnp.concatenate([dec_qlat[:, 0], query_rot], axis=-1)
    flat_queries = dec_queries.reshape(request_count * head_count, row_width)
    dec_scores = (
        jnp.dot(flat_pool, flat_queries.T, preferred_element_type=jnp.float32) * score_scale
    ).reshape(slot_count * page_rows, request_count, head_count)
    dec_seen = jnp.transpose(dec_visible[:, 0, :])[:, :, None]
    dec_masked = jnp.where(dec_seen, dec_scores, NEG_FILL)
    local_peak = jnp.max(dec_masked, axis=0)
    dec_weights = jnp.where(dec_seen, jnp.exp(dec_masked - local_peak[None]), 0.0)
    local_total = jnp.sum(dec_weights, axis=0)
    local_accum = lax.dot_general(
        dec_weights.astype(jnp.bfloat16).reshape(slot_count * page_rows, -1),
        flat_pool[:, :DC],
        (((0,), (0,)), ((), ())),
        preferred_element_type=jnp.float32,
    ).reshape(request_count, head_count, DC)

    dec_share = request_count // ctx_count
    part_width = 128 * ((DC + 2 + 127) // 128)
    dec_block = jnp.concatenate(
        [
            local_accum,
            local_peak[..., None],
            local_total[..., None],
            jnp.zeros((request_count, head_count, part_width - DC - 2), jnp.float32),
        ],
        axis=2,
    ).reshape(ctx_count, dec_share * head_count, part_width)
    keys_all, own_parts = context_exchange(stored, dec_block, ctx_count)
    moving = keys_all.reshape(ctx_count * shard_rows, row_width)
    own_parts = own_parts.reshape(ctx_count, dec_share, head_count, part_width)
    part_accum = own_parts[..., :DC]
    part_peak = own_parts[..., DC]
    part_total = own_parts[..., DC + 1]
    merged_peak = jnp.max(part_peak, axis=0)
    factor = jnp.exp(part_peak - merged_peak[None])
    merged_total = jnp.sum(part_total * factor, axis=0)
    merged_accum = jnp.sum(part_accum * factor[..., None], axis=0)
    own_mixed = (merged_accum / merged_total[..., None]).astype(jnp.bfloat16)

    key_pos_pre = block_position(block_order, jnp.arange(moving.shape[0]), shard_rows)
    query_rows = shard_rows * head_count
    scores = (
        jnp.dot(
            pre_qlat[0].reshape(query_rows, DC), moving[:, :DC].T,
            preferred_element_type=jnp.float32,
        )
        + jnp.dot(
            rotated.reshape(query_rows, DR), moving[:, DC:].T,
            preferred_element_type=jnp.float32,
        )
    ) * score_scale
    visible = jnp.repeat(key_pos_pre[None, :] <= own_pos[:, None], head_count, axis=0)
    masked = jnp.where(visible, scores, NEG_FILL)
    new_peak = jnp.max(masked, axis=-1)
    weights = jnp.where(visible, jnp.exp(masked - new_peak[..., None]), 0.0)
    totals = jnp.sum(weights, axis=-1)
    accumulated = jnp.dot(
        weights.astype(jnp.bfloat16), moving[:, :DC], preferred_element_type=jnp.float32
    )
    pre_mixed = (accumulated / totals[:, None]).astype(jnp.bfloat16).reshape(
        shard_rows, head_count, DC
    )

    own_resid = lax.dynamic_slice_in_dim(dec_resid[:, 0], ctx_index * dec_share, dec_share, 0)
    mixed_all = jnp.concatenate([pre_mixed, own_mixed], axis=0)
    resid_all = jnp.concatenate([pre_resid[0], own_resid], axis=0)
    values = jnp.einsum("nhc,hcv->nhv", mixed_all, w_uv, preferred_element_type=jnp.float32).astype(
        jnp.bfloat16
    )
    hidden_state = resid_all.astype(jnp.float32) + jnp.dot(
        values.reshape(values.shape[0], -1), w_out, preferred_element_type=jnp.float32
    )
    normed = (
        hidden_state
        * lax.rsqrt(jnp.mean(hidden_state * hidden_state, axis=-1, keepdims=True) + EPSILON)
        * norm_gain
    ).astype(jnp.bfloat16)
    logits = jnp.dot(normed.astype(jnp.float32), router, precision=lax.Precision.HIGHEST)
    probable = jax.nn.sigmoid(logits)
    row_count = normed.shape[0]
    width = normed.shape[1]
    top_count = routes.shape[1]
    expert_count = router.shape[1]
    devices = ctx_count * lax.axis_size("req")
    capacity = 2 * ((row_count * top_count + 2 * expert_count - 1) // (2 * expert_count))
    route_hit = routes[:, :, None] == jnp.arange(expert_count)[None, None, :]
    chosen = jnp.sum(jnp.where(route_hit, probable[:, None, :], 0.0), axis=-1)
    mixing = ROUTE_SCALE * chosen / jnp.sum(chosen, axis=1, keepdims=True)
    expert_hits = route_hit.astype(jnp.int32).sum(1)
    earlier = (jnp.arange(row_count)[None, :] < jnp.arange(row_count)[:, None]).astype(jnp.bfloat16)
    before = jnp.dot(
        earlier, expert_hits.astype(jnp.bfloat16), preferred_element_type=jnp.float32
    ).astype(jnp.int32)
    slot_index = jnp.sum(jnp.where(route_hit, before[:, None, :], 0), axis=-1)
    target_slot = routes * capacity + slot_index
    slot_hit = target_slot[:, :, None] == jnp.arange(expert_count * capacity)[None, None, :]
    dispatch = jnp.any(slot_hit, axis=1).astype(jnp.bfloat16)
    outgoing = lax.dot_general(
        dispatch, normed, (((0,), (0,)), ((), ())), preferred_element_type=jnp.float32
    ).astype(jnp.bfloat16).reshape(expert_count, capacity, width)
    doubled = jnp.broadcast_to(outgoing[:, None], (expert_count, 2, capacity, width)).reshape(
        devices, capacity, width
    )
    partial_out = expert_half(
        lax.all_to_all(doubled, ("ctx", "req"), split_axis=0, concat_axis=0, tiled=True),
        w_gate[0],
        w_up[0],
        w_down[0],
    )
    returned = lax.all_to_all(
        partial_out, ("ctx", "req"), split_axis=0, concat_axis=0, tiled=True
    ).reshape(expert_count, 2, capacity, width)
    results = (returned[:, 0].astype(jnp.float32) + returned[:, 1].astype(jnp.float32)).astype(
        jnp.bfloat16
    ).reshape(expert_count * capacity, width)
    combine = jnp.sum(jnp.where(slot_hit, mixing[:, :, None], 0.0), axis=1)
    moe = jnp.dot(combine, results.astype(jnp.float32), precision=lax.Precision.HIGHEST)
    final = (hidden_state + moe).astype(jnp.bfloat16)
    pre_out = final[:shard_rows][None]
    dec_out = final[shard_rows:][:, None]
    cache_out = flat_pool.reshape(cache_pool.shape)
    return (pre_out, dec_out, cache_out)


def solution(mesh):
    in_specs = (
        P("req", "ctx", None),
        P("req", "ctx", None, None),
        P("req", "ctx", None, None),
        P("req", "ctx", None),
        P(),
        P(None, "req", None),
        P(None, "req", None, None),
        P(None, "req", None, None),
        P(None, "req", None),
        P(None, "req"),
        P(None, "req", "ctx"),
        P(("ctx", "req"), None, None),
        P(),
        P(),
        P(),
        P(),
        P(("ctx", "req"), None),
        P(("ctx", "req"), None, None),
        P(("ctx", "req"), None, None),
        P(("ctx", "req"), None, None),
    )
    out_specs = (P("req", "ctx", None), P("ctx", "req", None), P(("ctx", "req"), None, None))
    return jax.shard_map(body, mesh=mesh, in_specs=in_specs, out_specs=out_specs, check_vma=False)
```

```python
import functools

import jax
import jax.numpy as jnp
from jax import lax
from jax.experimental import pallas as pl
from jax.experimental.pallas import tpu as pltpu
from jax.sharding import PartitionSpec as P

MESH = pl.DeviceIdType.MESH

DC = 512
DR = 64
DN = 128


THETA = 50000.0
ROUTE_SCALE = 2.446
EPSILON = 1e-06
NEG_FILL = -1e30


def joined(part, axis, combine):
    gathered = jax.tree.map(lambda a: lax.all_gather(a, axis), part)

    def take(source):
        return jax.tree.map(lambda a: lax.dynamic_index_in_dim(a, source, 0, False), gathered)

    return lax.fori_loop(
        1, lax.axis_size(axis), lambda source, state: combine(state, take(source)), take(0)
    )


def rope_tables(positions, rope_width):
    halfway = rope_width // 2
    inverse = THETA ** (-(jnp.arange(halfway).astype(jnp.float32) * 2.0) / rope_width)
    angles = positions.astype(jnp.float32)[..., None] * inverse
    return (jnp.cos(angles), jnp.sin(angles))


def rotate(values, cos_table, sin_table):
    halfway = values.shape[-1] // 2
    leading = values[..., :halfway].astype(jnp.float32)
    trailing = values[..., halfway:].astype(jnp.float32)
    return jnp.concatenate(
        [leading * cos_table - trailing * sin_table, trailing * cos_table + leading * sin_table],
        axis=-1,
    )


def block_position(block_order, global_rows, shard_rows):
    half_rows = shard_rows // 2
    block = global_rows // half_rows
    hit = block[:, None] == jnp.arange(block_order.shape[0])[None, :]
    logical = jnp.sum(jnp.where(hit, block_order[None, :], 0), axis=1)
    return logical * half_rows + global_rows % half_rows


def expert_half(inputs, gate_part, up_part, down_part):
    flat_rows = inputs.reshape(-1, inputs.shape[-1])
    gate_out = jnp.dot(flat_rows, gate_part, preferred_element_type=jnp.float32)
    upward = jnp.dot(flat_rows, up_part, preferred_element_type=jnp.float32)
    hidden = (jax.nn.silu(gate_out) * upward).astype(jnp.bfloat16)
    partial_out = jnp.dot(hidden, down_part, preferred_element_type=jnp.float32).astype(
        jnp.bfloat16
    )
    return partial_out.reshape(inputs.shape)


def merge_softmax(earlier, later):
    left_peak, left_total, left_accum = earlier
    right_peak, right_total, right_accum = later
    new_peak = jnp.maximum(left_peak, right_peak)
    left_factor = jnp.exp(left_peak - new_peak)
    right_factor = jnp.exp(right_peak - new_peak)
    merged_total = left_total * left_factor + right_total * right_factor
    merged_accum = left_accum * left_factor[..., None] + right_accum * right_factor[..., None]
    return (new_peak, merged_total, merged_accum)


def exchange_kernel(n_req, total, x_ref, out_ref, send_sem, recv_sem, local_sem):
    me = lax.axis_index("ctx") * n_req + lax.axis_index("req")

    def device(d):
        return (d // n_req, d % n_req)

    def outgoing(d):
        return pltpu.make_async_remote_copy(
            src_ref=x_ref.at[d],
            dst_ref=out_ref.at[me],
            send_sem=send_sem.at[d],
            recv_sem=recv_sem.at[me],
            device_id=device(d),
            device_id_type=MESH,
        )

    def incoming(s):
        return pltpu.make_async_remote_copy(
            src_ref=x_ref.at[me],
            dst_ref=out_ref.at[s],
            send_sem=send_sem.at[s],
            recv_sem=recv_sem.at[s],
            device_id=device(s),
            device_id_type=MESH,
        )

    barrier = pltpu.get_barrier_semaphore()

    def greet(k, carry):
        d = lax.rem(me + k, total)
        pl.semaphore_signal(barrier, inc=1, device_id=device(d), device_id_type=MESH)
        return carry

    lax.fori_loop(1, total, greet, 0)
    pl.semaphore_wait(barrier, total - 1)
    local = pltpu.make_async_copy(x_ref.at[me], out_ref.at[me], local_sem)
    local.start()

    def send(k, carry):
        outgoing(lax.rem(me + k, total)).start()
        return carry

    lax.fori_loop(1, total, send, 0)

    def finish(k, carry):
        outgoing(lax.rem(me + k, total)).wait_send()
        incoming(lax.rem(me + total - k, total)).wait_recv()
        return carry

    lax.fori_loop(1, total, finish, 0)
    local.wait()


def exchange(x, n_req, total, collective_id):
    return pl.pallas_call(
        functools.partial(exchange_kernel, n_req, total),
        out_shape=jax.ShapeDtypeStruct(x.shape, x.dtype),
        in_specs=[pl.BlockSpec(memory_space=pl.ANY)],
        out_specs=pl.BlockSpec(memory_space=pl.ANY),
        scratch_shapes=[
            pltpu.SemaphoreType.DMA((total,)),
            pltpu.SemaphoreType.DMA((total,)),
            pltpu.SemaphoreType.DMA(()),
        ],
        compiler_params=pltpu.CompilerParams(collective_id=collective_id, has_side_effects=True),
    )(x)


def context_kernel(n_ctx, keys_ref, parts_ref, keys_out, parts_out, sems):
    me = lax.axis_index("ctx")
    row = lax.axis_index("req")
    barrier = pltpu.get_barrier_semaphore()
    for step in range(1, n_ctx):
        other = lax.rem(me + step, n_ctx)
        pl.semaphore_signal(barrier, inc=1, device_id=(other, row), device_id_type=MESH)
    pl.semaphore_wait(barrier, n_ctx - 1)

    def key_copy(source, target):
        return pltpu.make_async_remote_copy(
            src_ref=keys_ref,
            dst_ref=keys_out.at[source],
            send_sem=sems.at[0, target],
            recv_sem=sems.at[1, source],
            device_id=(target, row),
            device_id_type=MESH,
        )

    def part_copy(source, target):
        return pltpu.make_async_remote_copy(
            src_ref=parts_ref.at[target],
            dst_ref=parts_out.at[source],
            send_sem=sems.at[2, target],
            recv_sem=sems.at[3, source],
            device_id=(target, row),
            device_id_type=MESH,
        )

    own_keys = pltpu.make_async_copy(keys_ref, keys_out.at[me], sems.at[4, 0])
    own_parts = pltpu.make_async_copy(parts_ref.at[me], parts_out.at[me], sems.at[4, 1])
    own_keys.start()
    own_parts.start()
    for step in range(1, n_ctx):
        other = lax.rem(me + step, n_ctx)
        key_copy(me, other).start()
        part_copy(me, other).start()
    for step in range(1, n_ctx):
        other = lax.rem(me + step, n_ctx)
        source = lax.rem(me + n_ctx - step, n_ctx)
        key_copy(me, other).wait_send()
        part_copy(me, other).wait_send()
        key_copy(source, me).wait_recv()
        part_copy(source, me).wait_recv()
    own_keys.wait()
    own_parts.wait()


def context_exchange(keys, parts, n_ctx):
    return pl.pallas_call(
        functools.partial(context_kernel, n_ctx),
        out_shape=(
            jax.ShapeDtypeStruct((n_ctx,) + keys.shape, keys.dtype),
            jax.ShapeDtypeStruct(parts.shape, parts.dtype),
        ),
        in_specs=[pl.BlockSpec(memory_space=pltpu.VMEM)] * 2,
        out_specs=(pl.BlockSpec(memory_space=pltpu.VMEM), pl.BlockSpec(memory_space=pltpu.VMEM)),
        scratch_shapes=[pltpu.SemaphoreType.DMA((5, n_ctx))],
        compiler_params=pltpu.CompilerParams(collective_id=2, has_side_effects=True),
    )(keys, parts)


def body(
    pre_latent,
    pre_qlat,
    pre_qrope,
    pre_resid,
    block_order,
    dec_new,
    dec_qlat,
    dec_qrope,
    dec_resid,
    cache_len,
    page_table,
    cache_pool,
    w_uv,
    w_out,
    norm_gain,
    router,
    routes,
    w_gate,
    w_up,
    w_down,
):
    ctx_count = lax.axis_size("ctx")
    ctx_index = lax.axis_index("ctx")
    score_scale = (DN + DR) ** (-0.5)
    latent = pre_latent[0]
    shard_rows = latent.shape[0]
    local_rows = jnp.arange(shard_rows)
    own_pos = block_position(block_order, ctx_index * shard_rows + local_rows, shard_rows)
    cos_table, sin_table = rope_tables(own_pos, DR)
    key_rope = rotate(latent[:, DC:], cos_table, sin_table).astype(jnp.bfloat16)
    stored = jnp.concatenate([latent[:, :DC], key_rope], axis=-1)
    rotated = rotate(pre_qrope[0], cos_table[:, None, :], sin_table[:, None, :]).astype(
        jnp.bfloat16
    )
    head_count = pre_qlat.shape[2]

    lengths = cache_len[:, 0]
    tables = page_table[:, 0, :]
    request_count = tables.shape[0]
    pages_dev = tables.shape[1]
    page_rows = cache_pool.shape[1]
    slot_count = cache_pool.shape[0]
    row_width = cache_pool.shape[2]
    cos_new, sin_new = rope_tables(lengths, DR)
    new_rope = rotate(dec_new[:, 0, DC:], cos_new, sin_new).astype(jnp.bfloat16)
    new_rows = jnp.concatenate([dec_new[:, 0, :DC], new_rope], axis=-1)
    page_index = lengths // page_rows
    owner_ctx = page_index // pages_dev
    page_hit = tables[:, :, None] == jnp.arange(slot_count)[None, None, :]
    wanted = jnp.arange(pages_dev)[None, :] == (page_index % pages_dev)[:, None]
    slot_of = jnp.sum(jnp.where(wanted, tables, 0), axis=1)
    target = jnp.where(
        owner_ctx == ctx_index, slot_of * page_rows + lengths % page_rows, slot_count * page_rows
    )
    row_ids = jnp.arange(slot_count * page_rows)[:, None]
    flat_pool = cache_pool.reshape(slot_count * page_rows, row_width)
    for request in range(request_count):
        flat_pool = jnp.where(row_ids == target[request], new_rows[request][None, :], flat_pool)
    page_valid = jnp.any(page_hit, axis=1)
    page_logical = jnp.sum(page_hit.astype(jnp.int32) * jnp.arange(pages_dev)[None, :, None], axis=1)
    page_start = (ctx_index * pages_dev + page_logical) * page_rows
    key_pos = (page_start[:, :, None] + jnp.arange(page_rows)[None, None, :]).reshape(
        request_count, slot_count * page_rows
    )
    dec_visible = (
        jnp.repeat(page_valid, page_rows, axis=1) & (key_pos <= lengths[:, None])
    )[:, None, :]
    query_rot = rotate(dec_qrope[:, 0], cos_new[:, None, :], sin_new[:, None, :]).astype(
        jnp.bfloat16
    )
    dec_queries = jnp.concatenate([dec_qlat[:, 0], query_rot], axis=-1)
    flat_queries = dec_queries.reshape(request_count * head_count, row_width)
    dec_scores = (
        jnp.dot(flat_pool, flat_queries.T, preferred_element_type=jnp.float32) * score_scale
    ).reshape(slot_count * page_rows, request_count, head_count)
    dec_seen = jnp.transpose(dec_visible[:, 0, :])[:, :, None]
    dec_masked = jnp.where(dec_seen, dec_scores, NEG_FILL)
    local_peak = jnp.max(dec_masked, axis=0)
    dec_weights = jnp.where(dec_seen, jnp.exp(dec_masked - local_peak[None]), 0.0)
    local_total = jnp.sum(dec_weights, axis=0)
    local_accum = lax.dot_general(
        dec_weights.astype(jnp.bfloat16).reshape(slot_count * page_rows, -1),
        flat_pool[:, :DC],
        (((0,), (0,)), ((), ())),
        preferred_element_type=jnp.float32,
    ).reshape(request_count, head_count, DC)

    dec_share = request_count // ctx_count
    part_width = 128 * ((DC + 2 + 127) // 128)
    dec_block = jnp.concatenate(
        [
            local_accum,
            local_peak[..., None],
            local_total[..., None],
            jnp.zeros((request_count, head_count, part_width - DC - 2), jnp.float32),
        ],
        axis=2,
    ).reshape(ctx_count, dec_share * head_count, part_width)
    keys_all, own_parts = context_exchange(stored, dec_block, ctx_count)
    moving = keys_all.reshape(ctx_count * shard_rows, row_width)
    own_parts = own_parts.reshape(ctx_count, dec_share, head_count, part_width)
    part_accum = own_parts[..., :DC]
    part_peak = own_parts[..., DC]
    part_total = own_parts[..., DC + 1]
    merged_peak = jnp.max(part_peak, axis=0)
    factor = jnp.exp(part_peak - merged_peak[None])
    merged_total = jnp.sum(part_total * factor, axis=0)
    merged_accum = jnp.sum(part_accum * factor[..., None], axis=0)
    own_mixed = (merged_accum / merged_total[..., None]).astype(jnp.bfloat16)

    key_pos_pre = block_position(block_order, jnp.arange(moving.shape[0]), shard_rows)
    query_rows = shard_rows * head_count
    scores = (
        jnp.dot(
            pre_qlat[0].reshape(query_rows, DC), moving[:, :DC].T,
            preferred_element_type=jnp.float32,
        )
        + jnp.dot(
            rotated.reshape(query_rows, DR), moving[:, DC:].T,
            preferred_element_type=jnp.float32,
        )
    ) * score_scale
    visible = jnp.repeat(key_pos_pre[None, :] <= own_pos[:, None], head_count, axis=0)
    masked = jnp.where(visible, scores, NEG_FILL)
    new_peak = jnp.max(masked, axis=-1)
    weights = jnp.where(visible, jnp.exp(masked - new_peak[..., None]), 0.0)
    totals = jnp.sum(weights, axis=-1)
    accumulated = jnp.dot(
        weights.astype(jnp.bfloat16), moving[:, :DC], preferred_element_type=jnp.float32
    )
    pre_mixed = (accumulated / totals[:, None]).astype(jnp.bfloat16).reshape(
        shard_rows, head_count, DC
    )

    own_resid = lax.dynamic_slice_in_dim(dec_resid[:, 0], ctx_index * dec_share, dec_share, 0)
    mixed_all = jnp.concatenate([pre_mixed, own_mixed], axis=0)
    resid_all = jnp.concatenate([pre_resid[0], own_resid], axis=0)
    values = jnp.einsum("nhc,hcv->nhv", mixed_all, w_uv, preferred_element_type=jnp.float32).astype(
        jnp.bfloat16
    )
    hidden_state = resid_all.astype(jnp.float32) + jnp.dot(
        values.reshape(values.shape[0], -1), w_out, preferred_element_type=jnp.float32
    )
    normed = (
        hidden_state
        * lax.rsqrt(jnp.mean(hidden_state * hidden_state, axis=-1, keepdims=True) + EPSILON)
        * norm_gain
    ).astype(jnp.bfloat16)
    logits = jnp.dot(normed.astype(jnp.float32), router, precision=lax.Precision.HIGHEST)
    probable = jax.nn.sigmoid(logits)
    row_count = normed.shape[0]
    width = normed.shape[1]
    top_count = routes.shape[1]
    expert_count = router.shape[1]
    devices = ctx_count * lax.axis_size("req")
    capacity = 2 * ((row_count * top_count + 2 * expert_count - 1) // (2 * expert_count))
    route_hit = routes[:, :, None] == jnp.arange(expert_count)[None, None, :]
    chosen = jnp.sum(jnp.where(route_hit, probable[:, None, :], 0.0), axis=-1)
    mixing = ROUTE_SCALE * chosen / jnp.sum(chosen, axis=1, keepdims=True)
    expert_hits = route_hit.astype(jnp.int32).sum(1)
    earlier = (jnp.arange(row_count)[None, :] < jnp.arange(row_count)[:, None]).astype(jnp.bfloat16)
    before = jnp.dot(
        earlier, expert_hits.astype(jnp.bfloat16), preferred_element_type=jnp.float32
    ).astype(jnp.int32)
    slot_index = jnp.sum(jnp.where(route_hit, before[:, None, :], 0), axis=-1)
    target_slot = routes * capacity + slot_index
    slot_hit = target_slot[:, :, None] == jnp.arange(expert_count * capacity)[None, None, :]
    dispatch = jnp.any(slot_hit, axis=1).astype(jnp.bfloat16)
    outgoing = lax.dot_general(
        dispatch, normed, (((0,), (0,)), ((), ())), preferred_element_type=jnp.float32
    ).astype(jnp.bfloat16).reshape(expert_count, capacity, width)
    doubled = jnp.broadcast_to(outgoing[:, None], (expert_count, 2, capacity, width)).reshape(
        devices, capacity, width
    )
    partial_out = expert_half(
        lax.all_to_all(doubled, ("ctx", "req"), split_axis=0, concat_axis=0, tiled=True),
        w_gate[0],
        w_up[0],
        w_down[0],
    )
    returned = lax.all_to_all(
        partial_out, ("ctx", "req"), split_axis=0, concat_axis=0, tiled=True
    ).reshape(expert_count, 2, capacity, width)
    results = (returned[:, 0].astype(jnp.float32) + returned[:, 1].astype(jnp.float32)).astype(
        jnp.bfloat16
    ).reshape(expert_count * capacity, width)
    combine = jnp.sum(jnp.where(slot_hit, mixing[:, :, None], 0.0), axis=1)
    moe = jnp.dot(combine, results.astype(jnp.float32), precision=lax.Precision.HIGHEST)
    final = (hidden_state + moe).astype(jnp.bfloat16)
    pre_out = final[:shard_rows][None]
    dec_out = final[shard_rows:][:, None]
    cache_out = flat_pool.reshape(cache_pool.shape)
    return (pre_out, dec_out, cache_out)


def solution(mesh):
    in_specs = (
        P("req", "ctx", None),
        P("req", "ctx", None, None),
        P("req", "ctx", None, None),
        P("req", "ctx", None),
        P(),
        P(None, "req", None),
        P(None, "req", None, None),
        P(None, "req", None, None),
        P(None, "req", None),
        P(None, "req"),
        P(None, "req", "ctx"),
        P(("ctx", "req"), None, None),
        P(),
        P(),
        P(),
        P(),
        P(("ctx", "req"), None),
        P(("ctx", "req"), None, None),
        P(("ctx", "req"), None, None),
        P(("ctx", "req"), None, None),
    )
    out_specs = (P("req", "ctx", None), P("ctx", "req", None), P(("ctx", "req"), None, None))
    return jax.shard_map(body, mesh=mesh, in_specs=in_specs, out_specs=out_specs, check_vma=False)
```

```python
import functools

import jax
import jax.numpy as jnp
from jax import lax
from jax.experimental import pallas as pl
from jax.experimental.pallas import tpu as pltpu
from jax.sharding import PartitionSpec as P

MESH = pl.DeviceIdType.MESH

DC = 512
DR = 64
DN = 128


THETA = 50000.0
ROUTE_SCALE = 2.446
EPSILON = 1e-06
NEG_FILL = -1e30


def joined(part, axis, combine):
    gathered = jax.tree.map(lambda a: lax.all_gather(a, axis), part)

    def take(source):
        return jax.tree.map(lambda a: lax.dynamic_index_in_dim(a, source, 0, False), gathered)

    return lax.fori_loop(
        1, lax.axis_size(axis), lambda source, state: combine(state, take(source)), take(0)
    )


def rope_tables(positions, rope_width):
    halfway = rope_width // 2
    inverse = THETA ** (-(jnp.arange(halfway).astype(jnp.float32) * 2.0) / rope_width)
    angles = positions.astype(jnp.float32)[..., None] * inverse
    return (jnp.cos(angles), jnp.sin(angles))


def rotate(values, cos_table, sin_table):
    halfway = values.shape[-1] // 2
    leading = values[..., :halfway].astype(jnp.float32)
    trailing = values[..., halfway:].astype(jnp.float32)
    return jnp.concatenate(
        [leading * cos_table - trailing * sin_table, trailing * cos_table + leading * sin_table],
        axis=-1,
    )


def block_position(block_order, global_rows, shard_rows):
    half_rows = shard_rows // 2
    block = global_rows // half_rows
    hit = block[:, None] == jnp.arange(block_order.shape[0])[None, :]
    logical = jnp.sum(jnp.where(hit, block_order[None, :], 0), axis=1)
    return logical * half_rows + global_rows % half_rows


def expert_half(inputs, gate_part, up_part, down_part):
    flat_rows = inputs.reshape(-1, inputs.shape[-1])
    gate_out = jnp.dot(flat_rows, gate_part, preferred_element_type=jnp.float32)
    upward = jnp.dot(flat_rows, up_part, preferred_element_type=jnp.float32)
    hidden = (jax.nn.silu(gate_out) * upward).astype(jnp.bfloat16)
    partial_out = jnp.dot(hidden, down_part, preferred_element_type=jnp.float32).astype(
        jnp.bfloat16
    )
    return partial_out.reshape(inputs.shape)


def merge_softmax(earlier, later):
    left_peak, left_total, left_accum = earlier
    right_peak, right_total, right_accum = later
    new_peak = jnp.maximum(left_peak, right_peak)
    left_factor = jnp.exp(left_peak - new_peak)
    right_factor = jnp.exp(right_peak - new_peak)
    merged_total = left_total * left_factor + right_total * right_factor
    merged_accum = left_accum * left_factor[..., None] + right_accum * right_factor[..., None]
    return (new_peak, merged_total, merged_accum)


def exchange_kernel(n_req, total, window, x_ref, out_ref, send_sem, recv_sem, local_sem):
    me = lax.axis_index("ctx") * n_req + lax.axis_index("req")

    def device(d):
        return (d // n_req, d % n_req)

    def outgoing(d):
        return pltpu.make_async_remote_copy(
            src_ref=x_ref.at[d],
            dst_ref=out_ref.at[me],
            send_sem=send_sem.at[d],
            recv_sem=recv_sem.at[me],
            device_id=device(d),
            device_id_type=MESH,
        )

    def incoming(s):
        return pltpu.make_async_remote_copy(
            src_ref=x_ref.at[me],
            dst_ref=out_ref.at[s],
            send_sem=send_sem.at[s],
            recv_sem=recv_sem.at[s],
            device_id=device(s),
            device_id_type=MESH,
        )

    barrier = pltpu.get_barrier_semaphore()

    def greet(k, carry):
        d = lax.rem(me + k, total)
        pl.semaphore_signal(barrier, inc=1, device_id=device(d), device_id_type=MESH)
        return carry

    lax.fori_loop(1, total, greet, 0)
    pl.semaphore_wait(barrier, total - 1)
    local = pltpu.make_async_copy(x_ref.at[me], out_ref.at[me], local_sem)
    local.start()

    def send(k, carry):
        outgoing(lax.rem(me + k, total)).start()

        @pl.when(k > window)
        def _():
            outgoing(lax.rem(me + k - window, total)).wait_send()

        return carry

    lax.fori_loop(1, total, send, 0)

    def drain(k, carry):
        outgoing(lax.rem(me + k, total)).wait_send()
        return carry

    lax.fori_loop(max(1, total - window), total, drain, 0)

    def finish(k, carry):
        incoming(lax.rem(me + total - k, total)).wait_recv()
        return carry

    lax.fori_loop(1, total, finish, 0)
    local.wait()


def exchange(x, n_req, total, collective_id):
    return pl.pallas_call(
        functools.partial(exchange_kernel, n_req, total, min(16, total // 4)),
        out_shape=jax.ShapeDtypeStruct(x.shape, x.dtype),
        in_specs=[pl.BlockSpec(memory_space=pl.ANY)],
        out_specs=pl.BlockSpec(memory_space=pl.ANY),
        scratch_shapes=[
            pltpu.SemaphoreType.DMA((total,)),
            pltpu.SemaphoreType.DMA((total,)),
            pltpu.SemaphoreType.DMA(()),
        ],
        compiler_params=pltpu.CompilerParams(collective_id=collective_id, has_side_effects=True),
    )(x)


def context_kernel(n_ctx, keys_ref, parts_ref, keys_out, parts_out, sems):
    me = lax.axis_index("ctx")
    row = lax.axis_index("req")
    barrier = pltpu.get_barrier_semaphore()
    for step in range(1, n_ctx):
        other = lax.rem(me + step, n_ctx)
        pl.semaphore_signal(barrier, inc=1, device_id=(other, row), device_id_type=MESH)
    pl.semaphore_wait(barrier, n_ctx - 1)

    def key_copy(source, target):
        return pltpu.make_async_remote_copy(
            src_ref=keys_ref,
            dst_ref=keys_out.at[source],
            send_sem=sems.at[0, target],
            recv_sem=sems.at[1, source],
            device_id=(target, row),
            device_id_type=MESH,
        )

    def part_copy(source, target):
        return pltpu.make_async_remote_copy(
            src_ref=parts_ref.at[target],
            dst_ref=parts_out.at[source],
            send_sem=sems.at[2, target],
            recv_sem=sems.at[3, source],
            device_id=(target, row),
            device_id_type=MESH,
        )

    own_keys = pltpu.make_async_copy(keys_ref, keys_out.at[me], sems.at[4, 0])
    own_parts = pltpu.make_async_copy(parts_ref.at[me], parts_out.at[me], sems.at[4, 1])
    own_keys.start()
    own_parts.start()
    for step in range(1, n_ctx):
        other = lax.rem(me + step, n_ctx)
        key_copy(me, other).start()
        part_copy(me, other).start()
    for step in range(1, n_ctx):
        other = lax.rem(me + step, n_ctx)
        source = lax.rem(me + n_ctx - step, n_ctx)
        key_copy(me, other).wait_send()
        part_copy(me, other).wait_send()
        key_copy(source, me).wait_recv()
        part_copy(source, me).wait_recv()
    own_keys.wait()
    own_parts.wait()


def context_exchange(keys, parts, n_ctx):
    return pl.pallas_call(
        functools.partial(context_kernel, n_ctx),
        out_shape=(
            jax.ShapeDtypeStruct((n_ctx,) + keys.shape, keys.dtype),
            jax.ShapeDtypeStruct(parts.shape, parts.dtype),
        ),
        in_specs=[pl.BlockSpec(memory_space=pl.ANY)] * 2,
        out_specs=(pl.BlockSpec(memory_space=pl.ANY), pl.BlockSpec(memory_space=pl.ANY)),
        scratch_shapes=[pltpu.SemaphoreType.DMA((5, n_ctx))],
        compiler_params=pltpu.CompilerParams(collective_id=2, has_side_effects=True),
    )(keys, parts)


def body(
    pre_latent,
    pre_qlat,
    pre_qrope,
    pre_resid,
    block_order,
    dec_new,
    dec_qlat,
    dec_qrope,
    dec_resid,
    cache_len,
    page_table,
    cache_pool,
    w_uv,
    w_out,
    norm_gain,
    router,
    routes,
    w_gate,
    w_up,
    w_down,
):
    ctx_count = lax.axis_size("ctx")
    ctx_index = lax.axis_index("ctx")
    score_scale = (DN + DR) ** (-0.5)
    latent = pre_latent[0]
    shard_rows = latent.shape[0]
    local_rows = jnp.arange(shard_rows)
    own_pos = block_position(block_order, ctx_index * shard_rows + local_rows, shard_rows)
    cos_table, sin_table = rope_tables(own_pos, DR)
    key_rope = rotate(latent[:, DC:], cos_table, sin_table).astype(jnp.bfloat16)
    stored = jnp.concatenate([latent[:, :DC], key_rope], axis=-1)
    rotated = rotate(pre_qrope[0], cos_table[:, None, :], sin_table[:, None, :]).astype(
        jnp.bfloat16
    )
    head_count = pre_qlat.shape[2]

    lengths = cache_len[:, 0]
    tables = page_table[:, 0, :]
    request_count = tables.shape[0]
    pages_dev = tables.shape[1]
    page_rows = cache_pool.shape[1]
    slot_count = cache_pool.shape[0]
    row_width = cache_pool.shape[2]
    cos_new, sin_new = rope_tables(lengths, DR)
    new_rope = rotate(dec_new[:, 0, DC:], cos_new, sin_new).astype(jnp.bfloat16)
    new_rows = jnp.concatenate([dec_new[:, 0, :DC], new_rope], axis=-1)
    page_index = lengths // page_rows
    owner_ctx = page_index // pages_dev
    page_hit = tables[:, :, None] == jnp.arange(slot_count)[None, None, :]
    wanted = jnp.arange(pages_dev)[None, :] == (page_index % pages_dev)[:, None]
    slot_of = jnp.sum(jnp.where(wanted, tables, 0), axis=1)
    target = jnp.where(
        owner_ctx == ctx_index, slot_of * page_rows + lengths % page_rows, slot_count * page_rows
    )
    row_ids = jnp.arange(slot_count * page_rows)[:, None]
    flat_pool = cache_pool.reshape(slot_count * page_rows, row_width)
    for request in range(request_count):
        flat_pool = jnp.where(row_ids == target[request], new_rows[request][None, :], flat_pool)
    page_valid = jnp.any(page_hit, axis=1)
    page_logical = jnp.sum(page_hit.astype(jnp.int32) * jnp.arange(pages_dev)[None, :, None], axis=1)
    page_start = (ctx_index * pages_dev + page_logical) * page_rows
    key_pos = (page_start[:, :, None] + jnp.arange(page_rows)[None, None, :]).reshape(
        request_count, slot_count * page_rows
    )
    dec_visible = (
        jnp.repeat(page_valid, page_rows, axis=1) & (key_pos <= lengths[:, None])
    )[:, None, :]
    query_rot = rotate(dec_qrope[:, 0], cos_new[:, None, :], sin_new[:, None, :]).astype(
        jnp.bfloat16
    )
    dec_queries = jnp.concatenate([dec_qlat[:, 0], query_rot], axis=-1)
    flat_queries = dec_queries.reshape(request_count * head_count, row_width)
    dec_scores = (
        jnp.dot(flat_pool, flat_queries.T, preferred_element_type=jnp.float32) * score_scale
    ).reshape(slot_count * page_rows, request_count, head_count)
    dec_seen = jnp.transpose(dec_visible[:, 0, :])[:, :, None]
    dec_masked = jnp.where(dec_seen, dec_scores, NEG_FILL)
    local_peak = jnp.max(dec_masked, axis=0)
    dec_weights = jnp.where(dec_seen, jnp.exp(dec_masked - local_peak[None]), 0.0)
    local_total = jnp.sum(dec_weights, axis=0)
    local_accum = lax.dot_general(
        dec_weights.astype(jnp.bfloat16).reshape(slot_count * page_rows, -1),
        flat_pool[:, :DC],
        (((0,), (0,)), ((), ())),
        preferred_element_type=jnp.float32,
    ).reshape(request_count, head_count, DC)

    dec_share = request_count // ctx_count
    part_width = 128 * ((DC + 2 + 127) // 128)
    dec_block = jnp.concatenate(
        [
            local_accum,
            local_peak[..., None],
            local_total[..., None],
            jnp.zeros((request_count, head_count, part_width - DC - 2), jnp.float32),
        ],
        axis=2,
    ).reshape(ctx_count, dec_share * head_count, part_width)
    keys_all, own_parts = context_exchange(stored, dec_block, ctx_count)
    moving = keys_all.reshape(ctx_count * shard_rows, row_width)
    own_parts = own_parts.reshape(ctx_count, dec_share, head_count, part_width)
    part_accum = own_parts[..., :DC]
    part_peak = own_parts[..., DC]
    part_total = own_parts[..., DC + 1]
    merged_peak = jnp.max(part_peak, axis=0)
    factor = jnp.exp(part_peak - merged_peak[None])
    merged_total = jnp.sum(part_total * factor, axis=0)
    merged_accum = jnp.sum(part_accum * factor[..., None], axis=0)
    own_mixed = (merged_accum / merged_total[..., None]).astype(jnp.bfloat16)

    key_pos_pre = block_position(block_order, jnp.arange(moving.shape[0]), shard_rows)
    query_rows = shard_rows * head_count
    scores = (
        jnp.dot(
            pre_qlat[0].reshape(query_rows, DC), moving[:, :DC].T,
            preferred_element_type=jnp.float32,
        )
        + jnp.dot(
            rotated.reshape(query_rows, DR), moving[:, DC:].T,
            preferred_element_type=jnp.float32,
        )
    ) * score_scale
    visible = jnp.repeat(key_pos_pre[None, :] <= own_pos[:, None], head_count, axis=0)
    masked = jnp.where(visible, scores, NEG_FILL)
    new_peak = jnp.max(masked, axis=-1)
    weights = jnp.where(visible, jnp.exp(masked - new_peak[..., None]), 0.0)
    totals = jnp.sum(weights, axis=-1)
    accumulated = jnp.dot(
        weights.astype(jnp.bfloat16), moving[:, :DC], preferred_element_type=jnp.float32
    )
    pre_mixed = (accumulated / totals[:, None]).astype(jnp.bfloat16).reshape(
        shard_rows, head_count, DC
    )

    own_resid = lax.dynamic_slice_in_dim(dec_resid[:, 0], ctx_index * dec_share, dec_share, 0)
    mixed_all = jnp.concatenate([pre_mixed, own_mixed], axis=0)
    resid_all = jnp.concatenate([pre_resid[0], own_resid], axis=0)
    values = jnp.einsum("nhc,hcv->nhv", mixed_all, w_uv, preferred_element_type=jnp.float32).astype(
        jnp.bfloat16
    )
    hidden_state = resid_all.astype(jnp.float32) + jnp.dot(
        values.reshape(values.shape[0], -1), w_out, preferred_element_type=jnp.float32
    )
    normed = (
        hidden_state
        * lax.rsqrt(jnp.mean(hidden_state * hidden_state, axis=-1, keepdims=True) + EPSILON)
        * norm_gain
    ).astype(jnp.bfloat16)
    logits = jnp.dot(normed.astype(jnp.float32), router, precision=lax.Precision.HIGHEST)
    probable = jax.nn.sigmoid(logits)
    row_count = normed.shape[0]
    width = normed.shape[1]
    top_count = routes.shape[1]
    expert_count = router.shape[1]
    devices = ctx_count * lax.axis_size("req")
    capacity = 2 * ((row_count * top_count + 2 * expert_count - 1) // (2 * expert_count))
    route_hit = routes[:, :, None] == jnp.arange(expert_count)[None, None, :]
    chosen = jnp.sum(jnp.where(route_hit, probable[:, None, :], 0.0), axis=-1)
    mixing = ROUTE_SCALE * chosen / jnp.sum(chosen, axis=1, keepdims=True)
    expert_hits = route_hit.astype(jnp.int32).sum(1)
    earlier = (jnp.arange(row_count)[None, :] < jnp.arange(row_count)[:, None]).astype(jnp.bfloat16)
    before = jnp.dot(
        earlier, expert_hits.astype(jnp.bfloat16), preferred_element_type=jnp.float32
    ).astype(jnp.int32)
    slot_index = jnp.sum(jnp.where(route_hit, before[:, None, :], 0), axis=-1)
    target_slot = routes * capacity + slot_index
    slot_hit = target_slot[:, :, None] == jnp.arange(expert_count * capacity)[None, None, :]
    dispatch = jnp.any(slot_hit, axis=1).astype(jnp.bfloat16)
    outgoing = lax.dot_general(
        dispatch, normed, (((0,), (0,)), ((), ())), preferred_element_type=jnp.float32
    ).astype(jnp.bfloat16).reshape(expert_count, capacity, width)
    doubled = jnp.broadcast_to(outgoing[:, None], (expert_count, 2, capacity, width)).reshape(
        devices, capacity, width
    )
    req_count = lax.axis_size("req")
    partial_out = expert_half(
        exchange(doubled, req_count, devices, 0),
        w_gate[0],
        w_up[0],
        w_down[0],
    )
    returned = exchange(partial_out, req_count, devices, 1).reshape(
        expert_count, 2, capacity, width
    )
    results = (returned[:, 0].astype(jnp.float32) + returned[:, 1].astype(jnp.float32)).astype(
        jnp.bfloat16
    ).reshape(expert_count * capacity, width)
    combine = jnp.sum(jnp.where(slot_hit, mixing[:, :, None], 0.0), axis=1)
    moe = jnp.dot(combine, results.astype(jnp.float32), precision=lax.Precision.HIGHEST)
    final = (hidden_state + moe).astype(jnp.bfloat16)
    pre_out = final[:shard_rows][None]
    dec_out = final[shard_rows:][:, None]
    cache_out = flat_pool.reshape(cache_pool.shape)
    return (pre_out, dec_out, cache_out)


def solution(mesh):
    in_specs = (
        P("req", "ctx", None),
        P("req", "ctx", None, None),
        P("req", "ctx", None, None),
        P("req", "ctx", None),
        P(),
        P(None, "req", None),
        P(None, "req", None, None),
        P(None, "req", None, None),
        P(None, "req", None),
        P(None, "req"),
        P(None, "req", "ctx"),
        P(("ctx", "req"), None, None),
        P(),
        P(),
        P(),
        P(),
        P(("ctx", "req"), None),
        P(("ctx", "req"), None, None),
        P(("ctx", "req"), None, None),
        P(("ctx", "req"), None, None),
    )
    out_specs = (P("req", "ctx", None), P("ctx", "req", None), P(("ctx", "req"), None, None))
    return jax.shard_map(body, mesh=mesh, in_specs=in_specs, out_specs=out_specs, check_vma=False)
```

```python
import functools

import jax
import jax.numpy as jnp
from jax import lax
from jax.experimental import pallas as pl
from jax.experimental.pallas import tpu as pltpu
from jax.sharding import PartitionSpec as P

MESH = pl.DeviceIdType.MESH

DC = 512
DR = 64
DN = 128


THETA = 50000.0
ROUTE_SCALE = 2.446
EPSILON = 1e-06
NEG_FILL = -1e30


def joined(part, axis, combine):
    gathered = jax.tree.map(lambda a: lax.all_gather(a, axis), part)

    def take(source):
        return jax.tree.map(lambda a: lax.dynamic_index_in_dim(a, source, 0, False), gathered)

    return lax.fori_loop(
        1, lax.axis_size(axis), lambda source, state: combine(state, take(source)), take(0)
    )


def rope_tables(positions, rope_width):
    halfway = rope_width // 2
    inverse = THETA ** (-(jnp.arange(halfway).astype(jnp.float32) * 2.0) / rope_width)
    angles = positions.astype(jnp.float32)[..., None] * inverse
    return (jnp.cos(angles), jnp.sin(angles))


def rotate(values, cos_table, sin_table):
    halfway = values.shape[-1] // 2
    leading = values[..., :halfway].astype(jnp.float32)
    trailing = values[..., halfway:].astype(jnp.float32)
    return jnp.concatenate(
        [leading * cos_table - trailing * sin_table, trailing * cos_table + leading * sin_table],
        axis=-1,
    )


def block_position(block_order, global_rows, shard_rows):
    half_rows = shard_rows // 2
    block = global_rows // half_rows
    hit = block[:, None] == jnp.arange(block_order.shape[0])[None, :]
    logical = jnp.sum(jnp.where(hit, block_order[None, :], 0), axis=1)
    return logical * half_rows + global_rows % half_rows


def expert_half(inputs, gate_part, up_part, down_part):
    flat_rows = inputs.reshape(-1, inputs.shape[-1])
    gate_out = jnp.dot(flat_rows, gate_part, preferred_element_type=jnp.float32)
    upward = jnp.dot(flat_rows, up_part, preferred_element_type=jnp.float32)
    hidden = (jax.nn.silu(gate_out) * upward).astype(jnp.bfloat16)
    partial_out = jnp.dot(hidden, down_part, preferred_element_type=jnp.float32).astype(
        jnp.bfloat16
    )
    return partial_out.reshape(inputs.shape)


def merge_softmax(earlier, later):
    left_peak, left_total, left_accum = earlier
    right_peak, right_total, right_accum = later
    new_peak = jnp.maximum(left_peak, right_peak)
    left_factor = jnp.exp(left_peak - new_peak)
    right_factor = jnp.exp(right_peak - new_peak)
    merged_total = left_total * left_factor + right_total * right_factor
    merged_accum = left_accum * left_factor[..., None] + right_accum * right_factor[..., None]
    return (new_peak, merged_total, merged_accum)


def exchange_kernel(n_req, total, x_ref, out_ref, send_sem, recv_sem, local_sem):
    me = lax.axis_index("ctx") * n_req + lax.axis_index("req")

    def device(d):
        return (d // n_req, d % n_req)

    def outgoing(d):
        return pltpu.make_async_remote_copy(
            src_ref=x_ref.at[d],
            dst_ref=out_ref.at[me],
            send_sem=send_sem.at[d],
            recv_sem=recv_sem.at[me],
            device_id=device(d),
            device_id_type=MESH,
        )

    def incoming(s):
        return pltpu.make_async_remote_copy(
            src_ref=x_ref.at[me],
            dst_ref=out_ref.at[s],
            send_sem=send_sem.at[s],
            recv_sem=recv_sem.at[s],
            device_id=device(s),
            device_id_type=MESH,
        )

    barrier = pltpu.get_barrier_semaphore()

    def greet(k, carry):
        d = lax.rem(me + k, total)
        pl.semaphore_signal(barrier, inc=1, device_id=device(d), device_id_type=MESH)
        return carry

    lax.fori_loop(1, total, greet, 0)
    pl.semaphore_wait(barrier, total - 1)
    local = pltpu.make_async_copy(x_ref.at[me], out_ref.at[me], local_sem)
    local.start()

    def send(k, carry):
        outgoing(lax.rem(me + k, total)).start()
        return carry

    lax.fori_loop(1, total, send, 0)

    def finish(k, carry):
        outgoing(lax.rem(me + k, total)).wait_send()
        incoming(lax.rem(me + total - k, total)).wait_recv()
        return carry

    lax.fori_loop(1, total, finish, 0)
    local.wait()


def exchange(x, n_req, total, collective_id):
    return pl.pallas_call(
        functools.partial(exchange_kernel, n_req, total),
        out_shape=jax.ShapeDtypeStruct(x.shape, x.dtype),
        in_specs=[pl.BlockSpec(memory_space=pl.ANY)],
        out_specs=pl.BlockSpec(memory_space=pl.ANY),
        scratch_shapes=[
            pltpu.SemaphoreType.DMA((total,)),
            pltpu.SemaphoreType.DMA((total,)),
            pltpu.SemaphoreType.DMA(()),
        ],
        compiler_params=pltpu.CompilerParams(collective_id=collective_id, has_side_effects=True),
    )(x)


def context_kernel(n_ctx, keys_ref, parts_ref, keys_out, parts_out, sems):
    me = lax.axis_index("ctx")
    row = lax.axis_index("req")
    barrier = pltpu.get_barrier_semaphore()
    for step in range(1, n_ctx):
        other = lax.rem(me + step, n_ctx)
        pl.semaphore_signal(barrier, inc=1, device_id=(other, row), device_id_type=MESH)
    pl.semaphore_wait(barrier, n_ctx - 1)

    def key_copy(source, target):
        return pltpu.make_async_remote_copy(
            src_ref=keys_ref,
            dst_ref=keys_out.at[source],
            send_sem=sems.at[0, target],
            recv_sem=sems.at[1, source],
            device_id=(target, row),
            device_id_type=MESH,
        )

    def part_copy(source, target):
        return pltpu.make_async_remote_copy(
            src_ref=parts_ref.at[target],
            dst_ref=parts_out.at[source],
            send_sem=sems.at[2, target],
            recv_sem=sems.at[3, source],
            device_id=(target, row),
            device_id_type=MESH,
        )

    own_keys = pltpu.make_async_copy(keys_ref, keys_out.at[me], sems.at[4, 0])
    own_parts = pltpu.make_async_copy(parts_ref.at[me], parts_out.at[me], sems.at[4, 1])
    own_keys.start()
    own_parts.start()
    for step in range(1, n_ctx):
        other = lax.rem(me + step, n_ctx)
        key_copy(me, other).start()
        part_copy(me, other).start()
    for step in range(1, n_ctx):
        other = lax.rem(me + step, n_ctx)
        source = lax.rem(me + n_ctx - step, n_ctx)
        key_copy(me, other).wait_send()
        part_copy(me, other).wait_send()
        key_copy(source, me).wait_recv()
        part_copy(source, me).wait_recv()
    own_keys.wait()
    own_parts.wait()


def context_exchange(keys, parts, n_ctx):
    return pl.pallas_call(
        functools.partial(context_kernel, n_ctx),
        out_shape=(
            jax.ShapeDtypeStruct((n_ctx,) + keys.shape, keys.dtype),
            jax.ShapeDtypeStruct(parts.shape, parts.dtype),
        ),
        in_specs=[pl.BlockSpec(memory_space=pl.ANY)] * 2,
        out_specs=(pl.BlockSpec(memory_space=pl.ANY), pl.BlockSpec(memory_space=pl.ANY)),
        scratch_shapes=[pltpu.SemaphoreType.DMA((5, n_ctx))],
        compiler_params=pltpu.CompilerParams(collective_id=2, has_side_effects=True),
    )(keys, parts)


def ffn_kernel(x_ref, gate_ref, up_ref, down_ref, out_ref):
    rows = x_ref[...]
    gate_out = jnp.dot(rows, gate_ref[...], preferred_element_type=jnp.float32)
    upward = jnp.dot(rows, up_ref[...], preferred_element_type=jnp.float32)
    hidden = (jax.nn.silu(gate_out) * upward).astype(jnp.bfloat16)
    out_ref[...] = jnp.dot(hidden, down_ref[...], preferred_element_type=jnp.float32).astype(
        out_ref.dtype
    )


def ffn_half(inputs, gate_part, up_part, down_part, tile=128):
    flat_rows = inputs.reshape(-1, inputs.shape[-1])
    rows, width = flat_rows.shape
    hidden = gate_part.shape[1]
    fixed = lambda i: (0, 0)
    out = pl.pallas_call(
        ffn_kernel,
        grid=(rows // tile,),
        in_specs=[
            pl.BlockSpec((tile, width), lambda i: (i, 0)),
            pl.BlockSpec((width, hidden), fixed),
            pl.BlockSpec((width, hidden), fixed),
            pl.BlockSpec((hidden, width), fixed),
        ],
        out_specs=pl.BlockSpec((tile, width), lambda i: (i, 0)),
        out_shape=jax.ShapeDtypeStruct((rows, width), jnp.bfloat16),
        compiler_params=pltpu.CompilerParams(vmem_limit_bytes=48 * 1024 * 1024),
        cost_estimate=pl.CostEstimate(
            flops=6 * rows * width * hidden,
            transcendentals=rows * hidden,
            bytes_accessed=2 * (2 * rows * width + 3 * width * hidden),
        ),
    )(flat_rows, gate_part, up_part, down_part)
    return out.reshape(inputs.shape)


def body(
    pre_latent,
    pre_qlat,
    pre_qrope,
    pre_resid,
    block_order,
    dec_new,
    dec_qlat,
    dec_qrope,
    dec_resid,
    cache_len,
    page_table,
    cache_pool,
    w_uv,
    w_out,
    norm_gain,
    router,
    routes,
    w_gate,
    w_up,
    w_down,
):
    ctx_count = lax.axis_size("ctx")
    ctx_index = lax.axis_index("ctx")
    score_scale = (DN + DR) ** (-0.5)
    latent = pre_latent[0]
    shard_rows = latent.shape[0]
    local_rows = jnp.arange(shard_rows)
    own_pos = block_position(block_order, ctx_index * shard_rows + local_rows, shard_rows)
    cos_table, sin_table = rope_tables(own_pos, DR)
    key_rope = rotate(latent[:, DC:], cos_table, sin_table).astype(jnp.bfloat16)
    stored = jnp.concatenate([latent[:, :DC], key_rope], axis=-1)
    rotated = rotate(pre_qrope[0], cos_table[:, None, :], sin_table[:, None, :]).astype(
        jnp.bfloat16
    )
    head_count = pre_qlat.shape[2]

    lengths = cache_len[:, 0]
    tables = page_table[:, 0, :]
    request_count = tables.shape[0]
    pages_dev = tables.shape[1]
    page_rows = cache_pool.shape[1]
    slot_count = cache_pool.shape[0]
    row_width = cache_pool.shape[2]
    cos_new, sin_new = rope_tables(lengths, DR)
    new_rope = rotate(dec_new[:, 0, DC:], cos_new, sin_new).astype(jnp.bfloat16)
    new_rows = jnp.concatenate([dec_new[:, 0, :DC], new_rope], axis=-1)
    page_index = lengths // page_rows
    owner_ctx = page_index // pages_dev
    page_hit = tables[:, :, None] == jnp.arange(slot_count)[None, None, :]
    wanted = jnp.arange(pages_dev)[None, :] == (page_index % pages_dev)[:, None]
    slot_of = jnp.sum(jnp.where(wanted, tables, 0), axis=1)
    target = jnp.where(
        owner_ctx == ctx_index, slot_of * page_rows + lengths % page_rows, slot_count * page_rows
    )
    row_ids = jnp.arange(slot_count * page_rows)[:, None]
    flat_pool = cache_pool.reshape(slot_count * page_rows, row_width)
    for request in range(request_count):
        flat_pool = jnp.where(row_ids == target[request], new_rows[request][None, :], flat_pool)
    page_valid = jnp.any(page_hit, axis=1)
    page_logical = jnp.sum(page_hit.astype(jnp.int32) * jnp.arange(pages_dev)[None, :, None], axis=1)
    page_start = (ctx_index * pages_dev + page_logical) * page_rows
    key_pos = (page_start[:, :, None] + jnp.arange(page_rows)[None, None, :]).reshape(
        request_count, slot_count * page_rows
    )
    dec_visible = (
        jnp.repeat(page_valid, page_rows, axis=1) & (key_pos <= lengths[:, None])
    )[:, None, :]
    query_rot = rotate(dec_qrope[:, 0], cos_new[:, None, :], sin_new[:, None, :]).astype(
        jnp.bfloat16
    )
    dec_queries = jnp.concatenate([dec_qlat[:, 0], query_rot], axis=-1)
    flat_queries = dec_queries.reshape(request_count * head_count, row_width)
    dec_scores = (
        jnp.dot(flat_pool, flat_queries.T, preferred_element_type=jnp.float32) * score_scale
    ).reshape(slot_count * page_rows, request_count, head_count)
    dec_seen = jnp.transpose(dec_visible[:, 0, :])[:, :, None]
    dec_masked = jnp.where(dec_seen, dec_scores, NEG_FILL)
    local_peak = jnp.max(dec_masked, axis=0)
    dec_weights = jnp.where(dec_seen, jnp.exp(dec_masked - local_peak[None]), 0.0)
    local_total = jnp.sum(dec_weights, axis=0)
    local_accum = lax.dot_general(
        dec_weights.astype(jnp.bfloat16).reshape(slot_count * page_rows, -1),
        flat_pool[:, :DC],
        (((0,), (0,)), ((), ())),
        preferred_element_type=jnp.float32,
    ).reshape(request_count, head_count, DC)

    dec_share = request_count // ctx_count
    part_width = 128 * ((DC + 2 + 127) // 128)
    dec_block = jnp.concatenate(
        [
            local_accum,
            local_peak[..., None],
            local_total[..., None],
            jnp.zeros((request_count, head_count, part_width - DC - 2), jnp.float32),
        ],
        axis=2,
    ).reshape(ctx_count, dec_share * head_count, part_width)
    keys_all, own_parts = context_exchange(stored, dec_block, ctx_count)
    moving = keys_all.reshape(ctx_count * shard_rows, row_width)
    own_parts = own_parts.reshape(ctx_count, dec_share, head_count, part_width)
    part_accum = own_parts[..., :DC]
    part_peak = own_parts[..., DC]
    part_total = own_parts[..., DC + 1]
    merged_peak = jnp.max(part_peak, axis=0)
    factor = jnp.exp(part_peak - merged_peak[None])
    merged_total = jnp.sum(part_total * factor, axis=0)
    merged_accum = jnp.sum(part_accum * factor[..., None], axis=0)
    own_mixed = (merged_accum / merged_total[..., None]).astype(jnp.bfloat16)

    key_pos_pre = block_position(block_order, jnp.arange(moving.shape[0]), shard_rows)
    query_rows = shard_rows * head_count
    scores = (
        jnp.dot(
            pre_qlat[0].reshape(query_rows, DC), moving[:, :DC].T,
            preferred_element_type=jnp.float32,
        )
        + jnp.dot(
            rotated.reshape(query_rows, DR), moving[:, DC:].T,
            preferred_element_type=jnp.float32,
        )
    ) * score_scale
    visible = jnp.repeat(key_pos_pre[None, :] <= own_pos[:, None], head_count, axis=0)
    masked = jnp.where(visible, scores, NEG_FILL)
    new_peak = jnp.max(masked, axis=-1)
    weights = jnp.where(visible, jnp.exp(masked - new_peak[..., None]), 0.0)
    totals = jnp.sum(weights, axis=-1)
    accumulated = jnp.dot(
        weights.astype(jnp.bfloat16), moving[:, :DC], preferred_element_type=jnp.float32
    )
    pre_mixed = (accumulated / totals[:, None]).astype(jnp.bfloat16).reshape(
        shard_rows, head_count, DC
    )

    own_resid = lax.dynamic_slice_in_dim(dec_resid[:, 0], ctx_index * dec_share, dec_share, 0)
    mixed_all = jnp.concatenate([pre_mixed, own_mixed], axis=0)
    resid_all = jnp.concatenate([pre_resid[0], own_resid], axis=0)
    values = jnp.einsum("nhc,hcv->nhv", mixed_all, w_uv, preferred_element_type=jnp.float32).astype(
        jnp.bfloat16
    )
    hidden_state = resid_all.astype(jnp.float32) + jnp.dot(
        values.reshape(values.shape[0], -1), w_out, preferred_element_type=jnp.float32
    )
    normed = (
        hidden_state
        * lax.rsqrt(jnp.mean(hidden_state * hidden_state, axis=-1, keepdims=True) + EPSILON)
        * norm_gain
    ).astype(jnp.bfloat16)
    logits = jnp.dot(normed.astype(jnp.float32), router, precision=lax.Precision.HIGHEST)
    probable = jax.nn.sigmoid(logits)
    row_count = normed.shape[0]
    width = normed.shape[1]
    top_count = routes.shape[1]
    expert_count = router.shape[1]
    devices = ctx_count * lax.axis_size("req")
    capacity = 2 * ((row_count * top_count + 2 * expert_count - 1) // (2 * expert_count))
    route_hit = routes[:, :, None] == jnp.arange(expert_count)[None, None, :]
    chosen = jnp.sum(jnp.where(route_hit, probable[:, None, :], 0.0), axis=-1)
    mixing = ROUTE_SCALE * chosen / jnp.sum(chosen, axis=1, keepdims=True)
    expert_hits = route_hit.astype(jnp.int32).sum(1)
    earlier = (jnp.arange(row_count)[None, :] < jnp.arange(row_count)[:, None]).astype(jnp.bfloat16)
    before = jnp.dot(
        earlier, expert_hits.astype(jnp.bfloat16), preferred_element_type=jnp.float32
    ).astype(jnp.int32)
    slot_index = jnp.sum(jnp.where(route_hit, before[:, None, :], 0), axis=-1)
    target_slot = routes * capacity + slot_index
    slot_hit = target_slot[:, :, None] == jnp.arange(expert_count * capacity)[None, None, :]
    dispatch = jnp.any(slot_hit, axis=1).astype(jnp.bfloat16)
    outgoing = lax.dot_general(
        dispatch, normed, (((0,), (0,)), ((), ())), preferred_element_type=jnp.float32
    ).astype(jnp.bfloat16).reshape(expert_count, capacity, width)
    doubled = jnp.broadcast_to(outgoing[:, None], (expert_count, 2, capacity, width)).reshape(
        devices, capacity, width
    )
    partial_out = ffn_half(
        lax.all_to_all(doubled, ("ctx", "req"), split_axis=0, concat_axis=0, tiled=True),
        w_gate[0],
        w_up[0],
        w_down[0],
    )
    returned = lax.all_to_all(
        partial_out, ("ctx", "req"), split_axis=0, concat_axis=0, tiled=True
    ).reshape(expert_count, 2, capacity, width)
    results = (returned[:, 0].astype(jnp.float32) + returned[:, 1].astype(jnp.float32)).astype(
        jnp.bfloat16
    ).reshape(expert_count * capacity, width)
    combine = jnp.sum(jnp.where(slot_hit, mixing[:, :, None], 0.0), axis=1)
    moe = jnp.dot(combine, results.astype(jnp.float32), precision=lax.Precision.HIGHEST)
    final = (hidden_state + moe).astype(jnp.bfloat16)
    pre_out = final[:shard_rows][None]
    dec_out = final[shard_rows:][:, None]
    cache_out = flat_pool.reshape(cache_pool.shape)
    return (pre_out, dec_out, cache_out)


def solution(mesh):
    in_specs = (
        P("req", "ctx", None),
        P("req", "ctx", None, None),
        P("req", "ctx", None, None),
        P("req", "ctx", None),
        P(),
        P(None, "req", None),
        P(None, "req", None, None),
        P(None, "req", None, None),
        P(None, "req", None),
        P(None, "req"),
        P(None, "req", "ctx"),
        P(("ctx", "req"), None, None),
        P(),
        P(),
        P(),
        P(),
        P(("ctx", "req"), None),
        P(("ctx", "req"), None, None),
        P(("ctx", "req"), None, None),
        P(("ctx", "req"), None, None),
    )
    out_specs = (P("req", "ctx", None), P("ctx", "req", None), P(("ctx", "req"), None, None))
    return jax.shard_map(body, mesh=mesh, in_specs=in_specs, out_specs=out_specs, check_vma=False)
```

```python
import functools

import jax
import jax.numpy as jnp
from jax import lax
from jax.experimental import pallas as pl
from jax.experimental.pallas import tpu as pltpu
from jax.sharding import PartitionSpec as P

MESH = pl.DeviceIdType.MESH

DC = 512
DR = 64
DN = 128


THETA = 50000.0
ROUTE_SCALE = 2.446
EPSILON = 1e-06
NEG_FILL = -1e30


def joined(part, axis, combine):
    gathered = jax.tree.map(lambda a: lax.all_gather(a, axis), part)

    def take(source):
        return jax.tree.map(lambda a: lax.dynamic_index_in_dim(a, source, 0, False), gathered)

    return lax.fori_loop(
        1, lax.axis_size(axis), lambda source, state: combine(state, take(source)), take(0)
    )


def rope_tables(positions, rope_width):
    halfway = rope_width // 2
    inverse = THETA ** (-(jnp.arange(halfway).astype(jnp.float32) * 2.0) / rope_width)
    angles = positions.astype(jnp.float32)[..., None] * inverse
    return (jnp.cos(angles), jnp.sin(angles))


def rotate(values, cos_table, sin_table):
    halfway = values.shape[-1] // 2
    leading = values[..., :halfway].astype(jnp.float32)
    trailing = values[..., halfway:].astype(jnp.float32)
    return jnp.concatenate(
        [leading * cos_table - trailing * sin_table, trailing * cos_table + leading * sin_table],
        axis=-1,
    )


def block_position(block_order, global_rows, shard_rows):
    half_rows = shard_rows // 2
    block = global_rows // half_rows
    hit = block[:, None] == jnp.arange(block_order.shape[0])[None, :]
    logical = jnp.sum(jnp.where(hit, block_order[None, :], 0), axis=1)
    return logical * half_rows + global_rows % half_rows


def expert_half(inputs, gate_part, up_part, down_part):
    flat_rows = inputs.reshape(-1, inputs.shape[-1])
    gate_out = jnp.dot(flat_rows, gate_part, preferred_element_type=jnp.float32)
    upward = jnp.dot(flat_rows, up_part, preferred_element_type=jnp.float32)
    hidden = (jax.nn.silu(gate_out) * upward).astype(jnp.bfloat16)
    partial_out = jnp.dot(hidden, down_part, preferred_element_type=jnp.float32).astype(
        jnp.bfloat16
    )
    return partial_out.reshape(inputs.shape)


def merge_softmax(earlier, later):
    left_peak, left_total, left_accum = earlier
    right_peak, right_total, right_accum = later
    new_peak = jnp.maximum(left_peak, right_peak)
    left_factor = jnp.exp(left_peak - new_peak)
    right_factor = jnp.exp(right_peak - new_peak)
    merged_total = left_total * left_factor + right_total * right_factor
    merged_accum = left_accum * left_factor[..., None] + right_accum * right_factor[..., None]
    return (new_peak, merged_total, merged_accum)


def exchange_kernel(n_req, total, x_ref, out_ref, send_sem, recv_sem, local_sem):
    me = lax.axis_index("ctx") * n_req + lax.axis_index("req")

    def device(d):
        return (d // n_req, d % n_req)

    def outgoing(d):
        return pltpu.make_async_remote_copy(
            src_ref=x_ref.at[d],
            dst_ref=out_ref.at[me],
            send_sem=send_sem.at[d],
            recv_sem=recv_sem.at[me],
            device_id=device(d),
            device_id_type=MESH,
        )

    def incoming(s):
        return pltpu.make_async_remote_copy(
            src_ref=x_ref.at[me],
            dst_ref=out_ref.at[s],
            send_sem=send_sem.at[s],
            recv_sem=recv_sem.at[s],
            device_id=device(s),
            device_id_type=MESH,
        )

    barrier = pltpu.get_barrier_semaphore()

    def greet(k, carry):
        d = lax.rem(me + k, total)
        pl.semaphore_signal(barrier, inc=1, device_id=device(d), device_id_type=MESH)
        return carry

    lax.fori_loop(1, total, greet, 0)
    pl.semaphore_wait(barrier, total - 1)
    local = pltpu.make_async_copy(x_ref.at[me], out_ref.at[me], local_sem)
    local.start()

    def send(k, carry):
        outgoing(lax.rem(me + k, total)).start()
        return carry

    lax.fori_loop(1, total, send, 0)

    def finish(k, carry):
        outgoing(lax.rem(me + k, total)).wait_send()
        incoming(lax.rem(me + total - k, total)).wait_recv()
        return carry

    lax.fori_loop(1, total, finish, 0)
    local.wait()


def exchange(x, n_req, total, collective_id):
    return pl.pallas_call(
        functools.partial(exchange_kernel, n_req, total),
        out_shape=jax.ShapeDtypeStruct(x.shape, x.dtype),
        in_specs=[pl.BlockSpec(memory_space=pl.ANY)],
        out_specs=pl.BlockSpec(memory_space=pl.ANY),
        scratch_shapes=[
            pltpu.SemaphoreType.DMA((total,)),
            pltpu.SemaphoreType.DMA((total,)),
            pltpu.SemaphoreType.DMA(()),
        ],
        compiler_params=pltpu.CompilerParams(collective_id=collective_id, has_side_effects=True),
    )(x)


def context_kernel(n_ctx, keys_ref, parts_ref, keys_out, parts_out, sems):
    me = lax.axis_index("ctx")
    row = lax.axis_index("req")
    barrier = pltpu.get_barrier_semaphore()
    for step in range(1, n_ctx):
        other = lax.rem(me + step, n_ctx)
        pl.semaphore_signal(barrier, inc=1, device_id=(other, row), device_id_type=MESH)
    pl.semaphore_wait(barrier, n_ctx - 1)

    def key_copy(source, target):
        return pltpu.make_async_remote_copy(
            src_ref=keys_ref,
            dst_ref=keys_out.at[source],
            send_sem=sems.at[0, target],
            recv_sem=sems.at[1, source],
            device_id=(target, row),
            device_id_type=MESH,
        )

    def part_copy(source, target):
        return pltpu.make_async_remote_copy(
            src_ref=parts_ref.at[target],
            dst_ref=parts_out.at[source],
            send_sem=sems.at[2, target],
            recv_sem=sems.at[3, source],
            device_id=(target, row),
            device_id_type=MESH,
        )

    own_keys = pltpu.make_async_copy(keys_ref, keys_out.at[me], sems.at[4, 0])
    own_parts = pltpu.make_async_copy(parts_ref.at[me], parts_out.at[me], sems.at[4, 1])
    own_keys.start()
    own_parts.start()
    for step in range(1, n_ctx):
        other = lax.rem(me + step, n_ctx)
        key_copy(me, other).start()
        part_copy(me, other).start()
    for step in range(1, n_ctx):
        other = lax.rem(me + step, n_ctx)
        source = lax.rem(me + n_ctx - step, n_ctx)
        key_copy(me, other).wait_send()
        part_copy(me, other).wait_send()
        key_copy(source, me).wait_recv()
        part_copy(source, me).wait_recv()
    own_keys.wait()
    own_parts.wait()


def context_exchange(keys, parts, n_ctx):
    return pl.pallas_call(
        functools.partial(context_kernel, n_ctx),
        out_shape=(
            jax.ShapeDtypeStruct((n_ctx,) + keys.shape, keys.dtype),
            jax.ShapeDtypeStruct(parts.shape, parts.dtype),
        ),
        in_specs=[pl.BlockSpec(memory_space=pl.ANY)] * 2,
        out_specs=(pl.BlockSpec(memory_space=pl.ANY), pl.BlockSpec(memory_space=pl.ANY)),
        scratch_shapes=[pltpu.SemaphoreType.DMA((5, n_ctx))],
        compiler_params=pltpu.CompilerParams(collective_id=2, has_side_effects=True),
    )(keys, parts)


def ffn_kernel(x_ref, gate_ref, up_ref, down_ref, out_ref):
    rows = x_ref[...]
    by_width = (((1,), (1,)), ((), ()))
    gate_out = lax.dot_general(rows, gate_ref[...], by_width, preferred_element_type=jnp.float32)
    upward = lax.dot_general(rows, up_ref[...], by_width, preferred_element_type=jnp.float32)
    hidden = (jax.nn.silu(gate_out) * upward).astype(jnp.bfloat16)
    out_ref[...] = jnp.dot(hidden, down_ref[...], preferred_element_type=jnp.float32).astype(
        out_ref.dtype
    )


def ffn_half(inputs, gate_part, up_part, down_part, tile=128):
    flat_rows = inputs.reshape(-1, inputs.shape[-1])
    rows, width = flat_rows.shape
    hidden = gate_part.shape[1]
    fixed = lambda i: (0, 0)
    out = pl.pallas_call(
        ffn_kernel,
        grid=(rows // tile,),
        in_specs=[
            pl.BlockSpec((tile, width), lambda i: (i, 0)),
            pl.BlockSpec((hidden, width), fixed),
            pl.BlockSpec((hidden, width), fixed),
            pl.BlockSpec((hidden, width), fixed),
        ],
        out_specs=pl.BlockSpec((tile, width), lambda i: (i, 0)),
        out_shape=jax.ShapeDtypeStruct((rows, width), jnp.bfloat16),
        compiler_params=pltpu.CompilerParams(vmem_limit_bytes=48 * 1024 * 1024),
        cost_estimate=pl.CostEstimate(
            flops=6 * rows * width * hidden,
            transcendentals=rows * hidden,
            bytes_accessed=2 * (2 * rows * width + 3 * width * hidden),
        ),
    )(flat_rows, jnp.swapaxes(gate_part, 0, 1), jnp.swapaxes(up_part, 0, 1), down_part)
    return out.reshape(inputs.shape)


def body(
    pre_latent,
    pre_qlat,
    pre_qrope,
    pre_resid,
    block_order,
    dec_new,
    dec_qlat,
    dec_qrope,
    dec_resid,
    cache_len,
    page_table,
    cache_pool,
    w_uv,
    w_out,
    norm_gain,
    router,
    routes,
    w_gate,
    w_up,
    w_down,
):
    ctx_count = lax.axis_size("ctx")
    ctx_index = lax.axis_index("ctx")
    score_scale = (DN + DR) ** (-0.5)
    latent = pre_latent[0]
    shard_rows = latent.shape[0]
    local_rows = jnp.arange(shard_rows)
    own_pos = block_position(block_order, ctx_index * shard_rows + local_rows, shard_rows)
    cos_table, sin_table = rope_tables(own_pos, DR)
    key_rope = rotate(latent[:, DC:], cos_table, sin_table).astype(jnp.bfloat16)
    stored = jnp.concatenate([latent[:, :DC], key_rope], axis=-1)
    rotated = rotate(pre_qrope[0], cos_table[:, None, :], sin_table[:, None, :]).astype(
        jnp.bfloat16
    )
    head_count = pre_qlat.shape[2]

    lengths = cache_len[:, 0]
    tables = page_table[:, 0, :]
    request_count = tables.shape[0]
    pages_dev = tables.shape[1]
    page_rows = cache_pool.shape[1]
    slot_count = cache_pool.shape[0]
    row_width = cache_pool.shape[2]
    cos_new, sin_new = rope_tables(lengths, DR)
    new_rope = rotate(dec_new[:, 0, DC:], cos_new, sin_new).astype(jnp.bfloat16)
    new_rows = jnp.concatenate([dec_new[:, 0, :DC], new_rope], axis=-1)
    page_index = lengths // page_rows
    owner_ctx = page_index // pages_dev
    page_hit = tables[:, :, None] == jnp.arange(slot_count)[None, None, :]
    wanted = jnp.arange(pages_dev)[None, :] == (page_index % pages_dev)[:, None]
    slot_of = jnp.sum(jnp.where(wanted, tables, 0), axis=1)
    target = jnp.where(
        owner_ctx == ctx_index, slot_of * page_rows + lengths % page_rows, slot_count * page_rows
    )
    row_ids = jnp.arange(slot_count * page_rows)[:, None]
    flat_pool = cache_pool.reshape(slot_count * page_rows, row_width)
    for request in range(request_count):
        flat_pool = jnp.where(row_ids == target[request], new_rows[request][None, :], flat_pool)
    page_valid = jnp.any(page_hit, axis=1)
    page_logical = jnp.sum(page_hit.astype(jnp.int32) * jnp.arange(pages_dev)[None, :, None], axis=1)
    page_start = (ctx_index * pages_dev + page_logical) * page_rows
    key_pos = (page_start[:, :, None] + jnp.arange(page_rows)[None, None, :]).reshape(
        request_count, slot_count * page_rows
    )
    dec_visible = (
        jnp.repeat(page_valid, page_rows, axis=1) & (key_pos <= lengths[:, None])
    )[:, None, :]
    query_rot = rotate(dec_qrope[:, 0], cos_new[:, None, :], sin_new[:, None, :]).astype(
        jnp.bfloat16
    )
    dec_queries = jnp.concatenate([dec_qlat[:, 0], query_rot], axis=-1)
    flat_queries = dec_queries.reshape(request_count * head_count, row_width)
    dec_scores = (
        jnp.dot(flat_pool, flat_queries.T, preferred_element_type=jnp.float32) * score_scale
    ).reshape(slot_count * page_rows, request_count, head_count)
    dec_seen = jnp.transpose(dec_visible[:, 0, :])[:, :, None]
    dec_masked = jnp.where(dec_seen, dec_scores, NEG_FILL)
    local_peak = jnp.max(dec_masked, axis=0)
    dec_weights = jnp.where(dec_seen, jnp.exp(dec_masked - local_peak[None]), 0.0)
    local_total = jnp.sum(dec_weights, axis=0)
    local_accum = lax.dot_general(
        dec_weights.astype(jnp.bfloat16).reshape(slot_count * page_rows, -1),
        flat_pool[:, :DC],
        (((0,), (0,)), ((), ())),
        preferred_element_type=jnp.float32,
    ).reshape(request_count, head_count, DC)

    dec_share = request_count // ctx_count
    part_width = 128 * ((DC + 2 + 127) // 128)
    dec_block = jnp.concatenate(
        [
            local_accum,
            local_peak[..., None],
            local_total[..., None],
            jnp.zeros((request_count, head_count, part_width - DC - 2), jnp.float32),
        ],
        axis=2,
    ).reshape(ctx_count, dec_share * head_count, part_width)
    keys_all, own_parts = context_exchange(stored, dec_block, ctx_count)
    moving = keys_all.reshape(ctx_count * shard_rows, row_width)
    own_parts = own_parts.reshape(ctx_count, dec_share, head_count, part_width)
    part_accum = own_parts[..., :DC]
    part_peak = own_parts[..., DC]
    part_total = own_parts[..., DC + 1]
    merged_peak = jnp.max(part_peak, axis=0)
    factor = jnp.exp(part_peak - merged_peak[None])
    merged_total = jnp.sum(part_total * factor, axis=0)
    merged_accum = jnp.sum(part_accum * factor[..., None], axis=0)
    own_mixed = (merged_accum / merged_total[..., None]).astype(jnp.bfloat16)

    key_pos_pre = block_position(block_order, jnp.arange(moving.shape[0]), shard_rows)
    query_rows = shard_rows * head_count
    scores = (
        jnp.dot(
            pre_qlat[0].reshape(query_rows, DC), moving[:, :DC].T,
            preferred_element_type=jnp.float32,
        )
        + jnp.dot(
            rotated.reshape(query_rows, DR), moving[:, DC:].T,
            preferred_element_type=jnp.float32,
        )
    ) * score_scale
    visible = jnp.repeat(key_pos_pre[None, :] <= own_pos[:, None], head_count, axis=0)
    masked = jnp.where(visible, scores, NEG_FILL)
    new_peak = jnp.max(masked, axis=-1)
    weights = jnp.where(visible, jnp.exp(masked - new_peak[..., None]), 0.0)
    totals = jnp.sum(weights, axis=-1)
    accumulated = jnp.dot(
        weights.astype(jnp.bfloat16), moving[:, :DC], preferred_element_type=jnp.float32
    )
    pre_mixed = (accumulated / totals[:, None]).astype(jnp.bfloat16).reshape(
        shard_rows, head_count, DC
    )

    own_resid = lax.dynamic_slice_in_dim(dec_resid[:, 0], ctx_index * dec_share, dec_share, 0)
    mixed_all = jnp.concatenate([pre_mixed, own_mixed], axis=0)
    resid_all = jnp.concatenate([pre_resid[0], own_resid], axis=0)
    values = jnp.einsum("nhc,hcv->nhv", mixed_all, w_uv, preferred_element_type=jnp.float32).astype(
        jnp.bfloat16
    )
    hidden_state = resid_all.astype(jnp.float32) + jnp.dot(
        values.reshape(values.shape[0], -1), w_out, preferred_element_type=jnp.float32
    )
    normed = (
        hidden_state
        * lax.rsqrt(jnp.mean(hidden_state * hidden_state, axis=-1, keepdims=True) + EPSILON)
        * norm_gain
    ).astype(jnp.bfloat16)
    logits = jnp.dot(normed.astype(jnp.float32), router, precision=lax.Precision.HIGHEST)
    probable = jax.nn.sigmoid(logits)
    row_count = normed.shape[0]
    width = normed.shape[1]
    top_count = routes.shape[1]
    expert_count = router.shape[1]
    devices = ctx_count * lax.axis_size("req")
    capacity = 2 * ((row_count * top_count + 2 * expert_count - 1) // (2 * expert_count))
    route_hit = routes[:, :, None] == jnp.arange(expert_count)[None, None, :]
    chosen = jnp.sum(jnp.where(route_hit, probable[:, None, :], 0.0), axis=-1)
    mixing = ROUTE_SCALE * chosen / jnp.sum(chosen, axis=1, keepdims=True)
    expert_hits = route_hit.astype(jnp.int32).sum(1)
    earlier = (jnp.arange(row_count)[None, :] < jnp.arange(row_count)[:, None]).astype(jnp.bfloat16)
    before = jnp.dot(
        earlier, expert_hits.astype(jnp.bfloat16), preferred_element_type=jnp.float32
    ).astype(jnp.int32)
    slot_index = jnp.sum(jnp.where(route_hit, before[:, None, :], 0), axis=-1)
    target_slot = routes * capacity + slot_index
    slot_hit = target_slot[:, :, None] == jnp.arange(expert_count * capacity)[None, None, :]
    dispatch = jnp.any(slot_hit, axis=1).astype(jnp.bfloat16)
    outgoing = lax.dot_general(
        dispatch, normed, (((0,), (0,)), ((), ())), preferred_element_type=jnp.float32
    ).astype(jnp.bfloat16).reshape(expert_count, capacity, width)
    doubled = jnp.broadcast_to(outgoing[:, None], (expert_count, 2, capacity, width)).reshape(
        devices, capacity, width
    )
    partial_out = ffn_half(
        lax.all_to_all(doubled, ("ctx", "req"), split_axis=0, concat_axis=0, tiled=True),
        w_gate[0],
        w_up[0],
        w_down[0],
    )
    returned = lax.all_to_all(
        partial_out, ("ctx", "req"), split_axis=0, concat_axis=0, tiled=True
    ).reshape(expert_count, 2, capacity, width)
    results = (returned[:, 0].astype(jnp.float32) + returned[:, 1].astype(jnp.float32)).astype(
        jnp.bfloat16
    ).reshape(expert_count * capacity, width)
    combine = jnp.sum(jnp.where(slot_hit, mixing[:, :, None], 0.0), axis=1)
    moe = jnp.dot(combine, results.astype(jnp.float32), precision=lax.Precision.HIGHEST)
    final = (hidden_state + moe).astype(jnp.bfloat16)
    pre_out = final[:shard_rows][None]
    dec_out = final[shard_rows:][:, None]
    cache_out = flat_pool.reshape(cache_pool.shape)
    return (pre_out, dec_out, cache_out)


def solution(mesh):
    in_specs = (
        P("req", "ctx", None),
        P("req", "ctx", None, None),
        P("req", "ctx", None, None),
        P("req", "ctx", None),
        P(),
        P(None, "req", None),
        P(None, "req", None, None),
        P(None, "req", None, None),
        P(None, "req", None),
        P(None, "req"),
        P(None, "req", "ctx"),
        P(("ctx", "req"), None, None),
        P(),
        P(),
        P(),
        P(),
        P(("ctx", "req"), None),
        P(("ctx", "req"), None, None),
        P(("ctx", "req"), None, None),
        P(("ctx", "req"), None, None),
    )
    out_specs = (P("req", "ctx", None), P("ctx", "req", None), P(("ctx", "req"), None, None))
    return jax.shard_map(body, mesh=mesh, in_specs=in_specs, out_specs=out_specs, check_vma=False)
```

```python
import functools

import jax
import jax.numpy as jnp
from jax import lax
from jax.experimental import pallas as pl
from jax.experimental.pallas import tpu as pltpu
from jax.sharding import PartitionSpec as P

MESH = pl.DeviceIdType.MESH

DC = 512
DR = 64
DN = 128


THETA = 50000.0
ROUTE_SCALE = 2.446
EPSILON = 1e-06
NEG_FILL = -1e30


def joined(part, axis, combine):
    gathered = jax.tree.map(lambda a: lax.all_gather(a, axis), part)

    def take(source):
        return jax.tree.map(lambda a: lax.dynamic_index_in_dim(a, source, 0, False), gathered)

    return lax.fori_loop(
        1, lax.axis_size(axis), lambda source, state: combine(state, take(source)), take(0)
    )


def rope_tables(positions, rope_width):
    halfway = rope_width // 2
    inverse = THETA ** (-(jnp.arange(halfway).astype(jnp.float32) * 2.0) / rope_width)
    angles = positions.astype(jnp.float32)[..., None] * inverse
    return (jnp.cos(angles), jnp.sin(angles))


def rotate(values, cos_table, sin_table):
    halfway = values.shape[-1] // 2
    leading = values[..., :halfway].astype(jnp.float32)
    trailing = values[..., halfway:].astype(jnp.float32)
    return jnp.concatenate(
        [leading * cos_table - trailing * sin_table, trailing * cos_table + leading * sin_table],
        axis=-1,
    )


def block_position(block_order, global_rows, shard_rows):
    half_rows = shard_rows // 2
    block = global_rows // half_rows
    hit = block[:, None] == jnp.arange(block_order.shape[0])[None, :]
    logical = jnp.sum(jnp.where(hit, block_order[None, :], 0), axis=1)
    return logical * half_rows + global_rows % half_rows


def expert_half(inputs, gate_part, up_part, down_part):
    flat_rows = inputs.reshape(-1, inputs.shape[-1])
    gate_out = jnp.dot(flat_rows, gate_part, preferred_element_type=jnp.float32)
    upward = jnp.dot(flat_rows, up_part, preferred_element_type=jnp.float32)
    hidden = (jax.nn.silu(gate_out) * upward).astype(jnp.bfloat16)
    partial_out = jnp.dot(hidden, down_part, preferred_element_type=jnp.float32).astype(
        jnp.bfloat16
    )
    return partial_out.reshape(inputs.shape)


def merge_softmax(earlier, later):
    left_peak, left_total, left_accum = earlier
    right_peak, right_total, right_accum = later
    new_peak = jnp.maximum(left_peak, right_peak)
    left_factor = jnp.exp(left_peak - new_peak)
    right_factor = jnp.exp(right_peak - new_peak)
    merged_total = left_total * left_factor + right_total * right_factor
    merged_accum = left_accum * left_factor[..., None] + right_accum * right_factor[..., None]
    return (new_peak, merged_total, merged_accum)


def exchange_kernel(n_req, total, x_ref, out_ref, send_sem, recv_sem, local_sem):
    me = lax.axis_index("ctx") * n_req + lax.axis_index("req")

    def device(d):
        return (d // n_req, d % n_req)

    def outgoing(d):
        return pltpu.make_async_remote_copy(
            src_ref=x_ref.at[d],
            dst_ref=out_ref.at[me],
            send_sem=send_sem.at[d],
            recv_sem=recv_sem.at[me],
            device_id=device(d),
            device_id_type=MESH,
        )

    def incoming(s):
        return pltpu.make_async_remote_copy(
            src_ref=x_ref.at[me],
            dst_ref=out_ref.at[s],
            send_sem=send_sem.at[s],
            recv_sem=recv_sem.at[s],
            device_id=device(s),
            device_id_type=MESH,
        )

    barrier = pltpu.get_barrier_semaphore()

    def greet(k, carry):
        d = lax.rem(me + k, total)
        pl.semaphore_signal(barrier, inc=1, device_id=device(d), device_id_type=MESH)
        return carry

    lax.fori_loop(1, total, greet, 0)
    pl.semaphore_wait(barrier, total - 1)
    local = pltpu.make_async_copy(x_ref.at[me], out_ref.at[me], local_sem)
    local.start()

    def send(k, carry):
        outgoing(lax.rem(me + k, total)).start()
        return carry

    lax.fori_loop(1, total, send, 0)

    def finish(k, carry):
        outgoing(lax.rem(me + k, total)).wait_send()
        incoming(lax.rem(me + total - k, total)).wait_recv()
        return carry

    lax.fori_loop(1, total, finish, 0)
    local.wait()


def exchange(x, n_req, total, collective_id):
    return pl.pallas_call(
        functools.partial(exchange_kernel, n_req, total),
        out_shape=jax.ShapeDtypeStruct(x.shape, x.dtype),
        in_specs=[pl.BlockSpec(memory_space=pl.ANY)],
        out_specs=pl.BlockSpec(memory_space=pl.ANY),
        scratch_shapes=[
            pltpu.SemaphoreType.DMA((total,)),
            pltpu.SemaphoreType.DMA((total,)),
            pltpu.SemaphoreType.DMA(()),
        ],
        compiler_params=pltpu.CompilerParams(collective_id=collective_id, has_side_effects=True),
    )(x)


def context_kernel(n_ctx, keys_ref, parts_ref, keys_out, parts_out, sems):
    me = lax.axis_index("ctx")
    row = lax.axis_index("req")
    barrier = pltpu.get_barrier_semaphore()
    for step in range(1, n_ctx):
        other = lax.rem(me + step, n_ctx)
        pl.semaphore_signal(barrier, inc=1, device_id=(other, row), device_id_type=MESH)
    pl.semaphore_wait(barrier, n_ctx - 1)

    def key_copy(source, target):
        return pltpu.make_async_remote_copy(
            src_ref=keys_ref,
            dst_ref=keys_out.at[source],
            send_sem=sems.at[0, target],
            recv_sem=sems.at[1, source],
            device_id=(target, row),
            device_id_type=MESH,
        )

    def part_copy(source, target):
        return pltpu.make_async_remote_copy(
            src_ref=parts_ref.at[target],
            dst_ref=parts_out.at[source],
            send_sem=sems.at[2, target],
            recv_sem=sems.at[3, source],
            device_id=(target, row),
            device_id_type=MESH,
        )

    own_keys = pltpu.make_async_copy(keys_ref, keys_out.at[me], sems.at[4, 0])
    own_parts = pltpu.make_async_copy(parts_ref.at[me], parts_out.at[me], sems.at[4, 1])
    own_keys.start()
    own_parts.start()
    for step in range(1, n_ctx):
        other = lax.rem(me + step, n_ctx)
        key_copy(me, other).start()
        part_copy(me, other).start()
    for step in range(1, n_ctx):
        other = lax.rem(me + step, n_ctx)
        source = lax.rem(me + n_ctx - step, n_ctx)
        key_copy(me, other).wait_send()
        part_copy(me, other).wait_send()
        key_copy(source, me).wait_recv()
        part_copy(source, me).wait_recv()
    own_keys.wait()
    own_parts.wait()


def context_exchange(keys, parts, n_ctx):
    return pl.pallas_call(
        functools.partial(context_kernel, n_ctx),
        out_shape=(
            jax.ShapeDtypeStruct((n_ctx,) + keys.shape, keys.dtype),
            jax.ShapeDtypeStruct(parts.shape, parts.dtype),
        ),
        in_specs=[pl.BlockSpec(memory_space=pl.ANY)] * 2,
        out_specs=(pl.BlockSpec(memory_space=pl.ANY), pl.BlockSpec(memory_space=pl.ANY)),
        scratch_shapes=[pltpu.SemaphoreType.DMA((5, n_ctx))],
        compiler_params=pltpu.CompilerParams(collective_id=2, has_side_effects=True),
    )(keys, parts)


def ffn_kernel(x_ref, gate_ref, up_ref, down_ref, out_ref):
    rows = x_ref[...]
    gate_out = jnp.dot(rows, gate_ref[...], preferred_element_type=jnp.float32)
    upward = jnp.dot(rows, up_ref[...], preferred_element_type=jnp.float32)
    hidden = (jax.nn.silu(gate_out) * upward).astype(jnp.bfloat16)
    out_ref[...] = jnp.dot(hidden, down_ref[...], preferred_element_type=jnp.float32).astype(
        out_ref.dtype
    )


def ffn_half(inputs, gate_part, up_part, down_part, tile=256):
    flat_rows = inputs.reshape(-1, inputs.shape[-1])
    rows, width = flat_rows.shape
    hidden = gate_part.shape[1]
    fixed = lambda i: (0, 0)
    out = pl.pallas_call(
        ffn_kernel,
        grid=(rows // tile,),
        in_specs=[
            pl.BlockSpec((tile, width), lambda i: (i, 0)),
            pl.BlockSpec((width, hidden), fixed),
            pl.BlockSpec((width, hidden), fixed),
            pl.BlockSpec((hidden, width), fixed),
        ],
        out_specs=pl.BlockSpec((tile, width), lambda i: (i, 0)),
        out_shape=jax.ShapeDtypeStruct((rows, width), jnp.bfloat16),
        compiler_params=pltpu.CompilerParams(vmem_limit_bytes=48 * 1024 * 1024),
        cost_estimate=pl.CostEstimate(
            flops=6 * rows * width * hidden,
            transcendentals=rows * hidden,
            bytes_accessed=2 * (2 * rows * width + 3 * width * hidden),
        ),
    )(flat_rows, gate_part, up_part, down_part)
    return out.reshape(inputs.shape)


def body(
    pre_latent,
    pre_qlat,
    pre_qrope,
    pre_resid,
    block_order,
    dec_new,
    dec_qlat,
    dec_qrope,
    dec_resid,
    cache_len,
    page_table,
    cache_pool,
    w_uv,
    w_out,
    norm_gain,
    router,
    routes,
    w_gate,
    w_up,
    w_down,
):
    ctx_count = lax.axis_size("ctx")
    ctx_index = lax.axis_index("ctx")
    score_scale = (DN + DR) ** (-0.5)
    latent = pre_latent[0]
    shard_rows = latent.shape[0]
    local_rows = jnp.arange(shard_rows)
    own_pos = block_position(block_order, ctx_index * shard_rows + local_rows, shard_rows)
    cos_table, sin_table = rope_tables(own_pos, DR)
    key_rope = rotate(latent[:, DC:], cos_table, sin_table).astype(jnp.bfloat16)
    stored = jnp.concatenate([latent[:, :DC], key_rope], axis=-1)
    rotated = rotate(pre_qrope[0], cos_table[:, None, :], sin_table[:, None, :]).astype(
        jnp.bfloat16
    )
    head_count = pre_qlat.shape[2]

    lengths = cache_len[:, 0]
    tables = page_table[:, 0, :]
    request_count = tables.shape[0]
    pages_dev = tables.shape[1]
    page_rows = cache_pool.shape[1]
    slot_count = cache_pool.shape[0]
    row_width = cache_pool.shape[2]
    cos_new, sin_new = rope_tables(lengths, DR)
    new_rope = rotate(dec_new[:, 0, DC:], cos_new, sin_new).astype(jnp.bfloat16)
    new_rows = jnp.concatenate([dec_new[:, 0, :DC], new_rope], axis=-1)
    page_index = lengths // page_rows
    owner_ctx = page_index // pages_dev
    page_hit = tables[:, :, None] == jnp.arange(slot_count)[None, None, :]
    wanted = jnp.arange(pages_dev)[None, :] == (page_index % pages_dev)[:, None]
    slot_of = jnp.sum(jnp.where(wanted, tables, 0), axis=1)
    target = jnp.where(
        owner_ctx == ctx_index, slot_of * page_rows + lengths % page_rows, slot_count * page_rows
    )
    row_ids = jnp.arange(slot_count * page_rows)[:, None]
    flat_pool = cache_pool.reshape(slot_count * page_rows, row_width)
    for request in range(request_count):
        flat_pool = jnp.where(row_ids == target[request], new_rows[request][None, :], flat_pool)
    page_valid = jnp.any(page_hit, axis=1)
    page_logical = jnp.sum(page_hit.astype(jnp.int32) * jnp.arange(pages_dev)[None, :, None], axis=1)
    page_start = (ctx_index * pages_dev + page_logical) * page_rows
    key_pos = (page_start[:, :, None] + jnp.arange(page_rows)[None, None, :]).reshape(
        request_count, slot_count * page_rows
    )
    dec_visible = (
        jnp.repeat(page_valid, page_rows, axis=1) & (key_pos <= lengths[:, None])
    )[:, None, :]
    query_rot = rotate(dec_qrope[:, 0], cos_new[:, None, :], sin_new[:, None, :]).astype(
        jnp.bfloat16
    )
    dec_queries = jnp.concatenate([dec_qlat[:, 0], query_rot], axis=-1)
    flat_queries = dec_queries.reshape(request_count * head_count, row_width)
    dec_scores = (
        jnp.dot(flat_pool, flat_queries.T, preferred_element_type=jnp.float32) * score_scale
    ).reshape(slot_count * page_rows, request_count, head_count)
    dec_seen = jnp.transpose(dec_visible[:, 0, :])[:, :, None]
    dec_masked = jnp.where(dec_seen, dec_scores, NEG_FILL)
    local_peak = jnp.max(dec_masked, axis=0)
    dec_weights = jnp.where(dec_seen, jnp.exp(dec_masked - local_peak[None]), 0.0)
    local_total = jnp.sum(dec_weights, axis=0)
    local_accum = lax.dot_general(
        dec_weights.astype(jnp.bfloat16).reshape(slot_count * page_rows, -1),
        flat_pool[:, :DC],
        (((0,), (0,)), ((), ())),
        preferred_element_type=jnp.float32,
    ).reshape(request_count, head_count, DC)

    dec_share = request_count // ctx_count
    part_width = 128 * ((DC + 2 + 127) // 128)
    dec_block = jnp.concatenate(
        [
            local_accum,
            local_peak[..., None],
            local_total[..., None],
            jnp.zeros((request_count, head_count, part_width - DC - 2), jnp.float32),
        ],
        axis=2,
    ).reshape(ctx_count, dec_share * head_count, part_width)
    keys_all, own_parts = context_exchange(stored, dec_block, ctx_count)
    moving = keys_all.reshape(ctx_count * shard_rows, row_width)
    own_parts = own_parts.reshape(ctx_count, dec_share, head_count, part_width)
    part_accum = own_parts[..., :DC]
    part_peak = own_parts[..., DC]
    part_total = own_parts[..., DC + 1]
    merged_peak = jnp.max(part_peak, axis=0)
    factor = jnp.exp(part_peak - merged_peak[None])
    merged_total = jnp.sum(part_total * factor, axis=0)
    merged_accum = jnp.sum(part_accum * factor[..., None], axis=0)
    own_mixed = (merged_accum / merged_total[..., None]).astype(jnp.bfloat16)

    key_pos_pre = block_position(block_order, jnp.arange(moving.shape[0]), shard_rows)
    query_rows = shard_rows * head_count
    scores = (
        jnp.dot(
            pre_qlat[0].reshape(query_rows, DC), moving[:, :DC].T,
            preferred_element_type=jnp.float32,
        )
        + jnp.dot(
            rotated.reshape(query_rows, DR), moving[:, DC:].T,
            preferred_element_type=jnp.float32,
        )
    ) * score_scale
    visible = jnp.repeat(key_pos_pre[None, :] <= own_pos[:, None], head_count, axis=0)
    masked = jnp.where(visible, scores, NEG_FILL)
    new_peak = jnp.max(masked, axis=-1)
    weights = jnp.where(visible, jnp.exp(masked - new_peak[..., None]), 0.0)
    totals = jnp.sum(weights, axis=-1)
    accumulated = jnp.dot(
        weights.astype(jnp.bfloat16), moving[:, :DC], preferred_element_type=jnp.float32
    )
    pre_mixed = (accumulated / totals[:, None]).astype(jnp.bfloat16).reshape(
        shard_rows, head_count, DC
    )

    own_resid = lax.dynamic_slice_in_dim(dec_resid[:, 0], ctx_index * dec_share, dec_share, 0)
    mixed_all = jnp.concatenate([pre_mixed, own_mixed], axis=0)
    resid_all = jnp.concatenate([pre_resid[0], own_resid], axis=0)
    values = jnp.einsum("nhc,hcv->nhv", mixed_all, w_uv, preferred_element_type=jnp.float32).astype(
        jnp.bfloat16
    )
    hidden_state = resid_all.astype(jnp.float32) + jnp.dot(
        values.reshape(values.shape[0], -1), w_out, preferred_element_type=jnp.float32
    )
    normed = (
        hidden_state
        * lax.rsqrt(jnp.mean(hidden_state * hidden_state, axis=-1, keepdims=True) + EPSILON)
        * norm_gain
    ).astype(jnp.bfloat16)
    logits = jnp.dot(normed.astype(jnp.float32), router, precision=lax.Precision.HIGHEST)
    probable = jax.nn.sigmoid(logits)
    row_count = normed.shape[0]
    width = normed.shape[1]
    top_count = routes.shape[1]
    expert_count = router.shape[1]
    devices = ctx_count * lax.axis_size("req")
    capacity = 2 * ((row_count * top_count + 2 * expert_count - 1) // (2 * expert_count))
    route_hit = routes[:, :, None] == jnp.arange(expert_count)[None, None, :]
    chosen = jnp.sum(jnp.where(route_hit, probable[:, None, :], 0.0), axis=-1)
    mixing = ROUTE_SCALE * chosen / jnp.sum(chosen, axis=1, keepdims=True)
    expert_hits = route_hit.astype(jnp.int32).sum(1)
    earlier = (jnp.arange(row_count)[None, :] < jnp.arange(row_count)[:, None]).astype(jnp.bfloat16)
    before = jnp.dot(
        earlier, expert_hits.astype(jnp.bfloat16), preferred_element_type=jnp.float32
    ).astype(jnp.int32)
    slot_index = jnp.sum(jnp.where(route_hit, before[:, None, :], 0), axis=-1)
    target_slot = routes * capacity + slot_index
    slot_hit = target_slot[:, :, None] == jnp.arange(expert_count * capacity)[None, None, :]
    dispatch = jnp.any(slot_hit, axis=1).astype(jnp.bfloat16)
    outgoing = lax.dot_general(
        dispatch, normed, (((0,), (0,)), ((), ())), preferred_element_type=jnp.float32
    ).astype(jnp.bfloat16).reshape(expert_count, capacity, width)
    doubled = jnp.broadcast_to(outgoing[:, None], (expert_count, 2, capacity, width)).reshape(
        devices, capacity, width
    )
    partial_out = ffn_half(
        lax.all_to_all(doubled, ("ctx", "req"), split_axis=0, concat_axis=0, tiled=True),
        w_gate[0],
        w_up[0],
        w_down[0],
    )
    returned = lax.all_to_all(
        partial_out, ("ctx", "req"), split_axis=0, concat_axis=0, tiled=True
    ).reshape(expert_count, 2, capacity, width)
    results = (returned[:, 0].astype(jnp.float32) + returned[:, 1].astype(jnp.float32)).astype(
        jnp.bfloat16
    ).reshape(expert_count * capacity, width)
    combine = jnp.sum(jnp.where(slot_hit, mixing[:, :, None], 0.0), axis=1)
    combine_high = combine.astype(jnp.bfloat16)
    combine_low = (combine - combine_high.astype(jnp.float32)).astype(jnp.bfloat16)
    moe = jnp.dot(combine_high, results, preferred_element_type=jnp.float32) + jnp.dot(
        combine_low, results, preferred_element_type=jnp.float32
    )
    final = (hidden_state + moe).astype(jnp.bfloat16)
    pre_out = final[:shard_rows][None]
    dec_out = final[shard_rows:][:, None]
    cache_out = flat_pool.reshape(cache_pool.shape)
    return (pre_out, dec_out, cache_out)


def solution(mesh):
    in_specs = (
        P("req", "ctx", None),
        P("req", "ctx", None, None),
        P("req", "ctx", None, None),
        P("req", "ctx", None),
        P(),
        P(None, "req", None),
        P(None, "req", None, None),
        P(None, "req", None, None),
        P(None, "req", None),
        P(None, "req"),
        P(None, "req", "ctx"),
        P(("ctx", "req"), None, None),
        P(),
        P(),
        P(),
        P(),
        P(("ctx", "req"), None),
        P(("ctx", "req"), None, None),
        P(("ctx", "req"), None, None),
        P(("ctx", "req"), None, None),
    )
    out_specs = (P("req", "ctx", None), P("ctx", "req", None), P(("ctx", "req"), None, None))
    return jax.shard_map(body, mesh=mesh, in_specs=in_specs, out_specs=out_specs, check_vma=False)
```

```python
import functools

import jax
import jax.numpy as jnp
from jax import lax
from jax.experimental import pallas as pl
from jax.experimental.pallas import tpu as pltpu
from jax.sharding import PartitionSpec as P

MESH = pl.DeviceIdType.MESH

DC = 512
DR = 64
DN = 128


THETA = 50000.0
ROUTE_SCALE = 2.446
EPSILON = 1e-06
NEG_FILL = -1e30


def joined(part, axis, combine):
    gathered = jax.tree.map(lambda a: lax.all_gather(a, axis), part)

    def take(source):
        return jax.tree.map(lambda a: lax.dynamic_index_in_dim(a, source, 0, False), gathered)

    return lax.fori_loop(
        1, lax.axis_size(axis), lambda source, state: combine(state, take(source)), take(0)
    )


def rope_tables(positions, rope_width):
    halfway = rope_width // 2
    inverse = THETA ** (-(jnp.arange(halfway).astype(jnp.float32) * 2.0) / rope_width)
    angles = positions.astype(jnp.float32)[..., None] * inverse
    return (jnp.cos(angles), jnp.sin(angles))


def rotate(values, cos_table, sin_table):
    halfway = values.shape[-1] // 2
    leading = values[..., :halfway].astype(jnp.float32)
    trailing = values[..., halfway:].astype(jnp.float32)
    return jnp.concatenate(
        [leading * cos_table - trailing * sin_table, trailing * cos_table + leading * sin_table],
        axis=-1,
    )


def block_position(block_order, global_rows, shard_rows):
    half_rows = shard_rows // 2
    block = global_rows // half_rows
    hit = block[:, None] == jnp.arange(block_order.shape[0])[None, :]
    logical = jnp.sum(jnp.where(hit, block_order[None, :], 0), axis=1)
    return logical * half_rows + global_rows % half_rows


def expert_half(inputs, gate_part, up_part, down_part):
    flat_rows = inputs.reshape(-1, inputs.shape[-1])
    gate_out = jnp.dot(flat_rows, gate_part, preferred_element_type=jnp.float32)
    upward = jnp.dot(flat_rows, up_part, preferred_element_type=jnp.float32)
    hidden = (jax.nn.silu(gate_out) * upward).astype(jnp.bfloat16)
    partial_out = jnp.dot(hidden, down_part, preferred_element_type=jnp.float32).astype(
        jnp.bfloat16
    )
    return partial_out.reshape(inputs.shape)


def merge_softmax(earlier, later):
    left_peak, left_total, left_accum = earlier
    right_peak, right_total, right_accum = later
    new_peak = jnp.maximum(left_peak, right_peak)
    left_factor = jnp.exp(left_peak - new_peak)
    right_factor = jnp.exp(right_peak - new_peak)
    merged_total = left_total * left_factor + right_total * right_factor
    merged_accum = left_accum * left_factor[..., None] + right_accum * right_factor[..., None]
    return (new_peak, merged_total, merged_accum)


def exchange_kernel(n_req, total, x_ref, out_ref, send_sem, recv_sem, local_sem):
    me = lax.axis_index("ctx") * n_req + lax.axis_index("req")

    def device(d):
        return (d // n_req, d % n_req)

    def outgoing(d):
        return pltpu.make_async_remote_copy(
            src_ref=x_ref.at[d],
            dst_ref=out_ref.at[me],
            send_sem=send_sem.at[d],
            recv_sem=recv_sem.at[me],
            device_id=device(d),
            device_id_type=MESH,
        )

    def incoming(s):
        return pltpu.make_async_remote_copy(
            src_ref=x_ref.at[me],
            dst_ref=out_ref.at[s],
            send_sem=send_sem.at[s],
            recv_sem=recv_sem.at[s],
            device_id=device(s),
            device_id_type=MESH,
        )

    barrier = pltpu.get_barrier_semaphore()

    def greet(k, carry):
        d = lax.rem(me + k, total)
        pl.semaphore_signal(barrier, inc=1, device_id=device(d), device_id_type=MESH)
        return carry

    lax.fori_loop(1, total, greet, 0)
    pl.semaphore_wait(barrier, total - 1)
    local = pltpu.make_async_copy(x_ref.at[me], out_ref.at[me], local_sem)
    local.start()

    def send(k, carry):
        outgoing(lax.rem(me + k, total)).start()
        return carry

    lax.fori_loop(1, total, send, 0)

    def finish(k, carry):
        outgoing(lax.rem(me + k, total)).wait_send()
        incoming(lax.rem(me + total - k, total)).wait_recv()
        return carry

    lax.fori_loop(1, total, finish, 0)
    local.wait()


def exchange(x, n_req, total, collective_id):
    return pl.pallas_call(
        functools.partial(exchange_kernel, n_req, total),
        out_shape=jax.ShapeDtypeStruct(x.shape, x.dtype),
        in_specs=[pl.BlockSpec(memory_space=pl.ANY)],
        out_specs=pl.BlockSpec(memory_space=pl.ANY),
        scratch_shapes=[
            pltpu.SemaphoreType.DMA((total,)),
            pltpu.SemaphoreType.DMA((total,)),
            pltpu.SemaphoreType.DMA(()),
        ],
        compiler_params=pltpu.CompilerParams(collective_id=collective_id, has_side_effects=True),
    )(x)


def context_kernel(n_ctx, keys_ref, parts_ref, keys_out, parts_out, sems):
    me = lax.axis_index("ctx")
    row = lax.axis_index("req")
    barrier = pltpu.get_barrier_semaphore()
    for step in range(1, n_ctx):
        other = lax.rem(me + step, n_ctx)
        pl.semaphore_signal(barrier, inc=1, device_id=(other, row), device_id_type=MESH)
    pl.semaphore_wait(barrier, n_ctx - 1)

    def key_copy(source, target):
        return pltpu.make_async_remote_copy(
            src_ref=keys_ref,
            dst_ref=keys_out.at[source],
            send_sem=sems.at[0, target],
            recv_sem=sems.at[1, source],
            device_id=(target, row),
            device_id_type=MESH,
        )

    def part_copy(source, target):
        return pltpu.make_async_remote_copy(
            src_ref=parts_ref.at[target],
            dst_ref=parts_out.at[source],
            send_sem=sems.at[2, target],
            recv_sem=sems.at[3, source],
            device_id=(target, row),
            device_id_type=MESH,
        )

    own_keys = pltpu.make_async_copy(keys_ref, keys_out.at[me], sems.at[4, 0])
    own_parts = pltpu.make_async_copy(parts_ref.at[me], parts_out.at[me], sems.at[4, 1])
    own_keys.start()
    own_parts.start()
    for step in range(1, n_ctx):
        other = lax.rem(me + step, n_ctx)
        key_copy(me, other).start()
        part_copy(me, other).start()
    for step in range(1, n_ctx):
        other = lax.rem(me + step, n_ctx)
        source = lax.rem(me + n_ctx - step, n_ctx)
        key_copy(me, other).wait_send()
        part_copy(me, other).wait_send()
        key_copy(source, me).wait_recv()
        part_copy(source, me).wait_recv()
    own_keys.wait()
    own_parts.wait()


def context_exchange(keys, parts, n_ctx):
    return pl.pallas_call(
        functools.partial(context_kernel, n_ctx),
        out_shape=(
            jax.ShapeDtypeStruct((n_ctx,) + keys.shape, keys.dtype),
            jax.ShapeDtypeStruct(parts.shape, parts.dtype),
        ),
        in_specs=[pl.BlockSpec(memory_space=pl.ANY)] * 2,
        out_specs=(pl.BlockSpec(memory_space=pl.ANY), pl.BlockSpec(memory_space=pl.ANY)),
        scratch_shapes=[pltpu.SemaphoreType.DMA((5, n_ctx))],
        compiler_params=pltpu.CompilerParams(collective_id=2, has_side_effects=True),
    )(keys, parts)


def ffn_kernel(x_ref, gate_ref, up_ref, down_ref, out_ref):
    rows = x_ref[...]
    gate_out = jnp.dot(rows, gate_ref[...], preferred_element_type=jnp.float32)
    upward = jnp.dot(rows, up_ref[...], preferred_element_type=jnp.float32)
    hidden = (jax.nn.silu(gate_out) * upward).astype(jnp.bfloat16)
    out_ref[...] = jnp.dot(hidden, down_ref[...], preferred_element_type=jnp.float32).astype(
        out_ref.dtype
    )


def ffn_half(inputs, gate_part, up_part, down_part, tile=256):
    flat_rows = inputs.reshape(-1, inputs.shape[-1])
    rows, width = flat_rows.shape
    hidden = gate_part.shape[1]
    fixed = lambda i: (0, 0)
    out = pl.pallas_call(
        ffn_kernel,
        grid=(rows // tile,),
        in_specs=[
            pl.BlockSpec((tile, width), lambda i: (i, 0)),
            pl.BlockSpec((width, hidden), fixed),
            pl.BlockSpec((width, hidden), fixed),
            pl.BlockSpec((hidden, width), fixed),
        ],
        out_specs=pl.BlockSpec((tile, width), lambda i: (i, 0)),
        out_shape=jax.ShapeDtypeStruct((rows, width), jnp.bfloat16),
        compiler_params=pltpu.CompilerParams(vmem_limit_bytes=48 * 1024 * 1024),
        cost_estimate=pl.CostEstimate(
            flops=6 * rows * width * hidden,
            transcendentals=rows * hidden,
            bytes_accessed=2 * (2 * rows * width + 3 * width * hidden),
        ),
    )(flat_rows, gate_part, up_part, down_part)
    return out.reshape(inputs.shape)


def body(
    pre_latent,
    pre_qlat,
    pre_qrope,
    pre_resid,
    block_order,
    dec_new,
    dec_qlat,
    dec_qrope,
    dec_resid,
    cache_len,
    page_table,
    cache_pool,
    w_uv,
    w_out,
    norm_gain,
    router,
    routes,
    w_gate,
    w_up,
    w_down,
):
    ctx_count = lax.axis_size("ctx")
    ctx_index = lax.axis_index("ctx")
    score_scale = (DN + DR) ** (-0.5)
    latent = pre_latent[0]
    shard_rows = latent.shape[0]
    local_rows = jnp.arange(shard_rows)
    own_pos = block_position(block_order, ctx_index * shard_rows + local_rows, shard_rows)
    cos_table, sin_table = rope_tables(own_pos, DR)
    key_rope = rotate(latent[:, DC:], cos_table, sin_table).astype(jnp.bfloat16)
    stored = jnp.concatenate([latent[:, :DC], key_rope], axis=-1)
    rotated = rotate(pre_qrope[0], cos_table[:, None, :], sin_table[:, None, :]).astype(
        jnp.bfloat16
    )
    head_count = pre_qlat.shape[2]

    lengths = cache_len[:, 0]
    tables = page_table[:, 0, :]
    request_count = tables.shape[0]
    pages_dev = tables.shape[1]
    page_rows = cache_pool.shape[1]
    slot_count = cache_pool.shape[0]
    row_width = cache_pool.shape[2]
    cos_new, sin_new = rope_tables(lengths, DR)
    new_rope = rotate(dec_new[:, 0, DC:], cos_new, sin_new).astype(jnp.bfloat16)
    new_rows = jnp.concatenate([dec_new[:, 0, :DC], new_rope], axis=-1)
    page_index = lengths // page_rows
    owner_ctx = page_index // pages_dev
    page_hit = tables[:, :, None] == jnp.arange(slot_count)[None, None, :]
    wanted = jnp.arange(pages_dev)[None, :] == (page_index % pages_dev)[:, None]
    slot_of = jnp.sum(jnp.where(wanted, tables, 0), axis=1)
    target = jnp.where(
        owner_ctx == ctx_index, slot_of * page_rows + lengths % page_rows, slot_count * page_rows
    )
    row_ids = jnp.arange(slot_count * page_rows)[:, None]
    flat_pool = cache_pool.reshape(slot_count * page_rows, row_width)
    for request in range(request_count):
        flat_pool = jnp.where(row_ids == target[request], new_rows[request][None, :], flat_pool)
    page_valid = jnp.any(page_hit, axis=1)
    page_logical = jnp.sum(page_hit.astype(jnp.int32) * jnp.arange(pages_dev)[None, :, None], axis=1)
    page_start = (ctx_index * pages_dev + page_logical) * page_rows
    key_pos = (page_start[:, :, None] + jnp.arange(page_rows)[None, None, :]).reshape(
        request_count, slot_count * page_rows
    )
    dec_visible = (
        jnp.repeat(page_valid, page_rows, axis=1) & (key_pos <= lengths[:, None])
    )[:, None, :]
    query_rot = rotate(dec_qrope[:, 0], cos_new[:, None, :], sin_new[:, None, :]).astype(
        jnp.bfloat16
    )
    dec_queries = jnp.concatenate([dec_qlat[:, 0], query_rot], axis=-1)
    flat_queries = dec_queries.reshape(request_count * head_count, row_width)
    dec_scores = (
        jnp.dot(flat_pool, flat_queries.T, preferred_element_type=jnp.float32) * score_scale
    ).reshape(slot_count * page_rows, request_count, head_count)
    dec_seen = jnp.transpose(dec_visible[:, 0, :])[:, :, None]
    dec_masked = jnp.where(dec_seen, dec_scores, NEG_FILL)
    local_peak = jnp.max(dec_masked, axis=0)
    dec_weights = jnp.where(dec_seen, jnp.exp(dec_masked - local_peak[None]), 0.0)
    local_total = jnp.sum(dec_weights, axis=0)
    local_accum = lax.dot_general(
        dec_weights.astype(jnp.bfloat16).reshape(slot_count * page_rows, -1),
        flat_pool[:, :DC],
        (((0,), (0,)), ((), ())),
        preferred_element_type=jnp.float32,
    ).reshape(request_count, head_count, DC)

    dec_share = request_count // ctx_count
    part_width = 128 * ((DC + 2 + 127) // 128)
    dec_block = jnp.concatenate(
        [
            local_accum,
            local_peak[..., None],
            local_total[..., None],
            jnp.zeros((request_count, head_count, part_width - DC - 2), jnp.float32),
        ],
        axis=2,
    ).reshape(ctx_count, dec_share * head_count, part_width)
    keys_all, own_parts = context_exchange(stored, dec_block, ctx_count)
    moving = keys_all.reshape(ctx_count * shard_rows, row_width)
    own_parts = own_parts.reshape(ctx_count, dec_share, head_count, part_width)
    part_accum = own_parts[..., :DC]
    part_peak = own_parts[..., DC]
    part_total = own_parts[..., DC + 1]
    merged_peak = jnp.max(part_peak, axis=0)
    factor = jnp.exp(part_peak - merged_peak[None])
    merged_total = jnp.sum(part_total * factor, axis=0)
    merged_accum = jnp.sum(part_accum * factor[..., None], axis=0)
    own_mixed = (merged_accum / merged_total[..., None]).astype(jnp.bfloat16)

    key_pos_pre = block_position(block_order, jnp.arange(moving.shape[0]), shard_rows)
    query_rows = shard_rows * head_count
    scores = (
        jnp.dot(
            pre_qlat[0].reshape(query_rows, DC), moving[:, :DC].T,
            preferred_element_type=jnp.float32,
        )
        + jnp.dot(
            rotated.reshape(query_rows, DR), moving[:, DC:].T,
            preferred_element_type=jnp.float32,
        )
    ) * score_scale
    visible = jnp.repeat(key_pos_pre[None, :] <= own_pos[:, None], head_count, axis=0)
    masked = jnp.where(visible, scores, NEG_FILL)
    new_peak = jnp.max(masked, axis=-1)
    weights = jnp.where(visible, jnp.exp(masked - new_peak[..., None]), 0.0)
    totals = jnp.sum(weights, axis=-1)
    accumulated = jnp.dot(
        weights.astype(jnp.bfloat16), moving[:, :DC], preferred_element_type=jnp.float32
    )
    pre_mixed = (accumulated / totals[:, None]).astype(jnp.bfloat16).reshape(
        shard_rows, head_count, DC
    )

    own_resid = lax.dynamic_slice_in_dim(dec_resid[:, 0], ctx_index * dec_share, dec_share, 0)
    mixed_all = jnp.concatenate([pre_mixed, own_mixed], axis=0)
    resid_all = jnp.concatenate([pre_resid[0], own_resid], axis=0)
    values = jnp.einsum("nhc,hcv->nhv", mixed_all, w_uv, preferred_element_type=jnp.float32).astype(
        jnp.bfloat16
    )
    hidden_state = resid_all.astype(jnp.float32) + jnp.dot(
        values.reshape(values.shape[0], -1), w_out, preferred_element_type=jnp.float32
    )
    normed = (
        hidden_state
        * lax.rsqrt(jnp.mean(hidden_state * hidden_state, axis=-1, keepdims=True) + EPSILON)
        * norm_gain
    ).astype(jnp.bfloat16)
    logits = jnp.dot(normed.astype(jnp.float32), router, precision=lax.Precision.HIGHEST)
    probable = jax.nn.sigmoid(logits)
    row_count = normed.shape[0]
    width = normed.shape[1]
    top_count = routes.shape[1]
    expert_count = router.shape[1]
    devices = ctx_count * lax.axis_size("req")
    capacity = 2 * ((row_count * top_count + 2 * expert_count - 1) // (2 * expert_count))
    route_hit = routes[:, :, None] == jnp.arange(expert_count)[None, None, :]
    chosen = jnp.sum(jnp.where(route_hit, probable[:, None, :], 0.0), axis=-1)
    mixing = ROUTE_SCALE * chosen / jnp.sum(chosen, axis=1, keepdims=True)
    expert_hits = route_hit.astype(jnp.int32).sum(1)
    earlier = (jnp.arange(row_count)[None, :] < jnp.arange(row_count)[:, None]).astype(jnp.bfloat16)
    before = jnp.dot(
        earlier, expert_hits.astype(jnp.bfloat16), preferred_element_type=jnp.float32
    ).astype(jnp.int32)
    slot_index = jnp.sum(jnp.where(route_hit, before[:, None, :], 0), axis=-1)
    target_slot = routes * capacity + slot_index
    slot_hit = target_slot[:, :, None] == jnp.arange(expert_count * capacity)[None, None, :]
    dispatch = jnp.any(slot_hit, axis=1).astype(jnp.bfloat16)
    outgoing = lax.dot_general(
        dispatch, normed, (((0,), (0,)), ((), ())), preferred_element_type=jnp.float32
    ).astype(jnp.bfloat16).reshape(expert_count, capacity, width)
    doubled = jnp.broadcast_to(outgoing[:, None], (expert_count, 2, capacity, width)).reshape(
        devices, capacity, width
    )
    partial_out = ffn_half(
        lax.all_to_all(doubled, ("ctx", "req"), split_axis=0, concat_axis=0, tiled=True),
        w_gate[0],
        w_up[0],
        w_down[0],
    )
    returned = lax.all_to_all(
        partial_out, ("ctx", "req"), split_axis=0, concat_axis=0, tiled=True
    ).reshape(expert_count, 2, capacity, width)
    results = (returned[:, 0].astype(jnp.float32) + returned[:, 1].astype(jnp.float32)).astype(
        jnp.bfloat16
    ).reshape(expert_count * capacity, width)
    combine = jnp.sum(jnp.where(slot_hit, mixing[:, :, None], 0.0), axis=1)
    moe = jnp.dot(combine, results.astype(jnp.float32), precision=lax.Precision.HIGHEST)
    final = (hidden_state + moe).astype(jnp.bfloat16)
    pre_out = final[:shard_rows][None]
    dec_out = final[shard_rows:][:, None]
    cache_out = flat_pool.reshape(cache_pool.shape)
    return (pre_out, dec_out, cache_out)


def solution(mesh):
    in_specs = (
        P("req", "ctx", None),
        P("req", "ctx", None, None),
        P("req", "ctx", None, None),
        P("req", "ctx", None),
        P(),
        P(None, "req", None),
        P(None, "req", None, None),
        P(None, "req", None, None),
        P(None, "req", None),
        P(None, "req"),
        P(None, "req", "ctx"),
        P(("ctx", "req"), None, None),
        P(),
        P(),
        P(),
        P(),
        P(("ctx", "req"), None),
        P(("ctx", "req"), None, None),
        P(("ctx", "req"), None, None),
        P(("ctx", "req"), None, None),
    )
    out_specs = (P("req", "ctx", None), P("ctx", "req", None), P(("ctx", "req"), None, None))
    return jax.shard_map(body, mesh=mesh, in_specs=in_specs, out_specs=out_specs, check_vma=False)
```

```python
import functools

import jax
import jax.numpy as jnp
from jax import lax
from jax.experimental import pallas as pl
from jax.experimental.pallas import tpu as pltpu
from jax.sharding import PartitionSpec as P

MESH = pl.DeviceIdType.MESH

DC = 512
DR = 64
DN = 128


THETA = 50000.0
ROUTE_SCALE = 2.446
EPSILON = 1e-06
NEG_FILL = -1e30


def joined(part, axis, combine):
    gathered = jax.tree.map(lambda a: lax.all_gather(a, axis), part)

    def take(source):
        return jax.tree.map(lambda a: lax.dynamic_index_in_dim(a, source, 0, False), gathered)

    return lax.fori_loop(
        1, lax.axis_size(axis), lambda source, state: combine(state, take(source)), take(0)
    )


def rope_tables(positions, rope_width):
    halfway = rope_width // 2
    inverse = THETA ** (-(jnp.arange(halfway).astype(jnp.float32) * 2.0) / rope_width)
    angles = positions.astype(jnp.float32)[..., None] * inverse
    return (jnp.cos(angles), jnp.sin(angles))


def rotate(values, cos_table, sin_table):
    halfway = values.shape[-1] // 2
    leading = values[..., :halfway].astype(jnp.float32)
    trailing = values[..., halfway:].astype(jnp.float32)
    return jnp.concatenate(
        [leading * cos_table - trailing * sin_table, trailing * cos_table + leading * sin_table],
        axis=-1,
    )


def block_position(block_order, global_rows, shard_rows):
    half_rows = shard_rows // 2
    block = global_rows // half_rows
    hit = block[:, None] == jnp.arange(block_order.shape[0])[None, :]
    logical = jnp.sum(jnp.where(hit, block_order[None, :], 0), axis=1)
    return logical * half_rows + global_rows % half_rows


def expert_half(inputs, gate_part, up_part, down_part):
    flat_rows = inputs.reshape(-1, inputs.shape[-1])
    gate_out = jnp.dot(flat_rows, gate_part, preferred_element_type=jnp.float32)
    upward = jnp.dot(flat_rows, up_part, preferred_element_type=jnp.float32)
    hidden = (jax.nn.silu(gate_out) * upward).astype(jnp.bfloat16)
    partial_out = jnp.dot(hidden, down_part, preferred_element_type=jnp.float32).astype(
        jnp.bfloat16
    )
    return partial_out.reshape(inputs.shape)


def merge_softmax(earlier, later):
    left_peak, left_total, left_accum = earlier
    right_peak, right_total, right_accum = later
    new_peak = jnp.maximum(left_peak, right_peak)
    left_factor = jnp.exp(left_peak - new_peak)
    right_factor = jnp.exp(right_peak - new_peak)
    merged_total = left_total * left_factor + right_total * right_factor
    merged_accum = left_accum * left_factor[..., None] + right_accum * right_factor[..., None]
    return (new_peak, merged_total, merged_accum)


def exchange_kernel(n_req, total, x_ref, out_ref, send_sem, recv_sem, local_sem):
    me = lax.axis_index("ctx") * n_req + lax.axis_index("req")

    def device(d):
        return (d // n_req, d % n_req)

    def outgoing(d):
        return pltpu.make_async_remote_copy(
            src_ref=x_ref.at[d],
            dst_ref=out_ref.at[me],
            send_sem=send_sem.at[d],
            recv_sem=recv_sem.at[me],
            device_id=device(d),
            device_id_type=MESH,
        )

    def incoming(s):
        return pltpu.make_async_remote_copy(
            src_ref=x_ref.at[me],
            dst_ref=out_ref.at[s],
            send_sem=send_sem.at[s],
            recv_sem=recv_sem.at[s],
            device_id=device(s),
            device_id_type=MESH,
        )

    barrier = pltpu.get_barrier_semaphore()

    def greet(k, carry):
        d = lax.rem(me + k, total)
        pl.semaphore_signal(barrier, inc=1, device_id=device(d), device_id_type=MESH)
        return carry

    lax.fori_loop(1, total, greet, 0)
    pl.semaphore_wait(barrier, total - 1)
    local = pltpu.make_async_copy(x_ref.at[me], out_ref.at[me], local_sem)
    local.start()

    def send(k, carry):
        outgoing(lax.rem(me + k, total)).start()
        return carry

    lax.fori_loop(1, total, send, 0)

    def finish(k, carry):
        outgoing(lax.rem(me + k, total)).wait_send()
        incoming(lax.rem(me + total - k, total)).wait_recv()
        return carry

    lax.fori_loop(1, total, finish, 0)
    local.wait()


def exchange(x, n_req, total, collective_id):
    return pl.pallas_call(
        functools.partial(exchange_kernel, n_req, total),
        out_shape=jax.ShapeDtypeStruct(x.shape, x.dtype),
        in_specs=[pl.BlockSpec(memory_space=pl.ANY)],
        out_specs=pl.BlockSpec(memory_space=pl.ANY),
        scratch_shapes=[
            pltpu.SemaphoreType.DMA((total,)),
            pltpu.SemaphoreType.DMA((total,)),
            pltpu.SemaphoreType.DMA(()),
        ],
        compiler_params=pltpu.CompilerParams(collective_id=collective_id, has_side_effects=True),
    )(x)


def context_kernel(n_ctx, keys_ref, parts_ref, keys_out, parts_out, sems):
    me = lax.axis_index("ctx")
    row = lax.axis_index("req")
    barrier = pltpu.get_barrier_semaphore()
    for step in range(1, n_ctx):
        other = lax.rem(me + step, n_ctx)
        pl.semaphore_signal(barrier, inc=1, device_id=(other, row), device_id_type=MESH)
    pl.semaphore_wait(barrier, n_ctx - 1)

    def key_copy(source, target):
        return pltpu.make_async_remote_copy(
            src_ref=keys_ref,
            dst_ref=keys_out.at[source],
            send_sem=sems.at[0, target],
            recv_sem=sems.at[1, source],
            device_id=(target, row),
            device_id_type=MESH,
        )

    def part_copy(source, target):
        return pltpu.make_async_remote_copy(
            src_ref=parts_ref.at[target],
            dst_ref=parts_out.at[source],
            send_sem=sems.at[2, target],
            recv_sem=sems.at[3, source],
            device_id=(target, row),
            device_id_type=MESH,
        )

    own_keys = pltpu.make_async_copy(keys_ref, keys_out.at[me], sems.at[4, 0])
    own_parts = pltpu.make_async_copy(parts_ref.at[me], parts_out.at[me], sems.at[4, 1])
    own_keys.start()
    own_parts.start()
    for step in range(1, n_ctx):
        other = lax.rem(me + step, n_ctx)
        key_copy(me, other).start()
        part_copy(me, other).start()
    for step in range(1, n_ctx):
        other = lax.rem(me + step, n_ctx)
        source = lax.rem(me + n_ctx - step, n_ctx)
        key_copy(me, other).wait_send()
        part_copy(me, other).wait_send()
        key_copy(source, me).wait_recv()
        part_copy(source, me).wait_recv()
    own_keys.wait()
    own_parts.wait()


def context_exchange(keys, parts, n_ctx):
    return pl.pallas_call(
        functools.partial(context_kernel, n_ctx),
        out_shape=(
            jax.ShapeDtypeStruct((n_ctx,) + keys.shape, keys.dtype),
            jax.ShapeDtypeStruct(parts.shape, parts.dtype),
        ),
        in_specs=[pl.BlockSpec(memory_space=pl.ANY)] * 2,
        out_specs=(pl.BlockSpec(memory_space=pl.ANY), pl.BlockSpec(memory_space=pl.ANY)),
        scratch_shapes=[pltpu.SemaphoreType.DMA((5, n_ctx))],
        compiler_params=pltpu.CompilerParams(collective_id=2, has_side_effects=True),
    )(keys, parts)


def ffn_kernel(x_ref, gate_ref, up_ref, down_ref, out_ref):
    rows = x_ref[...]
    gate_out = jnp.dot(rows, gate_ref[...], preferred_element_type=jnp.float32)
    upward = jnp.dot(rows, up_ref[...], preferred_element_type=jnp.float32)
    hidden = (jax.nn.silu(gate_out) * upward).astype(jnp.bfloat16)
    out_ref[...] = jnp.dot(hidden, down_ref[...], preferred_element_type=jnp.float32).astype(
        out_ref.dtype
    )


def ffn_half(inputs, gate_part, up_part, down_part, tile=256):
    flat_rows = inputs.reshape(-1, inputs.shape[-1])
    rows, width = flat_rows.shape
    hidden = gate_part.shape[1]
    fixed = lambda i: (0, 0)
    out = pl.pallas_call(
        ffn_kernel,
        grid=(rows // tile,),
        in_specs=[
            pl.BlockSpec((tile, width), lambda i: (i, 0)),
            pl.BlockSpec((width, hidden), fixed),
            pl.BlockSpec((width, hidden), fixed),
            pl.BlockSpec((hidden, width), fixed),
        ],
        out_specs=pl.BlockSpec((tile, width), lambda i: (i, 0)),
        out_shape=jax.ShapeDtypeStruct((rows, width), jnp.bfloat16),
        compiler_params=pltpu.CompilerParams(vmem_limit_bytes=48 * 1024 * 1024),
        cost_estimate=pl.CostEstimate(
            flops=6 * rows * width * hidden,
            transcendentals=rows * hidden,
            bytes_accessed=2 * (2 * rows * width + 3 * width * hidden),
        ),
    )(flat_rows, gate_part, up_part, down_part)
    return out.reshape(inputs.shape)


def body(
    pre_latent,
    pre_qlat,
    pre_qrope,
    pre_resid,
    block_order,
    dec_new,
    dec_qlat,
    dec_qrope,
    dec_resid,
    cache_len,
    page_table,
    cache_pool,
    w_uv,
    w_out,
    norm_gain,
    router,
    routes,
    w_gate,
    w_up,
    w_down,
):
    ctx_count = lax.axis_size("ctx")
    ctx_index = lax.axis_index("ctx")
    score_scale = (DN + DR) ** (-0.5)
    latent = pre_latent[0]
    shard_rows = latent.shape[0]
    local_rows = jnp.arange(shard_rows)
    own_pos = block_position(block_order, ctx_index * shard_rows + local_rows, shard_rows)
    cos_table, sin_table = rope_tables(own_pos, DR)
    key_rope = rotate(latent[:, DC:], cos_table, sin_table).astype(jnp.bfloat16)
    stored = jnp.concatenate([latent[:, :DC], key_rope], axis=-1)
    rotated = rotate(pre_qrope[0], cos_table[:, None, :], sin_table[:, None, :]).astype(
        jnp.bfloat16
    )
    head_count = pre_qlat.shape[2]

    lengths = cache_len[:, 0]
    tables = page_table[:, 0, :]
    request_count = tables.shape[0]
    pages_dev = tables.shape[1]
    page_rows = cache_pool.shape[1]
    slot_count = cache_pool.shape[0]
    row_width = cache_pool.shape[2]
    cos_new, sin_new = rope_tables(lengths, DR)
    new_rope = rotate(dec_new[:, 0, DC:], cos_new, sin_new).astype(jnp.bfloat16)
    new_rows = jnp.concatenate([dec_new[:, 0, :DC], new_rope], axis=-1)
    page_index = lengths // page_rows
    owner_ctx = page_index // pages_dev
    page_hit = tables[:, :, None] == jnp.arange(slot_count)[None, None, :]
    wanted = jnp.arange(pages_dev)[None, :] == (page_index % pages_dev)[:, None]
    slot_of = jnp.sum(jnp.where(wanted, tables, 0), axis=1)
    target = jnp.where(
        owner_ctx == ctx_index, slot_of * page_rows + lengths % page_rows, slot_count * page_rows
    )
    row_ids = jnp.arange(slot_count * page_rows)[:, None]
    flat_pool = cache_pool.reshape(slot_count * page_rows, row_width)
    for request in range(request_count):
        flat_pool = jnp.where(row_ids == target[request], new_rows[request][None, :], flat_pool)
    page_valid = jnp.any(page_hit, axis=1)
    page_logical = jnp.sum(page_hit.astype(jnp.int32) * jnp.arange(pages_dev)[None, :, None], axis=1)
    page_start = (ctx_index * pages_dev + page_logical) * page_rows
    key_pos = (page_start[:, :, None] + jnp.arange(page_rows)[None, None, :]).reshape(
        request_count, slot_count * page_rows
    )
    dec_visible = (
        jnp.repeat(page_valid, page_rows, axis=1) & (key_pos <= lengths[:, None])
    )[:, None, :]
    query_rot = rotate(dec_qrope[:, 0], cos_new[:, None, :], sin_new[:, None, :]).astype(
        jnp.bfloat16
    )
    dec_queries = jnp.concatenate([dec_qlat[:, 0], query_rot], axis=-1)
    flat_queries = dec_queries.reshape(request_count * head_count, row_width)
    dec_scores = (
        jnp.dot(flat_pool, flat_queries.T, preferred_element_type=jnp.float32) * score_scale
    ).reshape(slot_count * page_rows, request_count, head_count)
    dec_seen = jnp.transpose(dec_visible[:, 0, :])[:, :, None]
    dec_masked = jnp.where(dec_seen, dec_scores, NEG_FILL)
    local_peak = jnp.max(dec_masked, axis=0)
    dec_weights = jnp.where(dec_seen, jnp.exp(dec_masked - local_peak[None]), 0.0)
    local_total = jnp.sum(dec_weights, axis=0)
    local_accum = lax.dot_general(
        dec_weights.astype(jnp.bfloat16).reshape(slot_count * page_rows, -1),
        flat_pool[:, :DC],
        (((0,), (0,)), ((), ())),
        preferred_element_type=jnp.float32,
    ).reshape(request_count, head_count, DC)

    dec_share = request_count // ctx_count
    part_width = 128 * ((DC + 2 + 127) // 128)
    dec_block = jnp.concatenate(
        [
            local_accum,
            local_peak[..., None],
            local_total[..., None],
            jnp.zeros((request_count, head_count, part_width - DC - 2), jnp.float32),
        ],
        axis=2,
    ).reshape(ctx_count, dec_share * head_count, part_width)
    keys_all, own_parts = context_exchange(stored, dec_block, ctx_count)
    moving = keys_all.reshape(ctx_count * shard_rows, row_width)
    own_parts = own_parts.reshape(ctx_count, dec_share, head_count, part_width)
    part_accum = own_parts[..., :DC]
    part_peak = own_parts[..., DC]
    part_total = own_parts[..., DC + 1]
    merged_peak = jnp.max(part_peak, axis=0)
    factor = jnp.exp(part_peak - merged_peak[None])
    merged_total = jnp.sum(part_total * factor, axis=0)
    merged_accum = jnp.sum(part_accum * factor[..., None], axis=0)
    own_mixed = (merged_accum / merged_total[..., None]).astype(jnp.bfloat16)

    key_pos_pre = block_position(block_order, jnp.arange(moving.shape[0]), shard_rows)
    query_rows = shard_rows * head_count
    scores = (
        jnp.dot(
            pre_qlat[0].reshape(query_rows, DC), moving[:, :DC].T,
            preferred_element_type=jnp.float32,
        )
        + jnp.dot(
            rotated.reshape(query_rows, DR), moving[:, DC:].T,
            preferred_element_type=jnp.float32,
        )
    ) * score_scale
    visible = jnp.repeat(key_pos_pre[None, :] <= own_pos[:, None], head_count, axis=0)
    masked = jnp.where(visible, scores, NEG_FILL)
    new_peak = jnp.max(masked, axis=-1)
    weights = jnp.where(visible, jnp.exp(masked - new_peak[..., None]), 0.0)
    totals = jnp.sum(weights, axis=-1)
    accumulated = jnp.dot(
        weights.astype(jnp.bfloat16), moving[:, :DC], preferred_element_type=jnp.float32
    )
    pre_mixed = (accumulated / totals[:, None]).astype(jnp.bfloat16).reshape(
        shard_rows, head_count, DC
    )

    own_resid = lax.dynamic_slice_in_dim(dec_resid[:, 0], ctx_index * dec_share, dec_share, 0)
    mixed_all = jnp.concatenate([pre_mixed, own_mixed], axis=0)
    resid_all = jnp.concatenate([pre_resid[0], own_resid], axis=0)
    values = jnp.einsum("nhc,hcv->nhv", mixed_all, w_uv, preferred_element_type=jnp.float32).astype(
        jnp.bfloat16
    )
    hidden_state = resid_all.astype(jnp.float32) + jnp.dot(
        values.reshape(values.shape[0], -1), w_out, preferred_element_type=jnp.float32
    )
    normed = (
        hidden_state
        * lax.rsqrt(jnp.mean(hidden_state * hidden_state, axis=-1, keepdims=True) + EPSILON)
        * norm_gain
    ).astype(jnp.bfloat16)
    logits = jnp.dot(normed.astype(jnp.float32), router, precision=lax.Precision.HIGHEST)
    probable = jax.nn.sigmoid(logits)
    row_count = normed.shape[0]
    width = normed.shape[1]
    top_count = routes.shape[1]
    expert_count = router.shape[1]
    devices = ctx_count * lax.axis_size("req")
    capacity = 2 * ((row_count * top_count + 2 * expert_count - 1) // (2 * expert_count))
    route_hit = routes[:, :, None] == jnp.arange(expert_count)[None, None, :]
    chosen = jnp.sum(jnp.where(route_hit, probable[:, None, :], 0.0), axis=-1)
    mixing = ROUTE_SCALE * chosen / jnp.sum(chosen, axis=1, keepdims=True)
    expert_hits = route_hit.astype(jnp.int32).sum(1)
    earlier = (jnp.arange(row_count)[None, :] < jnp.arange(row_count)[:, None]).astype(jnp.bfloat16)
    before = jnp.dot(
        earlier, expert_hits.astype(jnp.bfloat16), preferred_element_type=jnp.float32
    ).astype(jnp.int32)
    slot_index = jnp.sum(jnp.where(route_hit, before[:, None, :], 0), axis=-1)
    target_slot = routes * capacity + slot_index
    slot_hit = target_slot[:, :, None] == jnp.arange(expert_count * capacity)[None, None, :]
    dispatch = jnp.any(slot_hit, axis=1).astype(jnp.bfloat16).reshape(row_count, expert_count, 1, capacity)
    dispatch = jnp.broadcast_to(dispatch, (row_count, expert_count, 2, capacity)).reshape(row_count, -1)
    doubled = lax.dot_general(
        dispatch, normed, (((0,), (0,)), ((), ())), preferred_element_type=jnp.float32
    ).astype(jnp.bfloat16).reshape(devices, capacity, width)
    partial_out = ffn_half(
        lax.all_to_all(doubled, ("ctx", "req"), split_axis=0, concat_axis=0, tiled=True),
        w_gate[0],
        w_up[0],
        w_down[0],
    )
    returned = lax.all_to_all(
        partial_out, ("ctx", "req"), split_axis=0, concat_axis=0, tiled=True
    ).reshape(expert_count, 2, capacity, width)
    results = (returned[:, 0].astype(jnp.float32) + returned[:, 1].astype(jnp.float32)).astype(
        jnp.bfloat16
    ).reshape(expert_count * capacity, width)
    combine = jnp.sum(jnp.where(slot_hit, mixing[:, :, None], 0.0), axis=1)
    moe = jnp.dot(combine, results.astype(jnp.float32), precision=lax.Precision.HIGHEST)
    final = (hidden_state + moe).astype(jnp.bfloat16)
    pre_out = final[:shard_rows][None]
    dec_out = final[shard_rows:][:, None]
    cache_out = flat_pool.reshape(cache_pool.shape)
    return (pre_out, dec_out, cache_out)


def solution(mesh):
    in_specs = (
        P("req", "ctx", None),
        P("req", "ctx", None, None),
        P("req", "ctx", None, None),
        P("req", "ctx", None),
        P(),
        P(None, "req", None),
        P(None, "req", None, None),
        P(None, "req", None, None),
        P(None, "req", None),
        P(None, "req"),
        P(None, "req", "ctx"),
        P(("ctx", "req"), None, None),
        P(),
        P(),
        P(),
        P(),
        P(("ctx", "req"), None),
        P(("ctx", "req"), None, None),
        P(("ctx", "req"), None, None),
        P(("ctx", "req"), None, None),
    )
    out_specs = (P("req", "ctx", None), P("ctx", "req", None), P(("ctx", "req"), None, None))
    return jax.shard_map(body, mesh=mesh, in_specs=in_specs, out_specs=out_specs, check_vma=False)
```

```python
import functools

import jax
import jax.numpy as jnp
from jax import lax
from jax.experimental import pallas as pl
from jax.experimental.pallas import tpu as pltpu
from jax.sharding import PartitionSpec as P

MESH = pl.DeviceIdType.MESH

DC = 512
DR = 64
DN = 128


THETA = 50000.0
ROUTE_SCALE = 2.446
EPSILON = 1e-06
NEG_FILL = -1e30


def joined(part, axis, combine):
    gathered = jax.tree.map(lambda a: lax.all_gather(a, axis), part)

    def take(source):
        return jax.tree.map(lambda a: lax.dynamic_index_in_dim(a, source, 0, False), gathered)

    return lax.fori_loop(
        1, lax.axis_size(axis), lambda source, state: combine(state, take(source)), take(0)
    )


def rope_tables(positions, rope_width):
    halfway = rope_width // 2
    inverse = THETA ** (-(jnp.arange(halfway).astype(jnp.float32) * 2.0) / rope_width)
    angles = positions.astype(jnp.float32)[..., None] * inverse
    return (jnp.cos(angles), jnp.sin(angles))


def rotate(values, cos_table, sin_table):
    halfway = values.shape[-1] // 2
    leading = values[..., :halfway].astype(jnp.float32)
    trailing = values[..., halfway:].astype(jnp.float32)
    return jnp.concatenate(
        [leading * cos_table - trailing * sin_table, trailing * cos_table + leading * sin_table],
        axis=-1,
    )


def block_position(block_order, global_rows, shard_rows):
    half_rows = shard_rows // 2
    block = global_rows // half_rows
    hit = block[:, None] == jnp.arange(block_order.shape[0])[None, :]
    logical = jnp.sum(jnp.where(hit, block_order[None, :], 0), axis=1)
    return logical * half_rows + global_rows % half_rows


def expert_half(inputs, gate_part, up_part, down_part):
    flat_rows = inputs.reshape(-1, inputs.shape[-1])
    gate_out = jnp.dot(flat_rows, gate_part, preferred_element_type=jnp.float32)
    upward = jnp.dot(flat_rows, up_part, preferred_element_type=jnp.float32)
    hidden = (jax.nn.silu(gate_out) * upward).astype(jnp.bfloat16)
    partial_out = jnp.dot(hidden, down_part, preferred_element_type=jnp.float32).astype(
        jnp.bfloat16
    )
    return partial_out.reshape(inputs.shape)


def merge_softmax(earlier, later):
    left_peak, left_total, left_accum = earlier
    right_peak, right_total, right_accum = later
    new_peak = jnp.maximum(left_peak, right_peak)
    left_factor = jnp.exp(left_peak - new_peak)
    right_factor = jnp.exp(right_peak - new_peak)
    merged_total = left_total * left_factor + right_total * right_factor
    merged_accum = left_accum * left_factor[..., None] + right_accum * right_factor[..., None]
    return (new_peak, merged_total, merged_accum)


def exchange_kernel(n_req, total, x_ref, out_ref, send_sem, recv_sem, local_sem):
    me = lax.axis_index("ctx") * n_req + lax.axis_index("req")

    def device(d):
        return (d // n_req, d % n_req)

    def outgoing(d):
        return pltpu.make_async_remote_copy(
            src_ref=x_ref.at[d],
            dst_ref=out_ref.at[me],
            send_sem=send_sem.at[d],
            recv_sem=recv_sem.at[me],
            device_id=device(d),
            device_id_type=MESH,
        )

    def incoming(s):
        return pltpu.make_async_remote_copy(
            src_ref=x_ref.at[me],
            dst_ref=out_ref.at[s],
            send_sem=send_sem.at[s],
            recv_sem=recv_sem.at[s],
            device_id=device(s),
            device_id_type=MESH,
        )

    barrier = pltpu.get_barrier_semaphore()

    def greet(k, carry):
        d = lax.rem(me + k, total)
        pl.semaphore_signal(barrier, inc=1, device_id=device(d), device_id_type=MESH)
        return carry

    lax.fori_loop(1, total, greet, 0)
    pl.semaphore_wait(barrier, total - 1)
    local = pltpu.make_async_copy(x_ref.at[me], out_ref.at[me], local_sem)
    local.start()

    def send(k, carry):
        outgoing(lax.rem(me + k, total)).start()
        return carry

    lax.fori_loop(1, total, send, 0)

    def finish(k, carry):
        outgoing(lax.rem(me + k, total)).wait_send()
        incoming(lax.rem(me + total - k, total)).wait_recv()
        return carry

    lax.fori_loop(1, total, finish, 0)
    local.wait()


def exchange(x, n_req, total, collective_id):
    return pl.pallas_call(
        functools.partial(exchange_kernel, n_req, total),
        out_shape=jax.ShapeDtypeStruct(x.shape, x.dtype),
        in_specs=[pl.BlockSpec(memory_space=pl.ANY)],
        out_specs=pl.BlockSpec(memory_space=pl.ANY),
        scratch_shapes=[
            pltpu.SemaphoreType.DMA((total,)),
            pltpu.SemaphoreType.DMA((total,)),
            pltpu.SemaphoreType.DMA(()),
        ],
        compiler_params=pltpu.CompilerParams(collective_id=collective_id, has_side_effects=True),
    )(x)


def context_kernel(n_ctx, keys_ref, parts_ref, keys_out, parts_out, sems):
    me = lax.axis_index("ctx")
    row = lax.axis_index("req")
    barrier = pltpu.get_barrier_semaphore()
    for step in range(1, n_ctx):
        other = lax.rem(me + step, n_ctx)
        pl.semaphore_signal(barrier, inc=1, device_id=(other, row), device_id_type=MESH)
    pl.semaphore_wait(barrier, n_ctx - 1)

    def key_copy(source, target):
        return pltpu.make_async_remote_copy(
            src_ref=keys_ref,
            dst_ref=keys_out.at[source],
            send_sem=sems.at[0, target],
            recv_sem=sems.at[1, source],
            device_id=(target, row),
            device_id_type=MESH,
        )

    def part_copy(source, target):
        return pltpu.make_async_remote_copy(
            src_ref=parts_ref.at[target],
            dst_ref=parts_out.at[source],
            send_sem=sems.at[2, target],
            recv_sem=sems.at[3, source],
            device_id=(target, row),
            device_id_type=MESH,
        )

    for step in range(1, n_ctx):
        other = lax.rem(me + step, n_ctx)
        key_copy(me, other).start()
        part_copy(me, other).start()
    for step in range(1, n_ctx):
        other = lax.rem(me + step, n_ctx)
        source = lax.rem(me + n_ctx - step, n_ctx)
        key_copy(me, other).wait_send()
        part_copy(me, other).wait_send()
        key_copy(source, me).wait_recv()
        part_copy(source, me).wait_recv()


def context_exchange(keys, parts, n_ctx):
    return pl.pallas_call(
        functools.partial(context_kernel, n_ctx),
        out_shape=(
            jax.ShapeDtypeStruct((n_ctx,) + keys.shape, keys.dtype),
            jax.ShapeDtypeStruct(parts.shape, parts.dtype),
        ),
        in_specs=[pl.BlockSpec(memory_space=pl.ANY)] * 2,
        out_specs=(pl.BlockSpec(memory_space=pl.ANY), pl.BlockSpec(memory_space=pl.ANY)),
        scratch_shapes=[pltpu.SemaphoreType.DMA((4, n_ctx))],
        compiler_params=pltpu.CompilerParams(collective_id=2, has_side_effects=True),
    )(keys, parts)


def ffn_kernel(x_ref, gate_ref, up_ref, down_ref, out_ref):
    rows = x_ref[...]
    gate_out = jnp.dot(rows, gate_ref[...], preferred_element_type=jnp.float32)
    upward = jnp.dot(rows, up_ref[...], preferred_element_type=jnp.float32)
    hidden = (jax.nn.silu(gate_out) * upward).astype(jnp.bfloat16)
    out_ref[...] = jnp.dot(hidden, down_ref[...], preferred_element_type=jnp.float32).astype(
        out_ref.dtype
    )


def ffn_half(inputs, gate_part, up_part, down_part, tile=256):
    flat_rows = inputs.reshape(-1, inputs.shape[-1])
    rows, width = flat_rows.shape
    hidden = gate_part.shape[1]
    fixed = lambda i: (0, 0)
    out = pl.pallas_call(
        ffn_kernel,
        grid=(rows // tile,),
        in_specs=[
            pl.BlockSpec((tile, width), lambda i: (i, 0)),
            pl.BlockSpec((width, hidden), fixed),
            pl.BlockSpec((width, hidden), fixed),
            pl.BlockSpec((hidden, width), fixed),
        ],
        out_specs=pl.BlockSpec((tile, width), lambda i: (i, 0)),
        out_shape=jax.ShapeDtypeStruct((rows, width), jnp.bfloat16),
        compiler_params=pltpu.CompilerParams(vmem_limit_bytes=48 * 1024 * 1024),
        cost_estimate=pl.CostEstimate(
            flops=6 * rows * width * hidden,
            transcendentals=rows * hidden,
            bytes_accessed=2 * (2 * rows * width + 3 * width * hidden),
        ),
    )(flat_rows, gate_part, up_part, down_part)
    return out.reshape(inputs.shape)


def body(
    pre_latent,
    pre_qlat,
    pre_qrope,
    pre_resid,
    block_order,
    dec_new,
    dec_qlat,
    dec_qrope,
    dec_resid,
    cache_len,
    page_table,
    cache_pool,
    w_uv,
    w_out,
    norm_gain,
    router,
    routes,
    w_gate,
    w_up,
    w_down,
):
    ctx_count = lax.axis_size("ctx")
    ctx_index = lax.axis_index("ctx")
    score_scale = (DN + DR) ** (-0.5)
    latent = pre_latent[0]
    shard_rows = latent.shape[0]
    local_rows = jnp.arange(shard_rows)
    own_pos = block_position(block_order, ctx_index * shard_rows + local_rows, shard_rows)
    cos_table, sin_table = rope_tables(own_pos, DR)
    key_rope = rotate(latent[:, DC:], cos_table, sin_table).astype(jnp.bfloat16)
    stored = jnp.concatenate([latent[:, :DC], key_rope], axis=-1)
    rotated = rotate(pre_qrope[0], cos_table[:, None, :], sin_table[:, None, :]).astype(
        jnp.bfloat16
    )
    head_count = pre_qlat.shape[2]

    lengths = cache_len[:, 0]
    tables = page_table[:, 0, :]
    request_count = tables.shape[0]
    pages_dev = tables.shape[1]
    page_rows = cache_pool.shape[1]
    slot_count = cache_pool.shape[0]
    row_width = cache_pool.shape[2]
    cos_new, sin_new = rope_tables(lengths, DR)
    new_rope = rotate(dec_new[:, 0, DC:], cos_new, sin_new).astype(jnp.bfloat16)
    new_rows = jnp.concatenate([dec_new[:, 0, :DC], new_rope], axis=-1)
    page_index = lengths // page_rows
    owner_ctx = page_index // pages_dev
    page_hit = tables[:, :, None] == jnp.arange(slot_count)[None, None, :]
    wanted = jnp.arange(pages_dev)[None, :] == (page_index % pages_dev)[:, None]
    slot_of = jnp.sum(jnp.where(wanted, tables, 0), axis=1)
    target = jnp.where(
        owner_ctx == ctx_index, slot_of * page_rows + lengths % page_rows, slot_count * page_rows
    )
    row_ids = jnp.arange(slot_count * page_rows)[:, None]
    flat_pool = cache_pool.reshape(slot_count * page_rows, row_width)
    for request in range(request_count):
        flat_pool = jnp.where(row_ids == target[request], new_rows[request][None, :], flat_pool)
    page_valid = jnp.any(page_hit, axis=1)
    page_logical = jnp.sum(page_hit.astype(jnp.int32) * jnp.arange(pages_dev)[None, :, None], axis=1)
    page_start = (ctx_index * pages_dev + page_logical) * page_rows
    key_pos = (page_start[:, :, None] + jnp.arange(page_rows)[None, None, :]).reshape(
        request_count, slot_count * page_rows
    )
    dec_visible = (
        jnp.repeat(page_valid, page_rows, axis=1) & (key_pos <= lengths[:, None])
    )[:, None, :]
    query_rot = rotate(dec_qrope[:, 0], cos_new[:, None, :], sin_new[:, None, :]).astype(
        jnp.bfloat16
    )
    dec_queries = jnp.concatenate([dec_qlat[:, 0], query_rot], axis=-1)
    flat_queries = dec_queries.reshape(request_count * head_count, row_width)
    dec_scores = (
        jnp.dot(flat_pool, flat_queries.T, preferred_element_type=jnp.float32) * score_scale
    ).reshape(slot_count * page_rows, request_count, head_count)
    dec_seen = jnp.transpose(dec_visible[:, 0, :])[:, :, None]
    dec_masked = jnp.where(dec_seen, dec_scores, NEG_FILL)
    local_peak = jnp.max(dec_masked, axis=0)
    dec_weights = jnp.where(dec_seen, jnp.exp(dec_masked - local_peak[None]), 0.0)
    local_total = jnp.sum(dec_weights, axis=0)
    local_accum = lax.dot_general(
        dec_weights.astype(jnp.bfloat16).reshape(slot_count * page_rows, -1),
        flat_pool[:, :DC],
        (((0,), (0,)), ((), ())),
        preferred_element_type=jnp.float32,
    ).reshape(request_count, head_count, DC)

    dec_share = request_count // ctx_count
    part_width = 128 * ((DC + 2 + 127) // 128)
    dec_block = jnp.concatenate(
        [
            local_accum,
            local_peak[..., None],
            local_total[..., None],
            jnp.zeros((request_count, head_count, part_width - DC - 2), jnp.float32),
        ],
        axis=2,
    ).reshape(ctx_count, dec_share * head_count, part_width)
    keys_all, own_parts = context_exchange(stored, dec_block, ctx_count)
    keys_all = lax.dynamic_update_index_in_dim(keys_all, stored, ctx_index, 0)
    own_parts = lax.dynamic_update_index_in_dim(
        own_parts, lax.dynamic_index_in_dim(dec_block, ctx_index, 0, False), ctx_index, 0
    )
    moving = keys_all.reshape(ctx_count * shard_rows, row_width)
    own_parts = own_parts.reshape(ctx_count, dec_share, head_count, part_width)
    part_accum = own_parts[..., :DC]
    part_peak = own_parts[..., DC]
    part_total = own_parts[..., DC + 1]
    merged_peak = jnp.max(part_peak, axis=0)
    factor = jnp.exp(part_peak - merged_peak[None])
    merged_total = jnp.sum(part_total * factor, axis=0)
    merged_accum = jnp.sum(part_accum * factor[..., None], axis=0)
    own_mixed = (merged_accum / merged_total[..., None]).astype(jnp.bfloat16)

    key_pos_pre = block_position(block_order, jnp.arange(moving.shape[0]), shard_rows)
    query_rows = shard_rows * head_count
    scores = (
        jnp.dot(
            pre_qlat[0].reshape(query_rows, DC), moving[:, :DC].T,
            preferred_element_type=jnp.float32,
        )
        + jnp.dot(
            rotated.reshape(query_rows, DR), moving[:, DC:].T,
            preferred_element_type=jnp.float32,
        )
    ) * score_scale
    visible = jnp.repeat(key_pos_pre[None, :] <= own_pos[:, None], head_count, axis=0)
    masked = jnp.where(visible, scores, NEG_FILL)
    new_peak = jnp.max(masked, axis=-1)
    weights = jnp.where(visible, jnp.exp(masked - new_peak[..., None]), 0.0)
    totals = jnp.sum(weights, axis=-1)
    accumulated = jnp.dot(
        weights.astype(jnp.bfloat16), moving[:, :DC], preferred_element_type=jnp.float32
    )
    pre_mixed = (accumulated / totals[:, None]).astype(jnp.bfloat16).reshape(
        shard_rows, head_count, DC
    )

    own_resid = lax.dynamic_slice_in_dim(dec_resid[:, 0], ctx_index * dec_share, dec_share, 0)
    mixed_all = jnp.concatenate([pre_mixed, own_mixed], axis=0)
    resid_all = jnp.concatenate([pre_resid[0], own_resid], axis=0)
    values = jnp.einsum("nhc,hcv->nhv", mixed_all, w_uv, preferred_element_type=jnp.float32).astype(
        jnp.bfloat16
    )
    hidden_state = resid_all.astype(jnp.float32) + jnp.dot(
        values.reshape(values.shape[0], -1), w_out, preferred_element_type=jnp.float32
    )
    normed = (
        hidden_state
        * lax.rsqrt(jnp.mean(hidden_state * hidden_state, axis=-1, keepdims=True) + EPSILON)
        * norm_gain
    ).astype(jnp.bfloat16)
    logits = jnp.dot(normed.astype(jnp.float32), router, precision=lax.Precision.HIGHEST)
    probable = jax.nn.sigmoid(logits)
    row_count = normed.shape[0]
    width = normed.shape[1]
    top_count = routes.shape[1]
    expert_count = router.shape[1]
    devices = ctx_count * lax.axis_size("req")
    capacity = 2 * ((row_count * top_count + 2 * expert_count - 1) // (2 * expert_count))
    route_hit = routes[:, :, None] == jnp.arange(expert_count)[None, None, :]
    chosen = jnp.sum(jnp.where(route_hit, probable[:, None, :], 0.0), axis=-1)
    mixing = ROUTE_SCALE * chosen / jnp.sum(chosen, axis=1, keepdims=True)
    expert_hits = route_hit.astype(jnp.int32).sum(1)
    earlier = (jnp.arange(row_count)[None, :] < jnp.arange(row_count)[:, None]).astype(jnp.bfloat16)
    before = jnp.dot(
        earlier, expert_hits.astype(jnp.bfloat16), preferred_element_type=jnp.float32
    ).astype(jnp.int32)
    slot_index = jnp.sum(jnp.where(route_hit, before[:, None, :], 0), axis=-1)
    target_slot = routes * capacity + slot_index
    slot_hit = target_slot[:, :, None] == jnp.arange(expert_count * capacity)[None, None, :]
    dispatch = jnp.any(slot_hit, axis=1).astype(jnp.bfloat16).reshape(row_count, expert_count, 1, capacity)
    dispatch = jnp.broadcast_to(dispatch, (row_count, expert_count, 2, capacity)).reshape(row_count, -1)
    doubled = lax.dot_general(
        dispatch, normed, (((0,), (0,)), ((), ())), preferred_element_type=jnp.float32
    ).astype(jnp.bfloat16).reshape(devices, capacity, width)
    partial_out = ffn_half(
        lax.all_to_all(doubled, ("ctx", "req"), split_axis=0, concat_axis=0, tiled=True),
        w_gate[0],
        w_up[0],
        w_down[0],
    )
    returned = lax.all_to_all(
        partial_out, ("ctx", "req"), split_axis=0, concat_axis=0, tiled=True
    ).reshape(expert_count, 2, capacity, width)
    results = (returned[:, 0].astype(jnp.float32) + returned[:, 1].astype(jnp.float32)).astype(
        jnp.bfloat16
    ).reshape(expert_count * capacity, width)
    combine = jnp.sum(jnp.where(slot_hit, mixing[:, :, None], 0.0), axis=1)
    moe = jnp.dot(combine, results.astype(jnp.float32), precision=lax.Precision.HIGHEST)
    final = (hidden_state + moe).astype(jnp.bfloat16)
    pre_out = final[:shard_rows][None]
    dec_out = final[shard_rows:][:, None]
    cache_out = flat_pool.reshape(cache_pool.shape)
    return (pre_out, dec_out, cache_out)


def solution(mesh):
    in_specs = (
        P("req", "ctx", None),
        P("req", "ctx", None, None),
        P("req", "ctx", None, None),
        P("req", "ctx", None),
        P(),
        P(None, "req", None),
        P(None, "req", None, None),
        P(None, "req", None, None),
        P(None, "req", None),
        P(None, "req"),
        P(None, "req", "ctx"),
        P(("ctx", "req"), None, None),
        P(),
        P(),
        P(),
        P(),
        P(("ctx", "req"), None),
        P(("ctx", "req"), None, None),
        P(("ctx", "req"), None, None),
        P(("ctx", "req"), None, None),
    )
    out_specs = (P("req", "ctx", None), P("ctx", "req", None), P(("ctx", "req"), None, None))
    return jax.shard_map(body, mesh=mesh, in_specs=in_specs, out_specs=out_specs, check_vma=False)
```

```python
import functools

import jax
import jax.numpy as jnp
from jax import lax
from jax.experimental import pallas as pl
from jax.experimental.pallas import tpu as pltpu
from jax.sharding import PartitionSpec as P

MESH = pl.DeviceIdType.MESH

DC = 512
DR = 64
DN = 128


THETA = 50000.0
ROUTE_SCALE = 2.446
EPSILON = 1e-06
NEG_FILL = -1e30


def joined(part, axis, combine):
    gathered = jax.tree.map(lambda a: lax.all_gather(a, axis), part)

    def take(source):
        return jax.tree.map(lambda a: lax.dynamic_index_in_dim(a, source, 0, False), gathered)

    return lax.fori_loop(
        1, lax.axis_size(axis), lambda source, state: combine(state, take(source)), take(0)
    )


def rope_tables(positions, rope_width):
    halfway = rope_width // 2
    inverse = THETA ** (-(jnp.arange(halfway).astype(jnp.float32) * 2.0) / rope_width)
    angles = positions.astype(jnp.float32)[..., None] * inverse
    return (jnp.cos(angles), jnp.sin(angles))


def rotate(values, cos_table, sin_table):
    halfway = values.shape[-1] // 2
    leading = values[..., :halfway].astype(jnp.float32)
    trailing = values[..., halfway:].astype(jnp.float32)
    return jnp.concatenate(
        [leading * cos_table - trailing * sin_table, trailing * cos_table + leading * sin_table],
        axis=-1,
    )


def block_position(block_order, global_rows, shard_rows):
    half_rows = shard_rows // 2
    block = global_rows // half_rows
    hit = block[:, None] == jnp.arange(block_order.shape[0])[None, :]
    logical = jnp.sum(jnp.where(hit, block_order[None, :], 0), axis=1)
    return logical * half_rows + global_rows % half_rows


def expert_half(inputs, gate_part, up_part, down_part):
    flat_rows = inputs.reshape(-1, inputs.shape[-1])
    gate_out = jnp.dot(flat_rows, gate_part, preferred_element_type=jnp.float32)
    upward = jnp.dot(flat_rows, up_part, preferred_element_type=jnp.float32)
    hidden = (jax.nn.silu(gate_out) * upward).astype(jnp.bfloat16)
    partial_out = jnp.dot(hidden, down_part, preferred_element_type=jnp.float32).astype(
        jnp.bfloat16
    )
    return partial_out.reshape(inputs.shape)


def merge_softmax(earlier, later):
    left_peak, left_total, left_accum = earlier
    right_peak, right_total, right_accum = later
    new_peak = jnp.maximum(left_peak, right_peak)
    left_factor = jnp.exp(left_peak - new_peak)
    right_factor = jnp.exp(right_peak - new_peak)
    merged_total = left_total * left_factor + right_total * right_factor
    merged_accum = left_accum * left_factor[..., None] + right_accum * right_factor[..., None]
    return (new_peak, merged_total, merged_accum)


def exchange_kernel(n_req, total, x_ref, out_ref, send_sem, recv_sem, local_sem):
    me = lax.axis_index("ctx") * n_req + lax.axis_index("req")

    def device(d):
        return (d // n_req, d % n_req)

    def outgoing(d):
        return pltpu.make_async_remote_copy(
            src_ref=x_ref.at[d],
            dst_ref=out_ref.at[me],
            send_sem=send_sem.at[d],
            recv_sem=recv_sem.at[me],
            device_id=device(d),
            device_id_type=MESH,
        )

    def incoming(s):
        return pltpu.make_async_remote_copy(
            src_ref=x_ref.at[me],
            dst_ref=out_ref.at[s],
            send_sem=send_sem.at[s],
            recv_sem=recv_sem.at[s],
            device_id=device(s),
            device_id_type=MESH,
        )

    barrier = pltpu.get_barrier_semaphore()

    def greet(k, carry):
        d = lax.rem(me + k, total)
        pl.semaphore_signal(barrier, inc=1, device_id=device(d), device_id_type=MESH)
        return carry

    lax.fori_loop(1, total, greet, 0)
    pl.semaphore_wait(barrier, total - 1)
    local = pltpu.make_async_copy(x_ref.at[me], out_ref.at[me], local_sem)
    local.start()

    def send(k, carry):
        outgoing(lax.rem(me + k, total)).start()
        return carry

    lax.fori_loop(1, total, send, 0)

    def finish(k, carry):
        outgoing(lax.rem(me + k, total)).wait_send()
        incoming(lax.rem(me + total - k, total)).wait_recv()
        return carry

    lax.fori_loop(1, total, finish, 0)
    local.wait()


def exchange(x, n_req, total, collective_id):
    return pl.pallas_call(
        functools.partial(exchange_kernel, n_req, total),
        out_shape=jax.ShapeDtypeStruct(x.shape, x.dtype),
        in_specs=[pl.BlockSpec(memory_space=pl.ANY)],
        out_specs=pl.BlockSpec(memory_space=pl.ANY),
        scratch_shapes=[
            pltpu.SemaphoreType.DMA((total,)),
            pltpu.SemaphoreType.DMA((total,)),
            pltpu.SemaphoreType.DMA(()),
        ],
        compiler_params=pltpu.CompilerParams(collective_id=collective_id, has_side_effects=True),
    )(x)


def context_kernel(n_ctx, keys_ref, parts_ref, keys_out, parts_out, sems):
    me = lax.axis_index("ctx")
    row = lax.axis_index("req")
    barrier = pltpu.get_barrier_semaphore()
    for step in range(1, n_ctx):
        other = lax.rem(me + step, n_ctx)
        pl.semaphore_signal(barrier, inc=1, device_id=(other, row), device_id_type=MESH)
    pl.semaphore_wait(barrier, n_ctx - 1)

    def key_copy(source, target):
        return pltpu.make_async_remote_copy(
            src_ref=keys_ref,
            dst_ref=keys_out.at[source],
            send_sem=sems.at[0, target],
            recv_sem=sems.at[1, source],
            device_id=(target, row),
            device_id_type=MESH,
        )

    def part_copy(source, target):
        return pltpu.make_async_remote_copy(
            src_ref=parts_ref.at[target],
            dst_ref=parts_out.at[source],
            send_sem=sems.at[2, target],
            recv_sem=sems.at[3, source],
            device_id=(target, row),
            device_id_type=MESH,
        )

    for step in range(1, n_ctx):
        other = lax.rem(me + step, n_ctx)
        key_copy(me, other).start()
        part_copy(me, other).start()
    for step in range(1, n_ctx):
        other = lax.rem(me + step, n_ctx)
        source = lax.rem(me + n_ctx - step, n_ctx)
        key_copy(me, other).wait_send()
        part_copy(me, other).wait_send()
        key_copy(source, me).wait_recv()
        part_copy(source, me).wait_recv()


def context_exchange(keys, parts, n_ctx):
    return pl.pallas_call(
        functools.partial(context_kernel, n_ctx),
        out_shape=(
            jax.ShapeDtypeStruct((n_ctx,) + keys.shape, keys.dtype),
            jax.ShapeDtypeStruct(parts.shape, parts.dtype),
        ),
        in_specs=[pl.BlockSpec(memory_space=pl.ANY)] * 2,
        out_specs=(pl.BlockSpec(memory_space=pl.ANY), pl.BlockSpec(memory_space=pl.ANY)),
        scratch_shapes=[pltpu.SemaphoreType.DMA((4, n_ctx))],
        compiler_params=pltpu.CompilerParams(collective_id=2, has_side_effects=True),
    )(keys, parts)


def ffn_kernel(x_ref, gate_ref, up_ref, down_ref, out_ref):
    rows = x_ref[...]
    gate_out = jnp.dot(rows, gate_ref[...], preferred_element_type=jnp.float32)
    upward = jnp.dot(rows, up_ref[...], preferred_element_type=jnp.float32)
    hidden = (jax.nn.silu(gate_out) * upward).astype(jnp.bfloat16)
    out_ref[...] = jnp.dot(hidden, down_ref[...], preferred_element_type=jnp.float32).astype(
        out_ref.dtype
    )


def ffn_half(inputs, gate_part, up_part, down_part, tile=256):
    flat_rows = inputs.reshape(-1, inputs.shape[-1])
    rows, width = flat_rows.shape
    hidden = gate_part.shape[1]
    fixed = lambda i: (0, 0)
    out = pl.pallas_call(
        ffn_kernel,
        grid=(rows // tile,),
        in_specs=[
            pl.BlockSpec((tile, width), lambda i: (i, 0)),
            pl.BlockSpec((width, hidden), fixed),
            pl.BlockSpec((width, hidden), fixed),
            pl.BlockSpec((hidden, width), fixed),
        ],
        out_specs=pl.BlockSpec((tile, width), lambda i: (i, 0)),
        out_shape=jax.ShapeDtypeStruct((rows, width), jnp.bfloat16),
        compiler_params=pltpu.CompilerParams(vmem_limit_bytes=48 * 1024 * 1024),
        cost_estimate=pl.CostEstimate(
            flops=6 * rows * width * hidden,
            transcendentals=rows * hidden,
            bytes_accessed=2 * (2 * rows * width + 3 * width * hidden),
        ),
    )(flat_rows, gate_part, up_part, down_part)
    return out.reshape(inputs.shape)


def body(
    pre_latent,
    pre_qlat,
    pre_qrope,
    pre_resid,
    block_order,
    dec_new,
    dec_qlat,
    dec_qrope,
    dec_resid,
    cache_len,
    page_table,
    cache_pool,
    w_uv,
    w_out,
    norm_gain,
    router,
    routes,
    w_gate,
    w_up,
    w_down,
):
    ctx_count = lax.axis_size("ctx")
    ctx_index = lax.axis_index("ctx")
    score_scale = (DN + DR) ** (-0.5)
    latent = pre_latent[0]
    shard_rows = latent.shape[0]
    local_rows = jnp.arange(shard_rows)
    own_pos = block_position(block_order, ctx_index * shard_rows + local_rows, shard_rows)
    cos_table, sin_table = rope_tables(own_pos, DR)
    key_rope = rotate(latent[:, DC:], cos_table, sin_table).astype(jnp.bfloat16)
    stored = jnp.concatenate([latent[:, :DC], key_rope], axis=-1)
    rotated = rotate(pre_qrope[0], cos_table[:, None, :], sin_table[:, None, :]).astype(
        jnp.bfloat16
    )
    head_count = pre_qlat.shape[2]

    lengths = cache_len[:, 0]
    tables = page_table[:, 0, :]
    request_count = tables.shape[0]
    pages_dev = tables.shape[1]
    page_rows = cache_pool.shape[1]
    slot_count = cache_pool.shape[0]
    row_width = cache_pool.shape[2]
    cos_new, sin_new = rope_tables(lengths, DR)
    new_rope = rotate(dec_new[:, 0, DC:], cos_new, sin_new).astype(jnp.bfloat16)
    new_rows = jnp.concatenate([dec_new[:, 0, :DC], new_rope], axis=-1)
    page_index = lengths // page_rows
    owner_ctx = page_index // pages_dev
    page_hit = tables[:, :, None] == jnp.arange(slot_count)[None, None, :]
    wanted = jnp.arange(pages_dev)[None, :] == (page_index % pages_dev)[:, None]
    slot_of = jnp.sum(jnp.where(wanted, tables, 0), axis=1)
    target = jnp.where(
        owner_ctx == ctx_index, slot_of * page_rows + lengths % page_rows, slot_count * page_rows
    )
    row_ids = jnp.arange(slot_count * page_rows)[:, None]
    raw_pool = cache_pool.reshape(slot_count * page_rows, row_width)
    flat_pool = raw_pool
    for request in range(request_count):
        flat_pool = jnp.where(row_ids == target[request], new_rows[request][None, :], flat_pool)
    new_hit = (row_ids == target[None, :])[:, :, None]
    page_valid = jnp.any(page_hit, axis=1)
    page_logical = jnp.sum(page_hit.astype(jnp.int32) * jnp.arange(pages_dev)[None, :, None], axis=1)
    page_start = (ctx_index * pages_dev + page_logical) * page_rows
    key_pos = (page_start[:, :, None] + jnp.arange(page_rows)[None, None, :]).reshape(
        request_count, slot_count * page_rows
    )
    dec_visible = (
        jnp.repeat(page_valid, page_rows, axis=1) & (key_pos <= lengths[:, None])
    )[:, None, :]
    query_rot = rotate(dec_qrope[:, 0], cos_new[:, None, :], sin_new[:, None, :]).astype(
        jnp.bfloat16
    )
    dec_queries = jnp.concatenate([dec_qlat[:, 0], query_rot], axis=-1)
    flat_queries = dec_queries.reshape(request_count * head_count, row_width)
    dec_scores = (
        jnp.dot(raw_pool, flat_queries.T, preferred_element_type=jnp.float32) * score_scale
    ).reshape(slot_count * page_rows, request_count, head_count)
    new_scores = (
        jnp.einsum("rd,rhd->rh", new_rows, dec_queries, preferred_element_type=jnp.float32)
        * score_scale
    )
    dec_scores = jnp.where(new_hit, new_scores[None], dec_scores)
    dec_seen = jnp.transpose(dec_visible[:, 0, :])[:, :, None]
    dec_masked = jnp.where(dec_seen, dec_scores, NEG_FILL)
    local_peak = jnp.max(dec_masked, axis=0)
    dec_weights = jnp.where(dec_seen, jnp.exp(dec_masked - local_peak[None]), 0.0)
    local_total = jnp.sum(dec_weights, axis=0)
    rounded = dec_weights.astype(jnp.bfloat16)
    new_weight = jnp.sum(jnp.where(new_hit, rounded, 0.0).astype(jnp.float32), axis=0)
    local_accum = lax.dot_general(
        jnp.where(new_hit, jnp.zeros_like(rounded), rounded).reshape(slot_count * page_rows, -1),
        raw_pool[:, :DC],
        (((0,), (0,)), ((), ())),
        preferred_element_type=jnp.float32,
    ).reshape(request_count, head_count, DC) + new_weight[..., None] * new_rows[:, None, :DC].astype(
        jnp.float32
    )

    dec_share = request_count // ctx_count
    part_width = 128 * ((DC + 2 + 127) // 128)
    dec_block = jnp.concatenate(
        [
            local_accum,
            local_peak[..., None],
            local_total[..., None],
            jnp.zeros((request_count, head_count, part_width - DC - 2), jnp.float32),
        ],
        axis=2,
    ).reshape(ctx_count, dec_share * head_count, part_width)
    keys_all, own_parts = context_exchange(stored, dec_block, ctx_count)
    keys_all = lax.dynamic_update_index_in_dim(keys_all, stored, ctx_index, 0)
    own_parts = lax.dynamic_update_index_in_dim(
        own_parts, lax.dynamic_index_in_dim(dec_block, ctx_index, 0, False), ctx_index, 0
    )
    moving = keys_all.reshape(ctx_count * shard_rows, row_width)
    own_parts = own_parts.reshape(ctx_count, dec_share, head_count, part_width)
    part_accum = own_parts[..., :DC]
    part_peak = own_parts[..., DC]
    part_total = own_parts[..., DC + 1]
    merged_peak = jnp.max(part_peak, axis=0)
    factor = jnp.exp(part_peak - merged_peak[None])
    merged_total = jnp.sum(part_total * factor, axis=0)
    merged_accum = jnp.sum(part_accum * factor[..., None], axis=0)
    own_mixed = (merged_accum / merged_total[..., None]).astype(jnp.bfloat16)

    key_pos_pre = block_position(block_order, jnp.arange(moving.shape[0]), shard_rows)
    query_rows = shard_rows * head_count
    scores = (
        jnp.dot(
            pre_qlat[0].reshape(query_rows, DC), moving[:, :DC].T,
            preferred_element_type=jnp.float32,
        )
        + jnp.dot(
            rotated.reshape(query_rows, DR), moving[:, DC:].T,
            preferred_element_type=jnp.float32,
        )
    ) * score_scale
    visible = jnp.repeat(key_pos_pre[None, :] <= own_pos[:, None], head_count, axis=0)
    masked = jnp.where(visible, scores, NEG_FILL)
    new_peak = jnp.max(masked, axis=-1)
    weights = jnp.where(visible, jnp.exp(masked - new_peak[..., None]), 0.0)
    totals = jnp.sum(weights, axis=-1)
    accumulated = jnp.dot(
        weights.astype(jnp.bfloat16), moving[:, :DC], preferred_element_type=jnp.float32
    )
    pre_mixed = (accumulated / totals[:, None]).astype(jnp.bfloat16).reshape(
        shard_rows, head_count, DC
    )

    own_resid = lax.dynamic_slice_in_dim(dec_resid[:, 0], ctx_index * dec_share, dec_share, 0)
    mixed_all = jnp.concatenate([pre_mixed, own_mixed], axis=0)
    resid_all = jnp.concatenate([pre_resid[0], own_resid], axis=0)
    values = jnp.einsum("nhc,hcv->nhv", mixed_all, w_uv, preferred_element_type=jnp.float32).astype(
        jnp.bfloat16
    )
    hidden_state = resid_all.astype(jnp.float32) + jnp.dot(
        values.reshape(values.shape[0], -1), w_out, preferred_element_type=jnp.float32
    )
    normed = (
        hidden_state
        * lax.rsqrt(jnp.mean(hidden_state * hidden_state, axis=-1, keepdims=True) + EPSILON)
        * norm_gain
    ).astype(jnp.bfloat16)
    logits = jnp.dot(normed.astype(jnp.float32), router, precision=lax.Precision.HIGHEST)
    probable = jax.nn.sigmoid(logits)
    row_count = normed.shape[0]
    width = normed.shape[1]
    top_count = routes.shape[1]
    expert_count = router.shape[1]
    devices = ctx_count * lax.axis_size("req")
    capacity = 2 * ((row_count * top_count + 2 * expert_count - 1) // (2 * expert_count))
    route_hit = routes[:, :, None] == jnp.arange(expert_count)[None, None, :]
    chosen = jnp.sum(jnp.where(route_hit, probable[:, None, :], 0.0), axis=-1)
    mixing = ROUTE_SCALE * chosen / jnp.sum(chosen, axis=1, keepdims=True)
    expert_hits = route_hit.astype(jnp.int32).sum(1)
    earlier = (jnp.arange(row_count)[None, :] < jnp.arange(row_count)[:, None]).astype(jnp.bfloat16)
    before = jnp.dot(
        earlier, expert_hits.astype(jnp.bfloat16), preferred_element_type=jnp.float32
    ).astype(jnp.int32)
    slot_index = jnp.sum(jnp.where(route_hit, before[:, None, :], 0), axis=-1)
    target_slot = routes * capacity + slot_index
    slot_hit = target_slot[:, :, None] == jnp.arange(expert_count * capacity)[None, None, :]
    dispatch = jnp.any(slot_hit, axis=1).astype(jnp.bfloat16).reshape(row_count, expert_count, 1, capacity)
    dispatch = jnp.broadcast_to(dispatch, (row_count, expert_count, 2, capacity)).reshape(row_count, -1)
    doubled = lax.dot_general(
        dispatch, normed, (((0,), (0,)), ((), ())), preferred_element_type=jnp.float32
    ).astype(jnp.bfloat16).reshape(devices, capacity, width)
    partial_out = ffn_half(
        lax.all_to_all(doubled, ("ctx", "req"), split_axis=0, concat_axis=0, tiled=True),
        w_gate[0],
        w_up[0],
        w_down[0],
    )
    returned = lax.all_to_all(
        partial_out, ("ctx", "req"), split_axis=0, concat_axis=0, tiled=True
    ).reshape(expert_count, 2, capacity, width)
    results = (returned[:, 0].astype(jnp.float32) + returned[:, 1].astype(jnp.float32)).astype(
        jnp.bfloat16
    ).reshape(expert_count * capacity, width)
    combine = jnp.sum(jnp.where(slot_hit, mixing[:, :, None], 0.0), axis=1)
    moe = jnp.dot(combine, results.astype(jnp.float32), precision=lax.Precision.HIGHEST)
    final = (hidden_state + moe).astype(jnp.bfloat16)
    pre_out = final[:shard_rows][None]
    dec_out = final[shard_rows:][:, None]
    cache_out = flat_pool.reshape(cache_pool.shape)
    return (pre_out, dec_out, cache_out)


def solution(mesh):
    in_specs = (
        P("req", "ctx", None),
        P("req", "ctx", None, None),
        P("req", "ctx", None, None),
        P("req", "ctx", None),
        P(),
        P(None, "req", None),
        P(None, "req", None, None),
        P(None, "req", None, None),
        P(None, "req", None),
        P(None, "req"),
        P(None, "req", "ctx"),
        P(("ctx", "req"), None, None),
        P(),
        P(),
        P(),
        P(),
        P(("ctx", "req"), None),
        P(("ctx", "req"), None, None),
        P(("ctx", "req"), None, None),
        P(("ctx", "req"), None, None),
    )
    out_specs = (P("req", "ctx", None), P("ctx", "req", None), P(("ctx", "req"), None, None))
    return jax.shard_map(body, mesh=mesh, in_specs=in_specs, out_specs=out_specs, check_vma=False)
```

```python
import functools

import jax
import jax.numpy as jnp
from jax import lax
from jax.experimental import pallas as pl
from jax.experimental.pallas import tpu as pltpu
from jax.sharding import PartitionSpec as P

MESH = pl.DeviceIdType.MESH

DC = 512
DR = 64
DN = 128


THETA = 50000.0
ROUTE_SCALE = 2.446
EPSILON = 1e-06
NEG_FILL = -1e30


def joined(part, axis, combine):
    gathered = jax.tree.map(lambda a: lax.all_gather(a, axis), part)

    def take(source):
        return jax.tree.map(lambda a: lax.dynamic_index_in_dim(a, source, 0, False), gathered)

    return lax.fori_loop(
        1, lax.axis_size(axis), lambda source, state: combine(state, take(source)), take(0)
    )


def rope_tables(positions, rope_width):
    halfway = rope_width // 2
    inverse = THETA ** (-(jnp.arange(halfway).astype(jnp.float32) * 2.0) / rope_width)
    angles = positions.astype(jnp.float32)[..., None] * inverse
    return (jnp.cos(angles), jnp.sin(angles))


def rotate(values, cos_table, sin_table):
    halfway = values.shape[-1] // 2
    leading = values[..., :halfway].astype(jnp.float32)
    trailing = values[..., halfway:].astype(jnp.float32)
    return jnp.concatenate(
        [leading * cos_table - trailing * sin_table, trailing * cos_table + leading * sin_table],
        axis=-1,
    )


def block_position(block_order, global_rows, shard_rows):
    half_rows = shard_rows // 2
    block = global_rows // half_rows
    hit = block[:, None] == jnp.arange(block_order.shape[0])[None, :]
    logical = jnp.sum(jnp.where(hit, block_order[None, :], 0), axis=1)
    return logical * half_rows + global_rows % half_rows


def expert_half(inputs, gate_part, up_part, down_part):
    flat_rows = inputs.reshape(-1, inputs.shape[-1])
    gate_out = jnp.dot(flat_rows, gate_part, preferred_element_type=jnp.float32)
    upward = jnp.dot(flat_rows, up_part, preferred_element_type=jnp.float32)
    hidden = (jax.nn.silu(gate_out) * upward).astype(jnp.bfloat16)
    partial_out = jnp.dot(hidden, down_part, preferred_element_type=jnp.float32).astype(
        jnp.bfloat16
    )
    return partial_out.reshape(inputs.shape)


def merge_softmax(earlier, later):
    left_peak, left_total, left_accum = earlier
    right_peak, right_total, right_accum = later
    new_peak = jnp.maximum(left_peak, right_peak)
    left_factor = jnp.exp(left_peak - new_peak)
    right_factor = jnp.exp(right_peak - new_peak)
    merged_total = left_total * left_factor + right_total * right_factor
    merged_accum = left_accum * left_factor[..., None] + right_accum * right_factor[..., None]
    return (new_peak, merged_total, merged_accum)


def exchange_kernel(n_req, total, x_ref, out_ref, send_sem, recv_sem, local_sem):
    me = lax.axis_index("ctx") * n_req + lax.axis_index("req")

    def device(d):
        return (d // n_req, d % n_req)

    def outgoing(d):
        return pltpu.make_async_remote_copy(
            src_ref=x_ref.at[d],
            dst_ref=out_ref.at[me],
            send_sem=send_sem.at[d],
            recv_sem=recv_sem.at[me],
            device_id=device(d),
            device_id_type=MESH,
        )

    def incoming(s):
        return pltpu.make_async_remote_copy(
            src_ref=x_ref.at[me],
            dst_ref=out_ref.at[s],
            send_sem=send_sem.at[s],
            recv_sem=recv_sem.at[s],
            device_id=device(s),
            device_id_type=MESH,
        )

    barrier = pltpu.get_barrier_semaphore()

    def greet(k, carry):
        d = lax.rem(me + k, total)
        pl.semaphore_signal(barrier, inc=1, device_id=device(d), device_id_type=MESH)
        return carry

    lax.fori_loop(1, total, greet, 0)
    pl.semaphore_wait(barrier, total - 1)
    local = pltpu.make_async_copy(x_ref.at[me], out_ref.at[me], local_sem)
    local.start()

    def send(k, carry):
        outgoing(lax.rem(me + k, total)).start()
        return carry

    lax.fori_loop(1, total, send, 0)

    def finish(k, carry):
        outgoing(lax.rem(me + k, total)).wait_send()
        incoming(lax.rem(me + total - k, total)).wait_recv()
        return carry

    lax.fori_loop(1, total, finish, 0)
    local.wait()


def exchange(x, n_req, total, collective_id):
    return pl.pallas_call(
        functools.partial(exchange_kernel, n_req, total),
        out_shape=jax.ShapeDtypeStruct(x.shape, x.dtype),
        in_specs=[pl.BlockSpec(memory_space=pl.ANY)],
        out_specs=pl.BlockSpec(memory_space=pl.ANY),
        scratch_shapes=[
            pltpu.SemaphoreType.DMA((total,)),
            pltpu.SemaphoreType.DMA((total,)),
            pltpu.SemaphoreType.DMA(()),
        ],
        compiler_params=pltpu.CompilerParams(collective_id=collective_id, has_side_effects=True),
    )(x)


def context_kernel(n_ctx, keys_ref, parts_ref, keys_out, parts_out, sems):
    me = lax.axis_index("ctx")
    row = lax.axis_index("req")
    barrier = pltpu.get_barrier_semaphore()
    for step in range(1, n_ctx):
        other = lax.rem(me + step, n_ctx)
        pl.semaphore_signal(barrier, inc=1, device_id=(other, row), device_id_type=MESH)
    pl.semaphore_wait(barrier, n_ctx - 1)

    def key_copy(source, target):
        return pltpu.make_async_remote_copy(
            src_ref=keys_ref,
            dst_ref=keys_out.at[source],
            send_sem=sems.at[0, target],
            recv_sem=sems.at[1, source],
            device_id=(target, row),
            device_id_type=MESH,
        )

    def part_copy(source, target):
        return pltpu.make_async_remote_copy(
            src_ref=parts_ref.at[target],
            dst_ref=parts_out.at[source],
            send_sem=sems.at[2, target],
            recv_sem=sems.at[3, source],
            device_id=(target, row),
            device_id_type=MESH,
        )

    for step in range(1, n_ctx):
        other = lax.rem(me + step, n_ctx)
        key_copy(me, other).start()
        part_copy(me, other).start()
    for step in range(1, n_ctx):
        other = lax.rem(me + step, n_ctx)
        source = lax.rem(me + n_ctx - step, n_ctx)
        key_copy(me, other).wait_send()
        part_copy(me, other).wait_send()
        key_copy(source, me).wait_recv()
        part_copy(source, me).wait_recv()


def context_exchange(keys, parts, n_ctx):
    return pl.pallas_call(
        functools.partial(context_kernel, n_ctx),
        out_shape=(
            jax.ShapeDtypeStruct((n_ctx,) + keys.shape, keys.dtype),
            jax.ShapeDtypeStruct(parts.shape, parts.dtype),
        ),
        in_specs=[pl.BlockSpec(memory_space=pl.ANY)] * 2,
        out_specs=(pl.BlockSpec(memory_space=pl.ANY), pl.BlockSpec(memory_space=pl.ANY)),
        scratch_shapes=[pltpu.SemaphoreType.DMA((4, n_ctx))],
        compiler_params=pltpu.CompilerParams(collective_id=2, has_side_effects=True),
    )(keys, parts)


def ffn_kernel(x_ref, gate_ref, up_ref, down_ref, out_ref):
    rows = x_ref[...]
    gate_out = jnp.dot(rows, gate_ref[...], preferred_element_type=jnp.float32)
    upward = jnp.dot(rows, up_ref[...], preferred_element_type=jnp.float32)
    hidden = (jax.nn.silu(gate_out) * upward).astype(jnp.bfloat16)
    out_ref[...] = jnp.dot(hidden, down_ref[...], preferred_element_type=jnp.float32).astype(
        out_ref.dtype
    )


def ffn_half(inputs, gate_part, up_part, down_part, tile=512):
    flat_rows = inputs.reshape(-1, inputs.shape[-1])
    rows, width = flat_rows.shape
    hidden = gate_part.shape[1]
    fixed = lambda i: (0, 0)
    out = pl.pallas_call(
        ffn_kernel,
        grid=(rows // tile,),
        in_specs=[
            pl.BlockSpec((tile, width), lambda i: (i, 0)),
            pl.BlockSpec((width, hidden), fixed),
            pl.BlockSpec((width, hidden), fixed),
            pl.BlockSpec((hidden, width), fixed),
        ],
        out_specs=pl.BlockSpec((tile, width), lambda i: (i, 0)),
        out_shape=jax.ShapeDtypeStruct((rows, width), jnp.bfloat16),
        compiler_params=pltpu.CompilerParams(vmem_limit_bytes=48 * 1024 * 1024),
        cost_estimate=pl.CostEstimate(
            flops=6 * rows * width * hidden,
            transcendentals=rows * hidden,
            bytes_accessed=2 * (2 * rows * width + 3 * width * hidden),
        ),
    )(flat_rows, gate_part, up_part, down_part)
    return out.reshape(inputs.shape)


def body(
    pre_latent,
    pre_qlat,
    pre_qrope,
    pre_resid,
    block_order,
    dec_new,
    dec_qlat,
    dec_qrope,
    dec_resid,
    cache_len,
    page_table,
    cache_pool,
    w_uv,
    w_out,
    norm_gain,
    router,
    routes,
    w_gate,
    w_up,
    w_down,
):
    ctx_count = lax.axis_size("ctx")
    ctx_index = lax.axis_index("ctx")
    score_scale = (DN + DR) ** (-0.5)
    latent = pre_latent[0]
    shard_rows = latent.shape[0]
    local_rows = jnp.arange(shard_rows)
    own_pos = block_position(block_order, ctx_index * shard_rows + local_rows, shard_rows)
    cos_table, sin_table = rope_tables(own_pos, DR)
    key_rope = rotate(latent[:, DC:], cos_table, sin_table).astype(jnp.bfloat16)
    stored = jnp.concatenate([latent[:, :DC], key_rope], axis=-1)
    rotated = rotate(pre_qrope[0], cos_table[:, None, :], sin_table[:, None, :]).astype(
        jnp.bfloat16
    )
    head_count = pre_qlat.shape[2]

    lengths = cache_len[:, 0]
    tables = page_table[:, 0, :]
    request_count = tables.shape[0]
    pages_dev = tables.shape[1]
    page_rows = cache_pool.shape[1]
    slot_count = cache_pool.shape[0]
    row_width = cache_pool.shape[2]
    cos_new, sin_new = rope_tables(lengths, DR)
    new_rope = rotate(dec_new[:, 0, DC:], cos_new, sin_new).astype(jnp.bfloat16)
    new_rows = jnp.concatenate([dec_new[:, 0, :DC], new_rope], axis=-1)
    page_index = lengths // page_rows
    owner_ctx = page_index // pages_dev
    page_hit = tables[:, :, None] == jnp.arange(slot_count)[None, None, :]
    wanted = jnp.arange(pages_dev)[None, :] == (page_index % pages_dev)[:, None]
    slot_of = jnp.sum(jnp.where(wanted, tables, 0), axis=1)
    target = jnp.where(
        owner_ctx == ctx_index, slot_of * page_rows + lengths % page_rows, slot_count * page_rows
    )
    row_ids = jnp.arange(slot_count * page_rows)[:, None]
    raw_pool = cache_pool.reshape(slot_count * page_rows, row_width)
    flat_pool = raw_pool
    for request in range(request_count):
        flat_pool = jnp.where(row_ids == target[request], new_rows[request][None, :], flat_pool)
    new_hit = (row_ids == target[None, :])[:, :, None]
    page_valid = jnp.any(page_hit, axis=1)
    page_logical = jnp.sum(page_hit.astype(jnp.int32) * jnp.arange(pages_dev)[None, :, None], axis=1)
    page_start = (ctx_index * pages_dev + page_logical) * page_rows
    key_pos = (page_start[:, :, None] + jnp.arange(page_rows)[None, None, :]).reshape(
        request_count, slot_count * page_rows
    )
    dec_visible = (
        jnp.repeat(page_valid, page_rows, axis=1) & (key_pos <= lengths[:, None])
    )[:, None, :]
    query_rot = rotate(dec_qrope[:, 0], cos_new[:, None, :], sin_new[:, None, :]).astype(
        jnp.bfloat16
    )
    dec_queries = jnp.concatenate([dec_qlat[:, 0], query_rot], axis=-1)
    flat_queries = dec_queries.reshape(request_count * head_count, row_width)
    dec_scores = (
        jnp.dot(raw_pool, flat_queries.T, preferred_element_type=jnp.float32) * score_scale
    ).reshape(slot_count * page_rows, request_count, head_count)
    new_scores = (
        jnp.einsum("rd,rhd->rh", new_rows, dec_queries, preferred_element_type=jnp.float32)
        * score_scale
    )
    dec_scores = jnp.where(new_hit, new_scores[None], dec_scores)
    dec_seen = jnp.transpose(dec_visible[:, 0, :])[:, :, None]
    dec_masked = jnp.where(dec_seen, dec_scores, NEG_FILL)
    local_peak = jnp.max(dec_masked, axis=0)
    dec_weights = jnp.where(dec_seen, jnp.exp(dec_masked - local_peak[None]), 0.0)
    local_total = jnp.sum(dec_weights, axis=0)
    rounded = dec_weights.astype(jnp.bfloat16)
    new_weight = jnp.sum(jnp.where(new_hit, rounded, 0.0).astype(jnp.float32), axis=0)
    local_accum = lax.dot_general(
        jnp.where(new_hit, jnp.zeros_like(rounded), rounded).reshape(slot_count * page_rows, -1),
        raw_pool[:, :DC],
        (((0,), (0,)), ((), ())),
        preferred_element_type=jnp.float32,
    ).reshape(request_count, head_count, DC) + new_weight[..., None] * new_rows[:, None, :DC].astype(
        jnp.float32
    )

    dec_share = request_count // ctx_count
    part_width = 128 * ((DC + 2 + 127) // 128)
    dec_block = jnp.concatenate(
        [
            local_accum,
            local_peak[..., None],
            local_total[..., None],
            jnp.zeros((request_count, head_count, part_width - DC - 2), jnp.float32),
        ],
        axis=2,
    ).reshape(ctx_count, dec_share * head_count, part_width)
    keys_all, own_parts = context_exchange(stored, dec_block, ctx_count)
    keys_all = lax.dynamic_update_index_in_dim(keys_all, stored, ctx_index, 0)
    own_parts = lax.dynamic_update_index_in_dim(
        own_parts, lax.dynamic_index_in_dim(dec_block, ctx_index, 0, False), ctx_index, 0
    )
    moving = keys_all.reshape(ctx_count * shard_rows, row_width)
    own_parts = own_parts.reshape(ctx_count, dec_share, head_count, part_width)
    part_accum = own_parts[..., :DC]
    part_peak = own_parts[..., DC]
    part_total = own_parts[..., DC + 1]
    merged_peak = jnp.max(part_peak, axis=0)
    factor = jnp.exp(part_peak - merged_peak[None])
    merged_total = jnp.sum(part_total * factor, axis=0)
    merged_accum = jnp.sum(part_accum * factor[..., None], axis=0)
    own_mixed = (merged_accum / merged_total[..., None]).astype(jnp.bfloat16)

    key_pos_pre = block_position(block_order, jnp.arange(moving.shape[0]), shard_rows)
    query_rows = shard_rows * head_count
    scores = (
        jnp.dot(
            pre_qlat[0].reshape(query_rows, DC), moving[:, :DC].T,
            preferred_element_type=jnp.float32,
        )
        + jnp.dot(
            rotated.reshape(query_rows, DR), moving[:, DC:].T,
            preferred_element_type=jnp.float32,
        )
    ) * score_scale
    visible = jnp.repeat(key_pos_pre[None, :] <= own_pos[:, None], head_count, axis=0)
    masked = jnp.where(visible, scores, NEG_FILL)
    new_peak = jnp.max(masked, axis=-1)
    weights = jnp.where(visible, jnp.exp(masked - new_peak[..., None]), 0.0)
    totals = jnp.sum(weights, axis=-1)
    accumulated = jnp.dot(
        weights.astype(jnp.bfloat16), moving[:, :DC], preferred_element_type=jnp.float32
    )
    pre_mixed = (accumulated / totals[:, None]).astype(jnp.bfloat16).reshape(
        shard_rows, head_count, DC
    )

    own_resid = lax.dynamic_slice_in_dim(dec_resid[:, 0], ctx_index * dec_share, dec_share, 0)
    mixed_all = jnp.concatenate([pre_mixed, own_mixed], axis=0)
    resid_all = jnp.concatenate([pre_resid[0], own_resid], axis=0)
    values = jnp.einsum("nhc,hcv->nhv", mixed_all, w_uv, preferred_element_type=jnp.float32).astype(
        jnp.bfloat16
    )
    hidden_state = resid_all.astype(jnp.float32) + jnp.dot(
        values.reshape(values.shape[0], -1), w_out, preferred_element_type=jnp.float32
    )
    normed = (
        hidden_state
        * lax.rsqrt(jnp.mean(hidden_state * hidden_state, axis=-1, keepdims=True) + EPSILON)
        * norm_gain
    ).astype(jnp.bfloat16)
    logits = jnp.dot(normed.astype(jnp.float32), router, precision=lax.Precision.HIGHEST)
    probable = jax.nn.sigmoid(logits)
    row_count = normed.shape[0]
    width = normed.shape[1]
    top_count = routes.shape[1]
    expert_count = router.shape[1]
    devices = ctx_count * lax.axis_size("req")
    capacity = 2 * ((row_count * top_count + 2 * expert_count - 1) // (2 * expert_count))
    route_hit = routes[:, :, None] == jnp.arange(expert_count)[None, None, :]
    chosen = jnp.sum(jnp.where(route_hit, probable[:, None, :], 0.0), axis=-1)
    mixing = ROUTE_SCALE * chosen / jnp.sum(chosen, axis=1, keepdims=True)
    expert_hits = route_hit.astype(jnp.int32).sum(1)
    earlier = (jnp.arange(row_count)[None, :] < jnp.arange(row_count)[:, None]).astype(jnp.bfloat16)
    before = jnp.dot(
        earlier, expert_hits.astype(jnp.bfloat16), preferred_element_type=jnp.float32
    ).astype(jnp.int32)
    slot_index = jnp.sum(jnp.where(route_hit, before[:, None, :], 0), axis=-1)
    target_slot = routes * capacity + slot_index
    slot_hit = target_slot[:, :, None] == jnp.arange(expert_count * capacity)[None, None, :]
    dispatch = jnp.any(slot_hit, axis=1).astype(jnp.bfloat16).reshape(row_count, expert_count, 1, capacity)
    dispatch = jnp.broadcast_to(dispatch, (row_count, expert_count, 2, capacity)).reshape(row_count, -1)
    doubled = lax.dot_general(
        dispatch, normed, (((0,), (0,)), ((), ())), preferred_element_type=jnp.float32
    ).astype(jnp.bfloat16).reshape(devices, capacity, width)
    partial_out = ffn_half(
        lax.all_to_all(doubled, ("ctx", "req"), split_axis=0, concat_axis=0, tiled=True),
        w_gate[0],
        w_up[0],
        w_down[0],
    )
    returned = lax.all_to_all(
        partial_out, ("ctx", "req"), split_axis=0, concat_axis=0, tiled=True
    ).reshape(expert_count, 2, capacity, width)
    results = (returned[:, 0].astype(jnp.float32) + returned[:, 1].astype(jnp.float32)).astype(
        jnp.bfloat16
    ).reshape(expert_count * capacity, width)
    combine = jnp.sum(jnp.where(slot_hit, mixing[:, :, None], 0.0), axis=1)
    moe = jnp.dot(combine, results.astype(jnp.float32), precision=lax.Precision.HIGHEST)
    final = (hidden_state + moe).astype(jnp.bfloat16)
    pre_out = final[:shard_rows][None]
    dec_out = final[shard_rows:][:, None]
    cache_out = flat_pool.reshape(cache_pool.shape)
    return (pre_out, dec_out, cache_out)


def solution(mesh):
    in_specs = (
        P("req", "ctx", None),
        P("req", "ctx", None, None),
        P("req", "ctx", None, None),
        P("req", "ctx", None),
        P(),
        P(None, "req", None),
        P(None, "req", None, None),
        P(None, "req", None, None),
        P(None, "req", None),
        P(None, "req"),
        P(None, "req", "ctx"),
        P(("ctx", "req"), None, None),
        P(),
        P(),
        P(),
        P(),
        P(("ctx", "req"), None),
        P(("ctx", "req"), None, None),
        P(("ctx", "req"), None, None),
        P(("ctx", "req"), None, None),
    )
    out_specs = (P("req", "ctx", None), P("ctx", "req", None), P(("ctx", "req"), None, None))
    return jax.shard_map(body, mesh=mesh, in_specs=in_specs, out_specs=out_specs, check_vma=False)
```

```python
import functools

import jax
import jax.numpy as jnp
from jax import lax
from jax.experimental import pallas as pl
from jax.experimental.pallas import tpu as pltpu
from jax.sharding import PartitionSpec as P

MESH = pl.DeviceIdType.MESH

DC = 512
DR = 64
DN = 128


THETA = 50000.0
ROUTE_SCALE = 2.446
EPSILON = 1e-06
NEG_FILL = -1e30


def joined(part, axis, combine):
    gathered = jax.tree.map(lambda a: lax.all_gather(a, axis), part)

    def take(source):
        return jax.tree.map(lambda a: lax.dynamic_index_in_dim(a, source, 0, False), gathered)

    return lax.fori_loop(
        1, lax.axis_size(axis), lambda source, state: combine(state, take(source)), take(0)
    )


def rope_tables(positions, rope_width):
    halfway = rope_width // 2
    inverse = THETA ** (-(jnp.arange(halfway).astype(jnp.float32) * 2.0) / rope_width)
    angles = positions.astype(jnp.float32)[..., None] * inverse
    return (jnp.cos(angles), jnp.sin(angles))


def rotate(values, cos_table, sin_table):
    halfway = values.shape[-1] // 2
    leading = values[..., :halfway].astype(jnp.float32)
    trailing = values[..., halfway:].astype(jnp.float32)
    return jnp.concatenate(
        [leading * cos_table - trailing * sin_table, trailing * cos_table + leading * sin_table],
        axis=-1,
    )


def block_position(block_order, global_rows, shard_rows):
    half_rows = shard_rows // 2
    block = global_rows // half_rows
    hit = block[:, None] == jnp.arange(block_order.shape[0])[None, :]
    logical = jnp.sum(jnp.where(hit, block_order[None, :], 0), axis=1)
    return logical * half_rows + global_rows % half_rows


def expert_half(inputs, gate_part, up_part, down_part):
    flat_rows = inputs.reshape(-1, inputs.shape[-1])
    gate_out = jnp.dot(flat_rows, gate_part, preferred_element_type=jnp.float32)
    upward = jnp.dot(flat_rows, up_part, preferred_element_type=jnp.float32)
    hidden = (jax.nn.silu(gate_out) * upward).astype(jnp.bfloat16)
    partial_out = jnp.dot(hidden, down_part, preferred_element_type=jnp.float32).astype(
        jnp.bfloat16
    )
    return partial_out.reshape(inputs.shape)


def merge_softmax(earlier, later):
    left_peak, left_total, left_accum = earlier
    right_peak, right_total, right_accum = later
    new_peak = jnp.maximum(left_peak, right_peak)
    left_factor = jnp.exp(left_peak - new_peak)
    right_factor = jnp.exp(right_peak - new_peak)
    merged_total = left_total * left_factor + right_total * right_factor
    merged_accum = left_accum * left_factor[..., None] + right_accum * right_factor[..., None]
    return (new_peak, merged_total, merged_accum)


def exchange_kernel(n_req, total, x_ref, out_ref, send_sem, recv_sem, local_sem):
    me = lax.axis_index("ctx") * n_req + lax.axis_index("req")

    def device(d):
        return (d // n_req, d % n_req)

    def outgoing(d):
        return pltpu.make_async_remote_copy(
            src_ref=x_ref.at[d],
            dst_ref=out_ref.at[me],
            send_sem=send_sem.at[d],
            recv_sem=recv_sem.at[me],
            device_id=device(d),
            device_id_type=MESH,
        )

    def incoming(s):
        return pltpu.make_async_remote_copy(
            src_ref=x_ref.at[me],
            dst_ref=out_ref.at[s],
            send_sem=send_sem.at[s],
            recv_sem=recv_sem.at[s],
            device_id=device(s),
            device_id_type=MESH,
        )

    barrier = pltpu.get_barrier_semaphore()

    def greet(k, carry):
        d = lax.rem(me + k, total)
        pl.semaphore_signal(barrier, inc=1, device_id=device(d), device_id_type=MESH)
        return carry

    lax.fori_loop(1, total, greet, 0)
    pl.semaphore_wait(barrier, total - 1)
    local = pltpu.make_async_copy(x_ref.at[me], out_ref.at[me], local_sem)
    local.start()

    def send(k, carry):
        outgoing(lax.rem(me + k, total)).start()
        return carry

    lax.fori_loop(1, total, send, 0)

    def finish(k, carry):
        outgoing(lax.rem(me + k, total)).wait_send()
        incoming(lax.rem(me + total - k, total)).wait_recv()
        return carry

    lax.fori_loop(1, total, finish, 0)
    local.wait()


def exchange(x, n_req, total, collective_id):
    return pl.pallas_call(
        functools.partial(exchange_kernel, n_req, total),
        out_shape=jax.ShapeDtypeStruct(x.shape, x.dtype),
        in_specs=[pl.BlockSpec(memory_space=pl.ANY)],
        out_specs=pl.BlockSpec(memory_space=pl.ANY),
        scratch_shapes=[
            pltpu.SemaphoreType.DMA((total,)),
            pltpu.SemaphoreType.DMA((total,)),
            pltpu.SemaphoreType.DMA(()),
        ],
        compiler_params=pltpu.CompilerParams(collective_id=collective_id, has_side_effects=True),
    )(x)


def context_kernel(n_ctx, keys_ref, parts_ref, keys_out, parts_out, sems):
    me = lax.axis_index("ctx")
    row = lax.axis_index("req")
    barrier = pltpu.get_barrier_semaphore()
    for step in range(1, n_ctx):
        other = lax.rem(me + step, n_ctx)
        pl.semaphore_signal(barrier, inc=1, device_id=(other, row), device_id_type=MESH)
    pl.semaphore_wait(barrier, n_ctx - 1)

    def key_copy(source, target):
        return pltpu.make_async_remote_copy(
            src_ref=keys_ref,
            dst_ref=keys_out.at[source],
            send_sem=sems.at[0, target],
            recv_sem=sems.at[1, source],
            device_id=(target, row),
            device_id_type=MESH,
        )

    def part_copy(source, target):
        return pltpu.make_async_remote_copy(
            src_ref=parts_ref.at[target],
            dst_ref=parts_out.at[source],
            send_sem=sems.at[2, target],
            recv_sem=sems.at[3, source],
            device_id=(target, row),
            device_id_type=MESH,
        )

    for step in range(1, n_ctx):
        other = lax.rem(me + step, n_ctx)
        key_copy(me, other).start()
        part_copy(me, other).start()
    for step in range(1, n_ctx):
        other = lax.rem(me + step, n_ctx)
        source = lax.rem(me + n_ctx - step, n_ctx)
        key_copy(me, other).wait_send()
        part_copy(me, other).wait_send()
        key_copy(source, me).wait_recv()
        part_copy(source, me).wait_recv()


def context_exchange(keys, parts, n_ctx):
    return pl.pallas_call(
        functools.partial(context_kernel, n_ctx),
        out_shape=(
            jax.ShapeDtypeStruct((n_ctx,) + keys.shape, keys.dtype),
            jax.ShapeDtypeStruct(parts.shape, parts.dtype),
        ),
        in_specs=[pl.BlockSpec(memory_space=pl.ANY)] * 2,
        out_specs=(pl.BlockSpec(memory_space=pl.ANY), pl.BlockSpec(memory_space=pl.ANY)),
        scratch_shapes=[pltpu.SemaphoreType.DMA((4, n_ctx))],
        compiler_params=pltpu.CompilerParams(collective_id=2, has_side_effects=True),
    )(keys, parts)


def ffn_kernel(x_ref, gate_ref, up_ref, down_ref, out_ref):
    rows = x_ref[...]
    gate_out = jnp.dot(rows, gate_ref[...], preferred_element_type=jnp.float32)
    upward = jnp.dot(rows, up_ref[...], preferred_element_type=jnp.float32)
    hidden = (jax.nn.silu(gate_out) * upward).astype(jnp.bfloat16)
    out_ref[...] = jnp.dot(hidden, down_ref[...], preferred_element_type=jnp.float32).astype(
        out_ref.dtype
    )


def ffn_half(inputs, gate_part, up_part, down_part, tile=256):
    flat_rows = inputs.reshape(-1, inputs.shape[-1])
    rows, width = flat_rows.shape
    hidden = gate_part.shape[1]
    fixed = lambda i: (0, 0)
    out = pl.pallas_call(
        ffn_kernel,
        grid=(rows // tile,),
        in_specs=[
            pl.BlockSpec((tile, width), lambda i: (i, 0)),
            pl.BlockSpec((width, hidden), fixed),
            pl.BlockSpec((width, hidden), fixed),
            pl.BlockSpec((hidden, width), fixed),
        ],
        out_specs=pl.BlockSpec((tile, width), lambda i: (i, 0)),
        out_shape=jax.ShapeDtypeStruct((rows, width), jnp.bfloat16),
        compiler_params=pltpu.CompilerParams(vmem_limit_bytes=48 * 1024 * 1024),
        cost_estimate=pl.CostEstimate(
            flops=6 * rows * width * hidden,
            transcendentals=rows * hidden,
            bytes_accessed=2 * (2 * rows * width + 3 * width * hidden),
        ),
    )(flat_rows, gate_part, up_part, down_part)
    return out.reshape(inputs.shape)


def body(
    pre_latent,
    pre_qlat,
    pre_qrope,
    pre_resid,
    block_order,
    dec_new,
    dec_qlat,
    dec_qrope,
    dec_resid,
    cache_len,
    page_table,
    cache_pool,
    w_uv,
    w_out,
    norm_gain,
    router,
    routes,
    w_gate,
    w_up,
    w_down,
):
    ctx_count = lax.axis_size("ctx")
    ctx_index = lax.axis_index("ctx")
    score_scale = (DN + DR) ** (-0.5)
    latent = pre_latent[0]
    shard_rows = latent.shape[0]
    local_rows = jnp.arange(shard_rows)
    own_pos = block_position(block_order, ctx_index * shard_rows + local_rows, shard_rows)
    cos_table, sin_table = rope_tables(own_pos, DR)
    key_rope = rotate(latent[:, DC:], cos_table, sin_table).astype(jnp.bfloat16)
    stored = jnp.concatenate([latent[:, :DC], key_rope], axis=-1)
    rotated = rotate(pre_qrope[0], cos_table[:, None, :], sin_table[:, None, :]).astype(
        jnp.bfloat16
    )
    head_count = pre_qlat.shape[2]

    lengths = cache_len[:, 0]
    tables = page_table[:, 0, :]
    request_count = tables.shape[0]
    pages_dev = tables.shape[1]
    page_rows = cache_pool.shape[1]
    slot_count = cache_pool.shape[0]
    row_width = cache_pool.shape[2]
    cos_new, sin_new = rope_tables(lengths, DR)
    new_rope = rotate(dec_new[:, 0, DC:], cos_new, sin_new).astype(jnp.bfloat16)
    new_rows = jnp.concatenate([dec_new[:, 0, :DC], new_rope], axis=-1)
    page_index = lengths // page_rows
    owner_ctx = page_index // pages_dev
    page_hit = tables[:, :, None] == jnp.arange(slot_count)[None, None, :]
    wanted = jnp.arange(pages_dev)[None, :] == (page_index % pages_dev)[:, None]
    slot_of = jnp.sum(jnp.where(wanted, tables, 0), axis=1)
    target = jnp.where(
        owner_ctx == ctx_index, slot_of * page_rows + lengths % page_rows, slot_count * page_rows
    )
    row_ids = jnp.arange(slot_count * page_rows)[:, None]
    raw_pool = cache_pool.reshape(slot_count * page_rows, row_width)
    flat_pool = raw_pool
    for request in range(request_count):
        flat_pool = jnp.where(row_ids == target[request], new_rows[request][None, :], flat_pool)
    new_hit = (row_ids == target[None, :])[:, :, None]
    page_valid = jnp.any(page_hit, axis=1)
    page_logical = jnp.sum(page_hit.astype(jnp.int32) * jnp.arange(pages_dev)[None, :, None], axis=1)
    page_start = (ctx_index * pages_dev + page_logical) * page_rows
    key_pos = (page_start[:, :, None] + jnp.arange(page_rows)[None, None, :]).reshape(
        request_count, slot_count * page_rows
    )
    dec_visible = (
        jnp.repeat(page_valid, page_rows, axis=1) & (key_pos <= lengths[:, None])
    )[:, None, :]
    query_rot = rotate(dec_qrope[:, 0], cos_new[:, None, :], sin_new[:, None, :]).astype(
        jnp.bfloat16
    )
    dec_queries = jnp.concatenate([dec_qlat[:, 0], query_rot], axis=-1)
    flat_queries = dec_queries.reshape(request_count * head_count, row_width)
    dec_scores = (
        jnp.dot(raw_pool, flat_queries.T, preferred_element_type=jnp.float32) * score_scale
    ).reshape(slot_count * page_rows, request_count, head_count)
    new_scores = (
        jnp.einsum("rd,rhd->rh", new_rows, dec_queries, preferred_element_type=jnp.float32)
        * score_scale
    )
    dec_scores = jnp.where(new_hit, new_scores[None], dec_scores)
    dec_seen = jnp.transpose(dec_visible[:, 0, :])[:, :, None]
    dec_masked = jnp.where(dec_seen, dec_scores, NEG_FILL)
    local_peak = jnp.max(dec_masked, axis=0)
    dec_weights = jnp.where(dec_seen, jnp.exp(dec_masked - local_peak[None]), 0.0)
    local_total = jnp.sum(dec_weights, axis=0)
    rounded = dec_weights.astype(jnp.bfloat16)
    new_weight = jnp.sum(jnp.where(new_hit, rounded, 0.0).astype(jnp.float32), axis=0)
    local_accum = lax.dot_general(
        jnp.where(new_hit, jnp.zeros_like(rounded), rounded).reshape(slot_count * page_rows, -1),
        raw_pool[:, :DC],
        (((0,), (0,)), ((), ())),
        preferred_element_type=jnp.float32,
    ).reshape(request_count, head_count, DC) + new_weight[..., None] * new_rows[:, None, :DC].astype(
        jnp.float32
    )

    dec_share = request_count // ctx_count
    part_width = 128 * ((DC + 2 + 127) // 128)
    dec_block = jnp.concatenate(
        [
            local_accum,
            local_peak[..., None],
            local_total[..., None],
            jnp.zeros((request_count, head_count, part_width - DC - 2), jnp.float32),
        ],
        axis=2,
    ).reshape(ctx_count, dec_share * head_count, part_width)
    keys_all, own_parts = context_exchange(stored, dec_block, ctx_count)
    keys_all = lax.dynamic_update_index_in_dim(keys_all, stored, ctx_index, 0)
    own_parts = lax.dynamic_update_index_in_dim(
        own_parts, lax.dynamic_index_in_dim(dec_block, ctx_index, 0, False), ctx_index, 0
    )
    moving = keys_all.reshape(ctx_count * shard_rows, row_width)
    own_parts = own_parts.reshape(ctx_count, dec_share, head_count, part_width)
    part_accum = own_parts[..., :DC]
    part_peak = own_parts[..., DC]
    part_total = own_parts[..., DC + 1]
    merged_peak = jnp.max(part_peak, axis=0)
    factor = jnp.exp(part_peak - merged_peak[None])
    merged_total = jnp.sum(part_total * factor, axis=0)
    merged_accum = jnp.sum(part_accum * factor[..., None], axis=0)
    own_mixed = (merged_accum / merged_total[..., None]).astype(jnp.bfloat16)

    key_pos_pre = block_position(block_order, jnp.arange(moving.shape[0]), shard_rows)
    query_rows = shard_rows * head_count
    scores = (
        jnp.dot(
            pre_qlat[0].reshape(query_rows, DC), moving[:, :DC].T,
            preferred_element_type=jnp.float32,
        )
        + jnp.dot(
            rotated.reshape(query_rows, DR), moving[:, DC:].T,
            preferred_element_type=jnp.float32,
        )
    ) * score_scale
    visible = key_pos_pre[None, :] <= jnp.repeat(own_pos, head_count)[:, None]
    masked = jnp.where(visible, scores, NEG_FILL)
    new_peak = jnp.max(masked, axis=-1)
    weights = jnp.where(visible, jnp.exp(masked - new_peak[..., None]), 0.0)
    totals = jnp.sum(weights, axis=-1)
    accumulated = jnp.dot(
        weights.astype(jnp.bfloat16), moving[:, :DC], preferred_element_type=jnp.float32
    )
    pre_mixed = (accumulated / totals[:, None]).astype(jnp.bfloat16).reshape(
        shard_rows, head_count, DC
    )

    own_resid = lax.dynamic_slice_in_dim(dec_resid[:, 0], ctx_index * dec_share, dec_share, 0)
    mixed_all = jnp.concatenate([pre_mixed, own_mixed], axis=0)
    resid_all = jnp.concatenate([pre_resid[0], own_resid], axis=0)
    values = jnp.einsum("nhc,hcv->nhv", mixed_all, w_uv, preferred_element_type=jnp.float32).astype(
        jnp.bfloat16
    )
    hidden_state = resid_all.astype(jnp.float32) + jnp.dot(
        values.reshape(values.shape[0], -1), w_out, preferred_element_type=jnp.float32
    )
    normed = (
        hidden_state
        * lax.rsqrt(jnp.mean(hidden_state * hidden_state, axis=-1, keepdims=True) + EPSILON)
        * norm_gain
    ).astype(jnp.bfloat16)
    logits = jnp.dot(normed.astype(jnp.float32), router, precision=lax.Precision.HIGHEST)
    probable = jax.nn.sigmoid(logits)
    row_count = normed.shape[0]
    width = normed.shape[1]
    top_count = routes.shape[1]
    expert_count = router.shape[1]
    devices = ctx_count * lax.axis_size("req")
    capacity = 2 * ((row_count * top_count + 2 * expert_count - 1) // (2 * expert_count))
    route_hit = routes[:, :, None] == jnp.arange(expert_count)[None, None, :]
    chosen = jnp.sum(jnp.where(route_hit, probable[:, None, :], 0.0), axis=-1)
    mixing = ROUTE_SCALE * chosen / jnp.sum(chosen, axis=1, keepdims=True)
    expert_hits = route_hit.astype(jnp.int32).sum(1)
    earlier = (jnp.arange(row_count)[None, :] < jnp.arange(row_count)[:, None]).astype(jnp.bfloat16)
    before = jnp.dot(
        earlier, expert_hits.astype(jnp.bfloat16), preferred_element_type=jnp.float32
    ).astype(jnp.int32)
    slot_index = jnp.sum(jnp.where(route_hit, before[:, None, :], 0), axis=-1)
    target_slot = routes * capacity + slot_index
    slot_hit = target_slot[:, :, None] == jnp.arange(expert_count * capacity)[None, None, :]
    dispatch = jnp.any(slot_hit, axis=1).astype(jnp.bfloat16).reshape(row_count, expert_count, 1, capacity)
    dispatch = jnp.broadcast_to(dispatch, (row_count, expert_count, 2, capacity)).reshape(row_count, -1)
    doubled = lax.dot_general(
        dispatch, normed, (((0,), (0,)), ((), ())), preferred_element_type=jnp.float32
    ).astype(jnp.bfloat16).reshape(devices, capacity, width)
    partial_out = ffn_half(
        lax.all_to_all(doubled, ("ctx", "req"), split_axis=0, concat_axis=0, tiled=True),
        w_gate[0],
        w_up[0],
        w_down[0],
    )
    returned = lax.all_to_all(
        partial_out, ("ctx", "req"), split_axis=0, concat_axis=0, tiled=True
    ).reshape(expert_count, 2, capacity, width)
    results = (returned[:, 0].astype(jnp.float32) + returned[:, 1].astype(jnp.float32)).astype(
        jnp.bfloat16
    ).reshape(expert_count * capacity, width)
    combine = jnp.sum(jnp.where(slot_hit, mixing[:, :, None], 0.0), axis=1)
    moe = jnp.dot(combine, results.astype(jnp.float32), precision=lax.Precision.HIGHEST)
    final = (hidden_state + moe).astype(jnp.bfloat16)
    pre_out = final[:shard_rows][None]
    dec_out = final[shard_rows:][:, None]
    cache_out = flat_pool.reshape(cache_pool.shape)
    return (pre_out, dec_out, cache_out)


def solution(mesh):
    in_specs = (
        P("req", "ctx", None),
        P("req", "ctx", None, None),
        P("req", "ctx", None, None),
        P("req", "ctx", None),
        P(),
        P(None, "req", None),
        P(None, "req", None, None),
        P(None, "req", None, None),
        P(None, "req", None),
        P(None, "req"),
        P(None, "req", "ctx"),
        P(("ctx", "req"), None, None),
        P(),
        P(),
        P(),
        P(),
        P(("ctx", "req"), None),
        P(("ctx", "req"), None, None),
        P(("ctx", "req"), None, None),
        P(("ctx", "req"), None, None),
    )
    out_specs = (P("req", "ctx", None), P("ctx", "req", None), P(("ctx", "req"), None, None))
    return jax.shard_map(body, mesh=mesh, in_specs=in_specs, out_specs=out_specs, check_vma=False)
```

```python
import functools

import jax
import jax.numpy as jnp
from jax import lax
from jax.experimental import pallas as pl
from jax.experimental.pallas import tpu as pltpu
from jax.sharding import PartitionSpec as P

MESH = pl.DeviceIdType.MESH

DC = 512
DR = 64
DN = 128


THETA = 50000.0
ROUTE_SCALE = 2.446
EPSILON = 1e-06
NEG_FILL = -1e30


def joined(part, axis, combine):
    gathered = jax.tree.map(lambda a: lax.all_gather(a, axis), part)

    def take(source):
        return jax.tree.map(lambda a: lax.dynamic_index_in_dim(a, source, 0, False), gathered)

    return lax.fori_loop(
        1, lax.axis_size(axis), lambda source, state: combine(state, take(source)), take(0)
    )


def rope_tables(positions, rope_width):
    halfway = rope_width // 2
    inverse = THETA ** (-(jnp.arange(halfway).astype(jnp.float32) * 2.0) / rope_width)
    angles = positions.astype(jnp.float32)[..., None] * inverse
    return (jnp.cos(angles), jnp.sin(angles))


def rotate(values, cos_table, sin_table):
    halfway = values.shape[-1] // 2
    leading = values[..., :halfway].astype(jnp.float32)
    trailing = values[..., halfway:].astype(jnp.float32)
    return jnp.concatenate(
        [leading * cos_table - trailing * sin_table, trailing * cos_table + leading * sin_table],
        axis=-1,
    )


def block_position(block_order, global_rows, shard_rows):
    half_rows = shard_rows // 2
    block = global_rows // half_rows
    hit = block[:, None] == jnp.arange(block_order.shape[0])[None, :]
    logical = jnp.sum(jnp.where(hit, block_order[None, :], 0), axis=1)
    return logical * half_rows + global_rows % half_rows


def expert_half(inputs, gate_part, up_part, down_part):
    flat_rows = inputs.reshape(-1, inputs.shape[-1])
    gate_out = jnp.dot(flat_rows, gate_part, preferred_element_type=jnp.float32)
    upward = jnp.dot(flat_rows, up_part, preferred_element_type=jnp.float32)
    hidden = (jax.nn.silu(gate_out) * upward).astype(jnp.bfloat16)
    partial_out = jnp.dot(hidden, down_part, preferred_element_type=jnp.float32).astype(
        jnp.bfloat16
    )
    return partial_out.reshape(inputs.shape)


def merge_softmax(earlier, later):
    left_peak, left_total, left_accum = earlier
    right_peak, right_total, right_accum = later
    new_peak = jnp.maximum(left_peak, right_peak)
    left_factor = jnp.exp(left_peak - new_peak)
    right_factor = jnp.exp(right_peak - new_peak)
    merged_total = left_total * left_factor + right_total * right_factor
    merged_accum = left_accum * left_factor[..., None] + right_accum * right_factor[..., None]
    return (new_peak, merged_total, merged_accum)


def exchange_kernel(n_req, total, x_ref, out_ref, send_sem, recv_sem, local_sem):
    me = lax.axis_index("ctx") * n_req + lax.axis_index("req")

    def device(d):
        return (d // n_req, d % n_req)

    def outgoing(d):
        return pltpu.make_async_remote_copy(
            src_ref=x_ref.at[d],
            dst_ref=out_ref.at[me],
            send_sem=send_sem.at[d],
            recv_sem=recv_sem.at[me],
            device_id=device(d),
            device_id_type=MESH,
        )

    def incoming(s):
        return pltpu.make_async_remote_copy(
            src_ref=x_ref.at[me],
            dst_ref=out_ref.at[s],
            send_sem=send_sem.at[s],
            recv_sem=recv_sem.at[s],
            device_id=device(s),
            device_id_type=MESH,
        )

    barrier = pltpu.get_barrier_semaphore()

    def greet(k, carry):
        d = lax.rem(me + k, total)
        pl.semaphore_signal(barrier, inc=1, device_id=device(d), device_id_type=MESH)
        return carry

    lax.fori_loop(1, total, greet, 0)
    pl.semaphore_wait(barrier, total - 1)
    local = pltpu.make_async_copy(x_ref.at[me], out_ref.at[me], local_sem)
    local.start()

    def send(k, carry):
        outgoing(lax.rem(me + k, total)).start()
        return carry

    lax.fori_loop(1, total, send, 0)

    def finish(k, carry):
        outgoing(lax.rem(me + k, total)).wait_send()
        incoming(lax.rem(me + total - k, total)).wait_recv()
        return carry

    lax.fori_loop(1, total, finish, 0)
    local.wait()


def exchange(x, n_req, total, collective_id):
    return pl.pallas_call(
        functools.partial(exchange_kernel, n_req, total),
        out_shape=jax.ShapeDtypeStruct(x.shape, x.dtype),
        in_specs=[pl.BlockSpec(memory_space=pl.ANY)],
        out_specs=pl.BlockSpec(memory_space=pl.ANY),
        scratch_shapes=[
            pltpu.SemaphoreType.DMA((total,)),
            pltpu.SemaphoreType.DMA((total,)),
            pltpu.SemaphoreType.DMA(()),
        ],
        compiler_params=pltpu.CompilerParams(collective_id=collective_id, has_side_effects=True),
    )(x)


def context_kernel(n_ctx, keys_ref, parts_ref, keys_out, parts_out, sems):
    me = lax.axis_index("ctx")
    row = lax.axis_index("req")
    barrier = pltpu.get_barrier_semaphore()
    for step in range(1, n_ctx):
        other = lax.rem(me + step, n_ctx)
        pl.semaphore_signal(barrier, inc=1, device_id=(other, row), device_id_type=MESH)
    pl.semaphore_wait(barrier, n_ctx - 1)

    def key_copy(source, target):
        return pltpu.make_async_remote_copy(
            src_ref=keys_ref,
            dst_ref=keys_out.at[source],
            send_sem=sems.at[0, target],
            recv_sem=sems.at[1, source],
            device_id=(target, row),
            device_id_type=MESH,
        )

    def part_copy(source, target):
        return pltpu.make_async_remote_copy(
            src_ref=parts_ref.at[target],
            dst_ref=parts_out.at[source],
            send_sem=sems.at[2, target],
            recv_sem=sems.at[3, source],
            device_id=(target, row),
            device_id_type=MESH,
        )

    for step in range(1, n_ctx):
        other = lax.rem(me + step, n_ctx)
        key_copy(me, other).start()
        part_copy(me, other).start()
    for step in range(1, n_ctx):
        other = lax.rem(me + step, n_ctx)
        source = lax.rem(me + n_ctx - step, n_ctx)
        key_copy(me, other).wait_send()
        part_copy(me, other).wait_send()
        key_copy(source, me).wait_recv()
        part_copy(source, me).wait_recv()


def context_exchange(keys, parts, n_ctx):
    return pl.pallas_call(
        functools.partial(context_kernel, n_ctx),
        out_shape=(
            jax.ShapeDtypeStruct((n_ctx,) + keys.shape, keys.dtype),
            jax.ShapeDtypeStruct(parts.shape, parts.dtype),
        ),
        in_specs=[pl.BlockSpec(memory_space=pl.ANY)] * 2,
        out_specs=(pl.BlockSpec(memory_space=pl.ANY), pl.BlockSpec(memory_space=pl.ANY)),
        scratch_shapes=[pltpu.SemaphoreType.DMA((4, n_ctx))],
        compiler_params=pltpu.CompilerParams(collective_id=2, has_side_effects=True),
    )(keys, parts)


def ffn_kernel(x_ref, gate_ref, up_ref, down_ref, out_ref):
    rows = x_ref[...]
    gate_out = jnp.dot(rows, gate_ref[...], preferred_element_type=jnp.float32)
    upward = jnp.dot(rows, up_ref[...], preferred_element_type=jnp.float32)
    hidden = (jax.nn.silu(gate_out) * upward).astype(jnp.bfloat16)
    out_ref[...] = jnp.dot(hidden, down_ref[...], preferred_element_type=jnp.float32).astype(
        out_ref.dtype
    )


def ffn_half(inputs, gate_part, up_part, down_part, tile=256):
    flat_rows = inputs.reshape(-1, inputs.shape[-1])
    rows, width = flat_rows.shape
    hidden = gate_part.shape[1]
    fixed = lambda i: (0, 0)
    out = pl.pallas_call(
        ffn_kernel,
        grid=(rows // tile,),
        in_specs=[
            pl.BlockSpec((tile, width), lambda i: (i, 0)),
            pl.BlockSpec((width, hidden), fixed),
            pl.BlockSpec((width, hidden), fixed),
            pl.BlockSpec((hidden, width), fixed),
        ],
        out_specs=pl.BlockSpec((tile, width), lambda i: (i, 0)),
        out_shape=jax.ShapeDtypeStruct((rows, width), jnp.bfloat16),
        compiler_params=pltpu.CompilerParams(vmem_limit_bytes=48 * 1024 * 1024),
        cost_estimate=pl.CostEstimate(
            flops=6 * rows * width * hidden,
            transcendentals=rows * hidden,
            bytes_accessed=2 * (2 * rows * width + 3 * width * hidden),
        ),
    )(flat_rows, gate_part, up_part, down_part)
    return out.reshape(inputs.shape)


def body(
    pre_latent,
    pre_qlat,
    pre_qrope,
    pre_resid,
    block_order,
    dec_new,
    dec_qlat,
    dec_qrope,
    dec_resid,
    cache_len,
    page_table,
    cache_pool,
    w_uv,
    w_out,
    norm_gain,
    router,
    routes,
    w_gate,
    w_up,
    w_down,
):
    ctx_count = lax.axis_size("ctx")
    ctx_index = lax.axis_index("ctx")
    score_scale = (DN + DR) ** (-0.5)
    latent = pre_latent[0]
    shard_rows = latent.shape[0]
    local_rows = jnp.arange(shard_rows)
    own_pos = block_position(block_order, ctx_index * shard_rows + local_rows, shard_rows)
    cos_table, sin_table = rope_tables(own_pos, DR)
    key_rope = rotate(latent[:, DC:], cos_table, sin_table).astype(jnp.bfloat16)
    stored = jnp.concatenate([latent[:, :DC], key_rope], axis=-1)
    rotated = rotate(pre_qrope[0], cos_table[:, None, :], sin_table[:, None, :]).astype(
        jnp.bfloat16
    )
    head_count = pre_qlat.shape[2]

    lengths = cache_len[:, 0]
    tables = page_table[:, 0, :]
    request_count = tables.shape[0]
    pages_dev = tables.shape[1]
    page_rows = cache_pool.shape[1]
    slot_count = cache_pool.shape[0]
    row_width = cache_pool.shape[2]
    cos_new, sin_new = rope_tables(lengths, DR)
    new_rope = rotate(dec_new[:, 0, DC:], cos_new, sin_new).astype(jnp.bfloat16)
    new_rows = jnp.concatenate([dec_new[:, 0, :DC], new_rope], axis=-1)
    page_index = lengths // page_rows
    owner_ctx = page_index // pages_dev
    page_hit = tables[:, :, None] == jnp.arange(slot_count)[None, None, :]
    wanted = jnp.arange(pages_dev)[None, :] == (page_index % pages_dev)[:, None]
    slot_of = jnp.sum(jnp.where(wanted, tables, 0), axis=1)
    target = jnp.where(
        owner_ctx == ctx_index, slot_of * page_rows + lengths % page_rows, slot_count * page_rows
    )
    row_ids = jnp.arange(slot_count * page_rows)[:, None]
    raw_pool = cache_pool.reshape(slot_count * page_rows, row_width)
    flat_pool = raw_pool
    for request in range(request_count):
        flat_pool = jnp.where(row_ids == target[request], new_rows[request][None, :], flat_pool)
    new_hit = (row_ids == target[None, :])[:, :, None]
    page_valid = jnp.any(page_hit, axis=1)
    page_logical = jnp.sum(page_hit.astype(jnp.int32) * jnp.arange(pages_dev)[None, :, None], axis=1)
    page_start = (ctx_index * pages_dev + page_logical) * page_rows
    key_pos = (page_start[:, :, None] + jnp.arange(page_rows)[None, None, :]).reshape(
        request_count, slot_count * page_rows
    )
    dec_visible = (
        jnp.repeat(page_valid, page_rows, axis=1) & (key_pos <= lengths[:, None])
    )[:, None, :]
    query_rot = rotate(dec_qrope[:, 0], cos_new[:, None, :], sin_new[:, None, :]).astype(
        jnp.bfloat16
    )
    dec_queries = jnp.concatenate([dec_qlat[:, 0], query_rot], axis=-1)
    flat_queries = dec_queries.reshape(request_count * head_count, row_width)
    dec_scores = (
        jnp.dot(raw_pool, flat_queries.T, preferred_element_type=jnp.float32) * score_scale
    ).reshape(slot_count * page_rows, request_count, head_count)
    new_scores = (
        jnp.einsum("rd,rhd->rh", new_rows, dec_queries, preferred_element_type=jnp.float32)
        * score_scale
    )
    dec_scores = jnp.where(new_hit, new_scores[None], dec_scores)
    dec_seen = jnp.transpose(dec_visible[:, 0, :])[:, :, None]
    dec_masked = jnp.where(dec_seen, dec_scores, NEG_FILL)
    local_peak = jnp.max(dec_masked, axis=0)
    dec_weights = jnp.where(dec_seen, jnp.exp(dec_masked - local_peak[None]), 0.0)
    local_total = jnp.sum(dec_weights, axis=0)
    rounded = dec_weights.astype(jnp.bfloat16)
    new_weight = jnp.sum(jnp.where(new_hit, rounded, 0.0).astype(jnp.float32), axis=0)
    local_accum = lax.dot_general(
        jnp.where(new_hit, jnp.zeros_like(rounded), rounded).reshape(slot_count * page_rows, -1),
        raw_pool[:, :DC],
        (((0,), (0,)), ((), ())),
        preferred_element_type=jnp.float32,
    ).reshape(request_count, head_count, DC) + new_weight[..., None] * new_rows[:, None, :DC].astype(
        jnp.float32
    )

    dec_share = request_count // ctx_count
    part_width = 128 * ((DC + 2 + 127) // 128)
    dec_block = jnp.concatenate(
        [
            local_accum,
            local_peak[..., None],
            local_total[..., None],
            jnp.zeros((request_count, head_count, part_width - DC - 2), jnp.float32),
        ],
        axis=2,
    ).reshape(ctx_count, dec_share * head_count, part_width)
    keys_all, own_parts = context_exchange(stored, dec_block, ctx_count)
    keys_all = lax.dynamic_update_index_in_dim(keys_all, stored, ctx_index, 0)
    own_parts = lax.dynamic_update_index_in_dim(
        own_parts, lax.dynamic_index_in_dim(dec_block, ctx_index, 0, False), ctx_index, 0
    )
    moving = keys_all.reshape(ctx_count * shard_rows, row_width)
    own_parts = own_parts.reshape(ctx_count, dec_share, head_count, part_width)
    part_accum = own_parts[..., :DC]
    part_peak = own_parts[..., DC]
    part_total = own_parts[..., DC + 1]
    merged_peak = jnp.max(part_peak, axis=0)
    factor = jnp.exp(part_peak - merged_peak[None])
    merged_total = jnp.sum(part_total * factor, axis=0)
    merged_accum = jnp.sum(part_accum * factor[..., None], axis=0)
    own_mixed = (merged_accum / merged_total[..., None]).astype(jnp.bfloat16)

    key_pos_pre = block_position(block_order, jnp.arange(moving.shape[0]), shard_rows)
    query_rows = shard_rows * head_count
    scores = (
        jnp.dot(
            pre_qlat[0].reshape(query_rows, DC), moving[:, :DC].T,
            preferred_element_type=jnp.float32,
        )
        + jnp.dot(
            rotated.reshape(query_rows, DR), moving[:, DC:].T,
            preferred_element_type=jnp.float32,
        )
    ) * score_scale
    visible = key_pos_pre[None, :] <= jnp.repeat(own_pos, head_count)[:, None]
    masked = jnp.where(visible, scores, NEG_FILL)
    new_peak = jnp.max(masked, axis=-1)
    weights = jnp.where(visible, jnp.exp(masked - new_peak[..., None]), 0.0)
    totals = jnp.sum(weights, axis=-1)
    accumulated = jnp.dot(
        weights.astype(jnp.bfloat16), moving[:, :DC], preferred_element_type=jnp.float32
    )
    pre_mixed = (accumulated / totals[:, None]).astype(jnp.bfloat16).reshape(
        shard_rows, head_count, DC
    )

    own_resid = lax.dynamic_slice_in_dim(dec_resid[:, 0], ctx_index * dec_share, dec_share, 0)
    mixed_all = jnp.concatenate([pre_mixed, own_mixed], axis=0)
    resid_all = jnp.concatenate([pre_resid[0], own_resid], axis=0)
    values = jnp.einsum("nhc,hcv->nhv", mixed_all, w_uv, preferred_element_type=jnp.float32).astype(
        jnp.bfloat16
    )
    hidden_state = resid_all.astype(jnp.float32) + jnp.dot(
        values.reshape(values.shape[0], -1), w_out, preferred_element_type=jnp.float32
    )
    normed = (
        hidden_state
        * lax.rsqrt(jnp.mean(hidden_state * hidden_state, axis=-1, keepdims=True) + EPSILON)
        * norm_gain
    ).astype(jnp.bfloat16)
    logits = jnp.dot(normed.astype(jnp.float32), router, precision=lax.Precision.HIGHEST)
    probable = jax.nn.sigmoid(logits)
    row_count = normed.shape[0]
    width = normed.shape[1]
    top_count = routes.shape[1]
    expert_count = router.shape[1]
    devices = ctx_count * lax.axis_size("req")
    capacity = 2 * ((row_count * top_count + 2 * expert_count - 1) // (2 * expert_count))
    route_hit = routes[:, :, None] == jnp.arange(expert_count)[None, None, :]
    chosen = jnp.sum(jnp.where(route_hit, probable[:, None, :], 0.0), axis=-1)
    mixing = ROUTE_SCALE * chosen / jnp.sum(chosen, axis=1, keepdims=True)
    expert_hits = route_hit.astype(jnp.int32).sum(1)
    earlier = (jnp.arange(row_count)[None, :] < jnp.arange(row_count)[:, None]).astype(jnp.bfloat16)
    before = jnp.dot(
        earlier, expert_hits.astype(jnp.bfloat16), preferred_element_type=jnp.float32
    ).astype(jnp.int32)
    slot_index = jnp.sum(jnp.where(route_hit, before[:, None, :], 0), axis=-1)
    target_slot = routes * capacity + slot_index
    slot_hit = target_slot[:, :, None] == jnp.arange(expert_count * capacity)[None, None, :]
    slot_ids = jnp.broadcast_to(
        (jnp.arange(expert_count) * capacity)[:, None, None] + jnp.arange(capacity)[None, None, :],
        (expert_count, 2, capacity),
    ).reshape(-1)
    dispatch = jnp.any(slot_ids[:, None, None] == target_slot[None], axis=2).astype(jnp.bfloat16)
    doubled = jnp.dot(dispatch, normed, preferred_element_type=jnp.float32).astype(
        jnp.bfloat16
    ).reshape(devices, capacity, width)
    partial_out = ffn_half(
        lax.all_to_all(doubled, ("ctx", "req"), split_axis=0, concat_axis=0, tiled=True),
        w_gate[0],
        w_up[0],
        w_down[0],
    )
    returned = lax.all_to_all(
        partial_out, ("ctx", "req"), split_axis=0, concat_axis=0, tiled=True
    ).reshape(expert_count, 2, capacity, width)
    results = (returned[:, 0].astype(jnp.float32) + returned[:, 1].astype(jnp.float32)).astype(
        jnp.bfloat16
    ).reshape(expert_count * capacity, width)
    combine = jnp.sum(jnp.where(slot_hit, mixing[:, :, None], 0.0), axis=1)
    moe = jnp.dot(combine, results.astype(jnp.float32), precision=lax.Precision.HIGHEST)
    final = (hidden_state + moe).astype(jnp.bfloat16)
    pre_out = final[:shard_rows][None]
    dec_out = final[shard_rows:][:, None]
    cache_out = flat_pool.reshape(cache_pool.shape)
    return (pre_out, dec_out, cache_out)


def solution(mesh):
    in_specs = (
        P("req", "ctx", None),
        P("req", "ctx", None, None),
        P("req", "ctx", None, None),
        P("req", "ctx", None),
        P(),
        P(None, "req", None),
        P(None, "req", None, None),
        P(None, "req", None, None),
        P(None, "req", None),
        P(None, "req"),
        P(None, "req", "ctx"),
        P(("ctx", "req"), None, None),
        P(),
        P(),
        P(),
        P(),
        P(("ctx", "req"), None),
        P(("ctx", "req"), None, None),
        P(("ctx", "req"), None, None),
        P(("ctx", "req"), None, None),
    )
    out_specs = (P("req", "ctx", None), P("ctx", "req", None), P(("ctx", "req"), None, None))
    return jax.shard_map(body, mesh=mesh, in_specs=in_specs, out_specs=out_specs, check_vma=False)
```
